256 devices in a mesh: lon: 32 (over x_lo, z, core), lat: 8 (over x_hi, y).
Axes of the slice: x: 4 (x_hi: 2, x_lo: 2; x = x_hi * 2 + x_lo), y: 4, z: 8, core: 2. Of those that a mesh axis runs over, the one named last changes fastest.
Arguments:
- cotangent: bfloat16 [1440, 160, 1024], P('lon', None, 'lat'), may hold values from -6 to 6
- winds: bfloat16 [1440, 64, 1024], P('lon', None, 'lat'), may hold values from -0.44921875 to 0.44921875
- filter_ops: bfloat16 [16, 1440, 1440], P('lat', 'lon'), may hold values from -0.3125 to 0.3125
- block_band: int32 [16], replicated, may hold values from 0 to 7, as said below
- block_row: int32 [16], replicated, may hold values from 0 to 127
Outputs:
- adjoint_state: float32 [1440, 160, 1024], P('lon', None, 'lat')
The draws below stay inside these ranges and needn't reach their ends.
Inputs may be any that keep to these rules, and one draw needn't show every extreme that they name: `block_band`: band 0 and band 8 - 1 each read exactly 5 blocks; the remaining blocks are spread over the other bands as evenly as possible, in an order drawn from the seed.
All inputs are finite; a program needn't handle non-finite values.
Results may differ from the reference program's by a relative error of at most 0.006.
Values may be sent and summed in bfloat16 or wider, within the bound.
No kernel may reach another device: no remote copies, remote signals or barrier semaphores. Data moves between devices by JAX's collectives and lax.ppermute only.
A program may use at most 128 MiB of HBM per device.

```python
import jax
import jax.numpy as jnp
from jax import lax

NLON = 1440
VAR = 5
LEV = 32
NSUB = 2
LAT_DEV = 128
C = 160
BANDS = 8
NLAT = 1024
NOPS = 16
POLAR_OPS = 5


def draw_block_band(key, part):
    positions = jnp.arange(NOPS, dtype=jnp.int32)
    middle = max(BANDS - 2, 1)
    profile = jnp.where(positions < POLAR_OPS, 0, jnp.where(positions < 2 * POLAR_OPS, BANDS - 1, 1 + (positions - 2 * POLAR_OPS) % middle))
    return jax.random.permutation(jax.random.fold_in(key, 7), profile.astype(jnp.int32)).astype(jnp.int32)


def set_ends(drawn, key, low, high):
    longest = drawn.shape.index(max(drawn.shape))
    spots = []
    for shift in (0, 1):
        where = [jax.random.randint(jax.random.fold_in(key, axis), (), 0, length) for axis, length in enumerate(drawn.shape)]
        where[longest] = (where[longest] + shift) % drawn.shape[longest]
        spots.append(tuple(where))
    return drawn.at[spots[0]].set(low).at[spots[1]].set(high)


def spiked(array, rng, source, target, blocks, factor):
    def block_of(axis_at):
        return (jnp.arange(array.shape[axis_at]) // (array.shape[axis_at] // blocks)).reshape((-1,) + (1,) * (array.ndim - 1 - axis_at))

    first = jax.random.permutation(rng, blocks)[block_of(target)]
    other_side = (block_of(target) + blocks // 2) % blocks
    return jnp.where((block_of(source) == first) | (block_of(source) == other_side), factor * array, array)


def steps_of(key, extent, cuts, least, largest):
    gain, own = 1.0, jax.random.fold_in(key, 6)
    for position, shards_of in cuts:
        steps = jnp.exp(jax.random.uniform(jax.random.fold_in(own, position), (shards_of,), jnp.float32, least / len(cuts), largest / len(cuts)))
        gain = gain * jnp.repeat(steps, extent[position] // shards_of).reshape([-1 if axis == position else 1 for axis in range(len(extent))])
    return gain


def gaussian(rng, shape, width, most, split=(), kind=jnp.bfloat16):
    drawn = width * jax.random.normal(rng, shape, jnp.float32)
    if split:
        drawn = drawn * steps_of(rng, shape, split, -0.22, 0.18)
    return jnp.clip(drawn, -most, most).astype(kind)


def gaussian_with(own_key, dims, deviation, reach, pieces, heavy, kind=jnp.bfloat16):
    values = deviation * jax.random.normal(own_key, dims, jnp.float32)
    if pieces:
        values = values * steps_of(own_key, dims, pieces, -0.22, 0.18)
    return jnp.clip(spiked(values, jax.random.fold_in(own_key, 3), *heavy), -reach, reach).astype(kind)


def setup_inputs(seed: int = 0) -> dict:
    key_list = jax.random.split(jax.random.key(seed), 6)
    cotangent = gaussian(key_list[0], (NLON, C, NLAT), 1.0, 6.0, ((0, 32), (2, 8)))
    winds = jnp.clip(jax.random.uniform(key_list[1], (NLON, 2 * LEV, NLAT), jnp.float32, -0.44921875, 0.44921875) * steps_of(key_list[1], (NLON, 2 * LEV, NLAT), ((0, 32), (2, 8)), -0.4, 0.0), -0.44921875, 0.44921875).astype(jnp.bfloat16)
    filter_ops = gaussian_with(key_list[2], (NOPS, NLON, NLON), NLON ** -0.5, 0.3125, ((0, 8), (1, 32)), (1, 2, 32, 2.75))
    block_band = draw_block_band(jax.random.fold_in(key_list[5], 71), 0)
    block_row = set_ends(jax.random.randint(key_list[4], (NOPS,), 0, LAT_DEV), jax.random.fold_in(key_list[4], 1), 0, LAT_DEV - 1).astype(jnp.int32)
    return dict(cotangent=cotangent, winds=winds, filter_ops=filter_ops, block_band=block_band, block_row=block_row)


def adjoint_advection(centre, east_coef, west_coef, north_coef, south_coef):
    east_side = jnp.roll(centre, -1, axis=1)
    west_side = jnp.roll(centre, 1, axis=1)
    zero_row = jnp.zeros_like(centre[:1])
    north_side = jnp.concatenate([centre[1:], zero_row], axis=0)
    south_side = jnp.concatenate([zero_row, centre[:-1]], axis=0)
    return (centre + east_coef * (east_side - centre) + west_coef * (centre - west_side)
            + north_coef * (north_side - centre) + south_coef * (centre - south_side))


def reference(cotangent, winds, filter_ops, block_band, block_row):
    cot_rows = jnp.transpose(cotangent, (2, 0, 1))
    wind_rows = jnp.transpose(winds, (2, 0, 1))
    courant_x = wind_rows[:, :, :LEV].astype(jnp.float32)
    courant_y = wind_rows[:, :, LEV:].astype(jnp.float32)
    interior = (jnp.arange(NLAT) < NLAT - 1).astype(jnp.float32)[:, None, None]
    courant_y = courant_y * interior
    east_coef = jnp.maximum(courant_x, 0.0)
    west_coef = jnp.roll(jnp.minimum(courant_x, 0.0), 1, axis=1)
    north_coef = jnp.maximum(courant_y, 0.0)
    south_coef = jnp.concatenate([jnp.zeros_like(courant_y[:1]), jnp.minimum(courant_y, 0.0)[:-1]], axis=0)
    block_rows = (block_band * LAT_DEV + block_row).astype(jnp.int32)
    fields = jnp.moveaxis(cot_rows.reshape(NLAT, NLON, VAR, LEV), 2, 0)

    def apply_block(block_pair):
        return jnp.dot(block_pair[0].T, block_pair[1], preferred_element_type=jnp.float32)

    def one_field(field):
        adjoint = field.astype(jnp.float32)
        for substep in range(NSUB):
            rounded = adjoint.astype(jnp.bfloat16)
            widened = lax.optimization_barrier(rounded).astype(jnp.float32)
            correction = lax.map(apply_block, (filter_ops, rounded[block_rows]))
            smoothed = widened.at[block_rows].add(correction).astype(jnp.bfloat16)
            centre = lax.optimization_barrier(smoothed).astype(jnp.float32)
            adjoint = adjoint_advection(centre, east_coef, west_coef, north_coef, south_coef)
        return adjoint

    results = lax.map(one_field, fields)
    merged = jnp.moveaxis(results, 0, 2).reshape(NLAT, NLON, VAR * LEV)
    return jnp.transpose(merged, (1, 2, 0))
```

```python
import functools

import jax
import jax.numpy as jnp
from jax import lax
from jax.experimental import pallas as pl
from jax.experimental.pallas import tpu as pltpu
from jax.sharding import PartitionSpec as P

VAR = 5
LEV = 32
COLS = VAR * LEV
XS = 45
ROWS = 48
LANES = 128
BANDS = 8
NLON = 1440
LON_DEV = 32
TARGETS = 16
BLOCKS = 16
WIRE = 192
PACK = 120

F32 = jnp.float32
BF16 = jnp.bfloat16
VM = pl.BlockSpec(memory_space=pltpu.VMEM)
SM = pl.BlockSpec(memory_space=pltpu.SMEM)


def shape(dims, kind):
    return jax.ShapeDtypeStruct(dims, kind)


def params(mib):
    return pltpu.CompilerParams(vmem_limit_bytes=mib * 2**20)


def iotas(dims):
    return (
        lax.broadcasted_iota(jnp.int32, dims, 0),
        lax.broadcasted_iota(jnp.int32, dims, 1),
    )


def lanes_below(value, limit):
    lane = lax.broadcasted_iota(jnp.int32, value.shape, 1)
    return jnp.where(lane < limit, value, jnp.zeros_like(value))


def dot_nt(a, b):
    return lax.dot_general(a, b, (((1,), (1,)), ((), ())), preferred_element_type=F32)


def dot_tn(a, b):
    return lax.dot_general(a, b, (((0,), (0,)), ((), ())), preferred_element_type=F32)


def slot(block):
    return (block % 2) * BANDS + block // 2


def operator_kernel(core_ref, ops_ref, own_ref, send_ref):
    core = core_ref[0]
    for t in range(TARGETS):
        tiles = []
        for parity in range(2):
            start = XS * (2 * t + parity) - 1
            total = None
            first = max(start, 0) // LANES * LANES
            spans = [(first, min(first + 2 * LANES, NLON))]
            if start < 0:
                spans.append(((NLON - 1) // LANES * LANES, NLON))
            if start + XS + 2 > NLON:
                spans.append((0, LANES))
            for low, high in spans:
                row, lane = iotas((ROWS, high - low))
                wanted = start + row
                wanted = jnp.where(wanted < 0, wanted + NLON, wanted)
                wanted = jnp.where(wanted >= NLON, wanted - NLON, wanted)
                hit = (lane + low == wanted) & (row < XS + 2)
                pick = jnp.where(hit, 1.0, 0.0).astype(BF16)
                window = ops_ref[:, :, low:high].reshape(2 * ROWS, high - low)
                part = dot_nt(pick, window)
                total = part if total is None else total + part
            tiles.append(total)
        rows = slice(ROWS * t, ROWS * (t + 1))
        mine = core == 0
        own_ref[rows, :] = jnp.where(mine, tiles[0], tiles[1]).astype(BF16)
        send_ref[rows, :] = jnp.where(mine, tiles[1], tiles[0]).astype(BF16)


def prepare_operators(core, ops):
    out = shape((TARGETS * ROWS, 2 * ROWS), BF16)
    return pl.pallas_call(
        operator_kernel,
        out_shape=(out, out),
        in_specs=[SM, VM],
        out_specs=(VM, VM),
        compiler_params=params(16),
        name="operators",
    )(core, ops)


def pick_weights(me, band_ref, row_ref):
    sub, lane = iotas((24, LANES))
    target = jnp.full((24, LANES), -1, jnp.int32)
    for block in range(BLOCKS):
        wanted = jnp.where(band_ref[block] == me, row_ref[block], -1)
        target = jnp.where(sub == slot(block), wanted, target)
    target = jnp.where((sub >= 16) & (sub == 15 + me), 0, target)
    target = jnp.where((sub >= 16) & (sub == 17 + me), LANES - 1, target)
    return jnp.where(lane == target, 1.0, 0.0).astype(BF16)


def pack_messages(main_ref, rest_ref, send_ref):
    for d in range(BANDS):
        rest = None
        for e in range(3):
            rows = slice((e * 8 + d) * ROWS, (e * 8 + d + 1) * ROWS)
            send_ref[d, e * ROWS : (e + 1) * ROWS, :] = main_ref[rows, :].astype(BF16)
            piece = rest_ref[rows, :]
            if e < 2:
                piece = lanes_below(piece, LEV)
            if e:
                piece = pltpu.roll(piece, LEV * e, axis=1)
            rest = piece if rest is None else rest + piece
        send_ref[d, 3 * ROWS :, :] = rest.astype(BF16)


def clear(*refs):
    for ref in refs:
        ref[...] = jnp.zeros(ref.shape, ref.dtype)


def pick_kernel(me_ref, band_ref, row_ref, cells_ref, winds_ref, send_ref, east_ref, west_ref, main_ref, rest_ref):
    clear(main_ref, rest_ref)
    weights = pick_weights(me_ref[0], band_ref, row_ref)
    blank = jnp.zeros((2 * LEV, LANES), BF16)

    def body(x, carry):
        main = dot_nt(weights, cells_ref[x, :LANES, :])
        tail = jnp.concatenate([cells_ref[x, LANES:, :], winds_ref[x, LEV:, :], blank], axis=0)
        rest = dot_nt(weights, tail)
        main_ref[pl.ds(x + 1, 24, stride=ROWS), :] = main
        rest_ref[pl.ds(x + 1, 24, stride=ROWS), :] = rest
        return carry

    lax.fori_loop(0, XS, body, 0, unroll=5)
    pack_messages(main_ref, rest_ref, send_ref)
    east_ref[:COLS, :] = cells_ref[XS - 1]
    east_ref[COLS:, :] = winds_ref[XS - 1, :LEV, :]
    west_ref[...] = cells_ref[0]


STAGE = pltpu.VMEM((24 * ROWS, LANES), F32)


def pick_rows(me, band, row, cells, winds):
    return pl.pallas_call(
        pick_kernel,
        out_shape=(
            shape((BANDS, WIRE, LANES), BF16),
            shape((COLS + LEV, LANES), BF16),
            shape((COLS, LANES), BF16),
        ),
        in_specs=[SM, SM, SM, VM, VM],
        out_specs=(VM, VM, VM),
        scratch_shapes=[STAGE, STAGE],
        compiler_params=params(16),
        name="pick",
    )(me, band, row, cells, winds)


def unpack_kernel(me_ref, recv_ref, rows_ref, halo_ref):
    me = me_ref[0]
    total = recv_ref[0].astype(F32)
    for s in range(1, BANDS):
        total = total + recv_ref[s].astype(F32)
    rows_ref[: 2 * ROWS, :] = total[: 2 * ROWS].astype(BF16)
    rows_ref[2 * ROWS :, :] = lanes_below(total[3 * ROWS :], 2 * LEV).astype(BF16)
    for at, (near, there) in enumerate(((me - 1, me > 0), (me + 1, me < BANDS - 1))):
        source = jnp.clip(near, 0, BANDS - 1)
        message = recv_ref[source].astype(F32)
        main = message[2 * ROWS : 3 * ROWS]
        rest = lanes_below(pltpu.roll(message[3 * ROWS :], 2 * LEV, axis=1), 2 * LEV)
        halo_ref[2 * at] = jnp.where(there, main, 0.0)
        halo_ref[2 * at + 1] = jnp.where(there, rest, 0.0)


def unpack_rows(me, recv):
    return pl.pallas_call(
        unpack_kernel,
        out_shape=(shape((3 * ROWS, LANES), BF16), shape((4, ROWS, LANES), F32)),
        in_specs=[SM, VM],
        out_specs=(VM, VM),
        compiler_params=params(16),
        name="unpack",
    )(me, recv)


def spread_blocks(rows_ref):
    first = rows_ref[:ROWS, :]
    second = rows_ref[ROWS : 2 * ROWS, :]
    rest = rows_ref[2 * ROWS :, :].astype(F32)
    lower = lanes_below(rest, LEV)
    upper = rest - lower
    blank = jnp.zeros_like(first)
    return jnp.concatenate(
        [
            jnp.concatenate([first, blank, lower.astype(BF16)], axis=1),
            jnp.concatenate([blank, second, upper.astype(BF16)], axis=1),
        ],
        axis=0,
    )


def product_kernel(rows_ref, other_ref, own_ops_ref, other_ops_ref, out_ref):
    mine = spread_blocks(rows_ref)
    theirs = spread_blocks(other_ref)
    for q in range(4):
        span = slice(4 * ROWS * q, 4 * ROWS * (q + 1))
        made = jnp.dot(own_ops_ref[span, :], mine, preferred_element_type=F32)
        made = made + jnp.dot(other_ops_ref[span, :], theirs, preferred_element_type=F32)
        for s in range(4):
            part = made[ROWS * s : ROWS * (s + 1)]
            rest = part[:, 2 * LANES :]
            t = 4 * q + s
            out_ref[t, :ROWS, :] = part[:, :LANES].astype(BF16)
            out_ref[t, ROWS : 2 * ROWS, :] = part[:, LANES : 2 * LANES].astype(BF16)
            packed = rest[: ROWS // 2] + pltpu.roll(rest[ROWS // 2 :], 2 * LEV, axis=1)
            out_ref[t, 2 * ROWS :, :] = packed.astype(BF16)


def products(rows, other, own_ops, other_ops):
    return pl.pallas_call(
        product_kernel,
        out_shape=shape((TARGETS, PACK, LANES), BF16),
        in_specs=[VM] * 4,
        out_specs=VM,
        compiler_params=params(24),
        name="product",
    )(rows, other, own_ops, other_ops)


def total_kernel(recv_ref, out_ref):
    total = recv_ref[0].astype(F32)
    for s in range(1, TARGETS):
        total = total + recv_ref[s].astype(F32)
    total = total.astype(BF16)
    for d in range(BANDS):
        out_ref[d] = total


def totals(recv):
    return pl.pallas_call(
        total_kernel,
        out_shape=shape((BANDS, PACK, LANES), BF16),
        in_specs=[VM],
        out_specs=VM,
        compiler_params=params(16),
        name="total",
    )(recv)


def stage_corrections(me, band_ref, row_ref, recv_ref, halo_ref, wind_halo_ref, main_ref, rest_ref):
    clear(main_ref, rest_ref)
    half = ROWS // 2
    for source in range(BANDS):
        packed = recv_ref[source, 2 * ROWS :, :].astype(F32)
        for b in range(2):
            at = (b * BANDS + source) * ROWS
            main_ref[at : at + ROWS, :] = recv_ref[source, b * ROWS : (b + 1) * ROWS, :].astype(F32)
            low = pltpu.roll(packed, LANES - LEV, axis=1) if b else packed
            high = pltpu.roll(packed, LEV if b else 2 * LEV, axis=1)
            rest_ref[at : at + half, :] = lanes_below(low, LEV)
            rest_ref[at + half : at + ROWS, :] = lanes_below(high, LEV)
    for at, (near, edge) in enumerate(((me - 1, LANES - 1), (me + 1, 0))):
        main = jnp.zeros((ROWS, LANES), F32)
        rest = jnp.zeros((ROWS, LANES), F32)
        for block in range(BLOCKS):
            hit = (band_ref[block] == near) & (row_ref[block] == edge)
            share = jnp.where(hit, 1.0, 0.0)
            k = slot(block) * ROWS
            main = main + share * main_ref[k : k + ROWS, :]
            rest = rest + share * rest_ref[k : k + ROWS, :]
        k = (16 + at) * ROWS
        main = halo_ref[2 * at] + main
        rest = lanes_below(halo_ref[2 * at + 1], LEV) + rest
        main_ref[k : k + ROWS, :] = main.astype(BF16).astype(F32)
        rest_ref[k : k + ROWS, :] = rest.astype(BF16).astype(F32)
    wind = wind_halo_ref[1]
    rest_ref[18 * ROWS : 19 * ROWS, :] = wind - lanes_below(wind, LEV)


def place_weights(me, band_ref, row_ref):
    sub, lane = iotas((24, 2 * LANES))
    target = jnp.full((24, 2 * LANES), -1, jnp.int32)
    for block in range(BLOCKS):
        wanted = jnp.where(band_ref[block] == me, row_ref[block], -1)
        target = jnp.where(sub == slot(block), wanted, target)
    target = jnp.where((sub == 16) | (sub == 18), LANES, target)
    target = jnp.where(sub == 17, 2 * LANES - 1, target)
    return jnp.where(lane == target, 1.0, 0.0).astype(BF16)


def smooth_all(weights, cells_ref, west_ref, east_ref, main_ref, rest_ref, smooth_ref, edge_ref, wind_ref):
    def placed(r):
        main = main_ref[pl.ds(r, 24, stride=ROWS), :].astype(BF16)
        rest = rest_ref[pl.ds(r, 24, stride=ROWS), :].astype(BF16)
        return dot_tn(main, weights), dot_tn(rest, weights)

    def store(r, base):
        main, rest = placed(r)
        base = base.astype(F32)
        smooth_ref[r, :LANES, :] = (base[:LANES] + main[:, :LANES]).astype(BF16).astype(F32)
        smooth_ref[r, LANES:, :] = (base[LANES:] + rest[:LEV, :LANES]).astype(BF16).astype(F32)
        return main, rest

    store(0, west_ref[:COLS, :])
    store(XS + 1, east_ref[...])

    def body(x, carry):
        main, rest = store(x + 1, cells_ref[x])
        edge_ref[x, :LANES, :] = main[:, LANES:]
        edge_ref[x, LANES:, :] = rest[:LEV, LANES:]
        wind_ref[x] = rest[LEV : 2 * LEV, LANES:]
        return carry

    lax.fori_loop(0, XS, body, 0, unroll=3)


def stencil(x, top, winds_ref, west_ref, smooth_ref, edge_ref, wind_ref):
    lane = lax.broadcasted_iota(jnp.int32, (LEV, LANES), 1)
    courant = winds_ref[x].astype(F32)
    before = winds_ref[jnp.maximum(x - 1, 0), :LEV, :].astype(F32)
    before = jnp.where(x == 0, west_ref[COLS:, :].astype(F32), before)
    across = courant[:LEV]
    along = jnp.where(top & (lane == LANES - 1), 0.0, courant[LEV:])
    south_along = jnp.where(lane == 0, wind_ref[x], pltpu.roll(along, 1, axis=1))
    east = jnp.maximum(across, 0.0)
    west = jnp.minimum(before, 0.0)
    north = jnp.maximum(along, 0.0)
    south = jnp.minimum(south_along, 0.0)
    centre = 1.0 - east + west - north + south
    made = []
    for v in range(VAR):
        span = slice(v * LEV, (v + 1) * LEV)
        here = smooth_ref[x + 1, span, :]
        edge = edge_ref[x, span, :]
        above = jnp.where(lane == LANES - 1, edge, pltpu.roll(here, LANES - 1, axis=1))
        below = jnp.where(lane == 0, edge, pltpu.roll(here, 1, axis=1))
        made.append(
            centre * here
            + (east * smooth_ref[x + 2, span, :] - west * smooth_ref[x, span, :])
            + (north * above - south * below)
        )
    return made


SCRATCH = [
    STAGE,
    STAGE,
    pltpu.VMEM((XS + 2, COLS, LANES), F32),
    pltpu.VMEM((XS, COLS, LANES), F32),
    pltpu.VMEM((XS, LEV, LANES), F32),
]


def first_kernel(
    me_ref, band_ref, row_ref, cells_ref, winds_ref, west_ref, east_ref, recv_ref, halo_ref, wind_halo_ref,
    out_ref, send_ref, to_east_ref, to_west_ref, main_ref, rest_ref, smooth_ref, edge_ref, wind_ref,
):
    me = me_ref[0]
    stage_corrections(me, band_ref, row_ref, recv_ref, halo_ref, wind_halo_ref, main_ref, rest_ref)
    smooth_all(
        place_weights(me, band_ref, row_ref), cells_ref, west_ref, east_ref, main_ref, rest_ref, smooth_ref, edge_ref,
        wind_ref,
    )
    clear(main_ref, rest_ref)
    weights = pick_weights(me, band_ref, row_ref)
    top = me == BANDS - 1
    blank = jnp.zeros((3 * LEV, LANES), BF16)

    def body(x, carry):
        made = [m.astype(BF16) for m in stencil(x, top, winds_ref, west_ref, smooth_ref, edge_ref, wind_ref)]
        for v in range(VAR):
            out_ref[x, v * LEV : (v + 1) * LEV, :] = made[v]
        main = dot_nt(weights, jnp.concatenate(made[:4], axis=0))
        rest = dot_nt(weights, jnp.concatenate([made[4], blank], axis=0))
        main_ref[pl.ds(x + 1, 24, stride=ROWS), :] = main
        rest_ref[pl.ds(x + 1, 24, stride=ROWS), :] = rest
        return carry

    lax.fori_loop(0, XS, body, 0, unroll=3)
    pack_messages(main_ref, rest_ref, send_ref)
    to_east_ref[...] = out_ref[XS - 1]
    to_west_ref[...] = out_ref[0]


def first_substep(*args):
    return pl.pallas_call(
        first_kernel,
        out_shape=(
            shape((XS, COLS, LANES), BF16),
            shape((BANDS, WIRE, LANES), BF16),
            shape((COLS, LANES), BF16),
            shape((COLS, LANES), BF16),
        ),
        in_specs=[SM] * 3 + [VM] * 7,
        out_specs=(VM,) * 4,
        scratch_shapes=SCRATCH,
        compiler_params=params(32),
        name="first",
    )(*args)


CHUNK = 9


def last_kernel(
    me_ref, band_ref, row_ref, cells_ref, winds_ref, west_ref, east_ref, recv_ref, halo_ref, wind_halo_ref, wind_west_ref,
    out_ref, main_ref, rest_ref, smooth_ref, edge_ref, wind_ref,
):
    me = me_ref[0]
    step = pl.program_id(0)

    @pl.when(step == 0)
    def _():
        stage_corrections(me, band_ref, row_ref, recv_ref, halo_ref, wind_halo_ref, main_ref, rest_ref)
        smooth_all(
            place_weights(me, band_ref, row_ref), cells_ref, west_ref, east_ref, main_ref, rest_ref, smooth_ref,
            edge_ref, wind_ref,
        )

    top = me == BANDS - 1

    def body(y, carry):
        x = step * CHUNK + y
        made = stencil(x, top, winds_ref, wind_west_ref, smooth_ref, edge_ref, wind_ref)
        for v in range(VAR):
            out_ref[y, v * LEV : (v + 1) * LEV, :] = made[v]
        return carry

    lax.fori_loop(0, CHUNK, body, 0, unroll=3)


def last_substep(*args):
    return pl.pallas_call(
        last_kernel,
        grid=(XS // CHUNK,),
        out_shape=shape((XS, COLS, LANES), F32),
        in_specs=[SM] * 3 + [VM] * 8,
        out_specs=pl.BlockSpec((CHUNK, COLS, LANES), lambda i: (i, 0, 0)),
        scratch_shapes=SCRATCH,
        compiler_params=params(32),
        name="last",
    )(*args)


SWAP = [(i, i ^ 1) for i in range(LON_DEV)]
EASTWARD = [(i, (i + 1) % LON_DEV) for i in range(LON_DEV)]
WESTWARD = [(i, (i - 1) % LON_DEV) for i in range(LON_DEV)]
SAME_CORE = [[2 * t + core for t in range(TARGETS)] for core in range(2)]


def corrections(me, recv, own_ops, other_ops):
    rows, halo = unpack_rows(me, recv)
    other = lax.ppermute(rows, "lon", SWAP)
    partial = products(rows, other, own_ops, other_ops)
    swapped = lax.all_to_all(partial, "lon", 0, 0, tiled=True, axis_index_groups=SAME_CORE)
    return lax.all_to_all(totals(swapped), "lat", 0, 0, tiled=True), halo


def shards(cotangent, winds, filter_ops, block_band, block_row):
    me = lax.axis_index("lat").astype(jnp.int32).reshape(1)
    core = (lax.axis_index("lon") % 2).astype(jnp.int32).reshape(1)
    own_ops, send_ops = prepare_operators(core, jnp.pad(filter_ops, ((0, 0), (1, 2), (0, 0))))
    other_ops = lax.ppermute(send_ops, "lon", SWAP)
    send, to_east, to_west = pick_rows(me, block_band, block_row, cotangent, winds)
    west = lax.ppermute(to_east, "lon", EASTWARD)
    east = lax.ppermute(to_west, "lon", WESTWARD)
    recv = lax.all_to_all(send, "lat", 0, 0, tiled=True)
    given, halo = corrections(me, recv, own_ops, other_ops)
    state, send, to_east, to_west = first_substep(
        me, block_band, block_row, cotangent, winds, west, east, given, halo, halo
    )
    west2 = lax.ppermute(to_east, "lon", EASTWARD)
    east2 = lax.ppermute(to_west, "lon", WESTWARD)
    recv = lax.all_to_all(send, "lat", 0, 0, tiled=True)
    given, halo2 = corrections(me, recv, own_ops, other_ops)
    return last_substep(me, block_band, block_row, state, winds, west2, east2, given, halo2, halo, west)


def solution(mesh):
    return jax.shard_map(
        shards,
        mesh=mesh,
        in_specs=(P("lon", None, "lat"), P("lon", None, "lat"), P("lat", "lon", None), P(), P()),
        out_specs=P("lon", None, "lat"),
        check_vma=False,
    )
```

```python
import jax
import jax.numpy as jnp
from jax import lax
from jax.experimental import pallas as pl
from jax.experimental.pallas import tpu as pltpu
from jax.sharding import PartitionSpec as P

VAR = 5
LEV = 32
COLS = VAR * LEV
XS = 45
ROWS = 48
LANES = 128
BANDS = 8
NLON = 1440
LON_DEV = 32
TARGETS = 16
BLOCKS = 16
PIECES = 7
WIRE = (PIECES + 4) * ROWS
PACK = 120
HALO = 72
CHUNK = 9

F32 = jnp.float32
BF16 = jnp.bfloat16
VM = pl.BlockSpec(memory_space=pltpu.VMEM)
SM = pl.BlockSpec(memory_space=pltpu.SMEM)


def shape(dims, kind):
    return jax.ShapeDtypeStruct(dims, kind)


def params(mib):
    return pltpu.CompilerParams(vmem_limit_bytes=mib * 2**20)


def iotas(dims):
    return (
        lax.broadcasted_iota(jnp.int32, dims, 0),
        lax.broadcasted_iota(jnp.int32, dims, 1),
    )


def lanes_below(value, limit):
    lane = lax.broadcasted_iota(jnp.int32, value.shape, 1)
    return jnp.where(lane < limit, value, jnp.zeros_like(value))


def dot_nt(a, b):
    return lax.dot_general(a, b, (((1,), (1,)), ((), ())), preferred_element_type=F32)


def dot_tn(a, b):
    return lax.dot_general(a, b, (((0,), (0,)), ((), ())), preferred_element_type=F32)


def operator_kernel(meta_ref, ops_ref, own_ref, send_ref):
    core = meta_ref[1]
    for t in range(TARGETS):
        tiles = []
        for parity in range(2):
            start = XS * (2 * t + parity) - 1
            total = None
            first = max(start, 0) // LANES * LANES
            spans = [(first, min(first + 2 * LANES, NLON))]
            if start < 0:
                spans.append(((NLON - 1) // LANES * LANES, NLON))
            if start + XS + 2 > NLON:
                spans.append((0, LANES))
            for low, high in spans:
                row, lane = iotas((ROWS, high - low))
                wanted = start + row
                wanted = jnp.where(wanted < 0, wanted + NLON, wanted)
                wanted = jnp.where(wanted >= NLON, wanted - NLON, wanted)
                hit = (lane + low == wanted) & (row < XS + 2)
                pick = jnp.where(hit, 1.0, 0.0).astype(BF16)
                window = ops_ref[:, :, low:high].reshape(2 * ROWS, high - low)
                part = dot_nt(pick, window)
                total = part if total is None else total + part
            tiles.append(total)
        rows = slice(ROWS * t, ROWS * (t + 1))
        mine = core == 0
        own_ref[rows, :] = jnp.where(mine, tiles[0], tiles[1]).astype(BF16)
        send_ref[rows, :] = jnp.where(mine, tiles[1], tiles[0]).astype(BF16)


def prepare_operators(meta, ops):
    out = shape((TARGETS * ROWS, 2 * ROWS), BF16)
    return pl.pallas_call(
        operator_kernel,
        out_shape=(out, out),
        in_specs=[SM, VM],
        out_specs=(VM, VM),
        compiler_params=params(16),
        name="operators",
    )(meta, ops)


def slot(block):
    return (block % 2) * BANDS + block // 2


def global_row(meta_ref, block):
    return meta_ref[2 + block] * LANES + meta_ref[2 + BLOCKS + block]


def clear_rims(ref, count):
    blank = jnp.zeros((count, LANES), ref.dtype)
    for r in (0, XS + 1, XS + 2):
        ref[pl.ds(r, count, stride=ROWS), :] = blank


def pick_weights(meta_ref):
    me = meta_ref[0]
    sub, lane = iotas((PIECES * BANDS, LANES))
    target = jnp.full(sub.shape, -1, jnp.int32)
    for block in range(BLOCKS):
        at = global_row(meta_ref, block) - me * LANES
        for near in range(3):
            k = near * 2 * BANDS + slot(block)
            target = jnp.where(sub == k, at + (near - 1), target)
    base = 6 * BANDS
    target = jnp.where((sub >= base) & (sub == base - 1 + me), 0, target)
    target = jnp.where((sub >= base) & (sub == base + 1 + me), LANES - 1, target)
    return jnp.where(lane == target, 1.0, 0.0).astype(BF16)


def keep(value, *starts):
    lane = lax.broadcasted_iota(jnp.int32, value.shape, 1)
    hit = (lane >= starts[0]) & (lane < starts[0] + LEV)
    for start in starts[1:]:
        hit = hit | ((lane >= start) & (lane < start + LEV))
    return jnp.where(hit, value, jnp.zeros_like(value))


def pull(value, start):
    moved = pltpu.roll(value, LANES - start, axis=1) if start else value
    return lanes_below(moved, LEV)


def pack_messages(main_ref, rest_ref, send_ref):
    for d in range(BANDS):
        pieces = []
        for p in range(PIECES):
            rows = slice((p * BANDS + d) * ROWS, (p * BANDS + d + 1) * ROWS)
            send_ref[d, p * ROWS : (p + 1) * ROWS, :] = main_ref[rows, :].astype(BF16)
            pieces.append(rest_ref[rows, :])
        tails = [
            pieces[2 + e] + pltpu.roll(keep(pieces[4 + e], 0), 3 * LEV, axis=1) for e in range(2)
        ]
        tails.append(keep(pieces[0], 0, 2 * LEV) + pltpu.roll(keep(pieces[1], 0, 2 * LEV), LEV, axis=1))
        tails.append(pieces[6])
        for p, tail in enumerate(tails):
            at = (PIECES + p) * ROWS
            send_ref[d, at : at + ROWS, :] = tail.astype(BF16)


def clear(*refs):
    for ref in refs:
        ref[...] = jnp.zeros(ref.shape, ref.dtype)


def pick_kernel(meta_ref, cells_ref, winds_ref, send_ref, east_ref, west_ref, main_ref, rest_ref):
    step = pl.program_id(0)

    @pl.when(step == 0)
    def _():
        clear_rims(main_ref, PIECES * BANDS)
        clear_rims(rest_ref, PIECES * BANDS)
        west_ref[...] = cells_ref[0]

    weights = pick_weights(meta_ref)
    blank = jnp.zeros((LEV, LANES), BF16)
    for y in range(CHUNK):
        main = dot_nt(weights, cells_ref[y, :LANES, :])
        tail = jnp.concatenate([cells_ref[y, LANES:, :], winds_ref[y], blank], axis=0)
        rest = dot_nt(weights, tail)
        at = pl.ds(step * CHUNK + y + 1, PIECES * BANDS, stride=ROWS)
        main_ref[at, :] = main
        rest_ref[at, :] = rest

    @pl.when(step == XS // CHUNK - 1)
    def _():
        pack_messages(main_ref, rest_ref, send_ref)
        east_ref[:COLS, :] = cells_ref[CHUNK - 1]
        east_ref[COLS:, :] = winds_ref[CHUNK - 1, :LEV, :]


STAGE = pltpu.VMEM((24 * ROWS, LANES), F32)
PICKED = pltpu.VMEM((PIECES * BANDS * ROWS, LANES), F32)


def pick_rows(meta, cells, winds):
    return pl.pallas_call(
        pick_kernel,
        grid=(XS // CHUNK,),
        out_shape=(
            shape((BANDS, WIRE, LANES), BF16),
            shape((COLS + LEV, LANES), BF16),
            shape((COLS, LANES), BF16),
        ),
        in_specs=[
            SM,
            pl.BlockSpec((CHUNK, COLS, LANES), lambda i: (i, 0, 0)),
            pl.BlockSpec((CHUNK, 2 * LEV, LANES), lambda i: (i, 0, 0)),
        ],
        out_specs=(VM, VM, VM),
        scratch_shapes=[PICKED, PICKED],
        compiler_params=params(24),
        name="pick",
    )(meta, cells, winds)


def unpack_kernel(meta_ref, recv_ref, rows_ref, context_ref, to_east_ref, to_west_ref, halo_ref):
    me = meta_ref[0]

    def added(tile):
        span = slice(tile * ROWS, (tile + 1) * ROWS)
        total = recv_ref[0, span, :].astype(F32)
        for s in range(1, BANDS):
            total = total + recv_ref[s, span, :].astype(F32)
        return total

    tiles = [added(p) for p in (0, 1, 2, 3, 4, 5, 7, 8, 9)]
    for p, tile in enumerate(tiles):
        context_ref[p * ROWS : (p + 1) * ROWS, :] = tile.astype(BF16)
    rows_ref[:ROWS, :] = tiles[2].astype(BF16)
    rows_ref[ROWS : 2 * ROWS, :] = tiles[3].astype(BF16)
    rest = lanes_below(tiles[6], LEV) + pltpu.roll(lanes_below(tiles[7], LEV), LEV, axis=1)
    rows_ref[2 * ROWS :, :] = rest.astype(BF16)
    clear(to_east_ref, to_west_ref)
    for at, p in enumerate((2, 3, 6, 7)):
        to_east_ref[at : at + 1, :] = tiles[p][XS : XS + 1]
        to_west_ref[at : at + 1, :] = tiles[p][1:2]
    for at, (near, there) in enumerate(((me - 1, me > 0), (me + 1, me < BANDS - 1))):
        source = jnp.clip(near, 0, BANDS - 1)
        main = recv_ref[source, 6 * ROWS : 7 * ROWS, :].astype(F32)
        rest = recv_ref[source, 10 * ROWS :, :].astype(F32)
        rest = pull(rest, 0) + pltpu.roll(pull(rest, 2 * LEV), LEV, axis=1)
        halo_ref[2 * at] = jnp.where(there, main, 0.0)
        halo_ref[2 * at + 1] = jnp.where(there, rest, 0.0)


def unpack_rows(meta, recv):
    edge = shape((8, LANES), F32)
    return pl.pallas_call(
        unpack_kernel,
        out_shape=(
            shape((3 * ROWS, LANES), BF16), shape((9 * ROWS, LANES), BF16), edge, edge, shape((4, ROWS, LANES), F32)
        ),
        in_specs=[SM, VM],
        out_specs=(VM,) * 5,
        compiler_params=params(16),
        name="unpack",
    )(meta, recv)


def spread_blocks(rows_ref):
    first = rows_ref[:ROWS, :]
    second = rows_ref[ROWS : 2 * ROWS, :]
    rest = rows_ref[2 * ROWS :, :].astype(F32)
    lower = lanes_below(rest, LEV)
    upper = rest - lower
    blank = jnp.zeros_like(first)
    return jnp.concatenate(
        [
            jnp.concatenate([first, blank, lower.astype(BF16)], axis=1),
            jnp.concatenate([blank, second, upper.astype(BF16)], axis=1),
        ],
        axis=0,
    )


def product_kernel(rows_ref, other_ref, own_ops_ref, other_ops_ref, out_ref):
    mine = spread_blocks(rows_ref)
    theirs = spread_blocks(other_ref)
    for q in range(4):
        span = slice(4 * ROWS * q, 4 * ROWS * (q + 1))
        made = jnp.dot(own_ops_ref[span, :], mine, preferred_element_type=F32)
        made = made + jnp.dot(other_ops_ref[span, :], theirs, preferred_element_type=F32)
        for s in range(4):
            part = made[ROWS * s : ROWS * (s + 1)]
            rest = part[:, 2 * LANES :]
            t = 4 * q + s
            out_ref[t, :ROWS, :] = part[:, :LANES].astype(BF16)
            out_ref[t, ROWS : 2 * ROWS, :] = part[:, LANES : 2 * LANES].astype(BF16)
            packed = rest[: ROWS // 2] + pltpu.roll(rest[ROWS // 2 :], 2 * LEV, axis=1)
            out_ref[t, 2 * ROWS :, :] = packed.astype(BF16)


def products(rows, other, own_ops, other_ops):
    return pl.pallas_call(
        product_kernel,
        out_shape=shape((TARGETS, PACK, LANES), BF16),
        in_specs=[VM] * 4,
        out_specs=VM,
        compiler_params=params(24),
        name="product",
    )(rows, other, own_ops, other_ops)


def total_kernel(meta_ref, recv_ref, *refs):
    out_ref = refs[-1]
    total = recv_ref[0].astype(F32)
    for s in range(1, TARGETS):
        total = total + recv_ref[s].astype(F32)
    total = total.astype(BF16)
    for d in range(BANDS):
        out_ref[d, :PACK, :] = total
    if len(refs) > 1:
        me = meta_ref[0]
        for d in range(BANDS):
            edge = jnp.where(d == me + 1, refs[0][1], jnp.zeros((HALO, LANES), BF16))
            out_ref[d, PACK:, :] = jnp.where(d == me - 1, refs[0][0], edge)


def totals(meta, recv, *halo):
    return pl.pallas_call(
        total_kernel,
        out_shape=shape((BANDS, PACK + (HALO if halo else 0), LANES), BF16),
        in_specs=[SM] + [VM] * (1 + len(halo)),
        out_specs=VM,
        compiler_params=params(16),
        name="total",
    )(meta, recv, *halo)


def stage_blocks(recv_ref, main_ref, rest_ref):
    half = ROWS // 2
    for source in range(BANDS):
        packed = recv_ref[source, 2 * ROWS : PACK, :].astype(F32)
        for b in range(2):
            at = (b * BANDS + source) * ROWS
            main_ref[at : at + ROWS, :] = recv_ref[source, b * ROWS : (b + 1) * ROWS, :].astype(F32)
            rest_ref[at : at + half, :] = pull(packed, b * LEV)
            rest_ref[at + half : at + ROWS, :] = pull(packed, (2 + b) * LEV)


def block_sum(meta_ref, row, main_ref, rest_ref):
    main = jnp.zeros((ROWS, LANES), F32)
    rest = jnp.zeros((ROWS, LANES), F32)
    for block in range(BLOCKS):
        share = jnp.where(global_row(meta_ref, block) == row, 1.0, 0.0)
        k = slot(block) * ROWS
        main = main + share * main_ref[k : k + ROWS, :]
        rest = rest + share * rest_ref[k : k + ROWS, :]
    return main, rest


def stage_corrections(meta_ref, recv_ref, halos, wind, main_ref, rest_ref):
    stage_blocks(recv_ref, main_ref, rest_ref)
    main_ref[18 * ROWS :, :] = jnp.zeros((6 * ROWS, LANES), F32)
    rest_ref[18 * ROWS :, :] = jnp.zeros((6 * ROWS, LANES), F32)
    me = meta_ref[0]
    for at, row in enumerate((me * LANES - 1, (me + 1) * LANES)):
        main, rest = block_sum(meta_ref, row, main_ref, rest_ref)
        k = (16 + at) * ROWS
        main_ref[k : k + ROWS, :] = (halos[at][0] + main).astype(BF16).astype(F32)
        rest_ref[k : k + ROWS, :] = (halos[at][1] + rest).astype(BF16).astype(F32)
    rest_ref[18 * ROWS : 19 * ROWS, :] = keep(wind, LEV)


def rows_kernel(meta_ref, context_ref, west_ref, east_ref, recv_ref, out_ref, main_ref, rest_ref):
    stage_blocks(recv_ref, main_ref, rest_ref)
    me = meta_ref[0]
    sub = lax.broadcasted_iota(jnp.int32, (ROWS, LANES), 0)
    inner = (sub >= 1) & (sub <= XS)

    def tile(p):
        return context_ref[p * ROWS : (p + 1) * ROWS, :].astype(F32)

    def rimmed(value, at):
        value = jnp.where(sub == 0, west_ref[at : at + 1, :], value)
        return jnp.where(sub == XS + 1, east_ref[at : at + 1, :], value)

    def rounded(value):
        return value.astype(BF16).astype(F32)

    def wide(value):
        value = value + pltpu.roll(value, LEV, axis=1)
        return value + pltpu.roll(value, 2 * LEV, axis=1)

    last = None
    behind = tile(8)
    for e in range(2):
        row = global_row(meta_ref, 2 * me + e)
        tail = rimmed(tile(6 + e), 2 + e)
        mains = [tile(e), rimmed(tile(2 + e), e), tile(4 + e)]
        rests = [pull(behind, e * LEV), pull(tail, 0), pull(tail, 3 * LEV)]
        for near in range(3):
            main, rest = block_sum(meta_ref, row + (near - 1), main_ref, rest_ref)
            mains[near] = rounded(mains[near] + main)
            rests[near] = rounded(rests[near] + rest)
        across = pull(tail, LEV)
        along = pull(tail, 2 * LEV)
        before = pull(behind, (2 + e) * LEV)
        east = jnp.maximum(across, 0.0)
        west = jnp.minimum(pltpu.roll(across, 1, axis=0), 0.0)
        north = jnp.where(row == BANDS * LANES - 1, 0.0, jnp.maximum(along, 0.0))
        south = jnp.minimum(before, 0.0)
        coefs = (east, west, north, south)

        def moved(coefs, values):
            east, west, north, south = coefs
            centre = 1.0 - east + west - north + south
            below, here, above = values
            made = (
                centre * here
                + (east * pltpu.roll(here, ROWS - 1, axis=0) - west * pltpu.roll(here, 1, axis=0))
                + (north * above - south * below)
            )
            return jnp.where(inner, made, 0.0)

        out_ref[e * ROWS : (e + 1) * ROWS, :] = moved([wide(c) for c in coefs], mains).astype(BF16)
        rest = lanes_below(moved(coefs, rests), LEV)
        last = rest if e == 0 else last + pltpu.roll(rest, LEV, axis=1)
    out_ref[2 * ROWS :, :] = last.astype(BF16)


def next_rows(*args):
    return pl.pallas_call(
        rows_kernel,
        out_shape=shape((3 * ROWS, LANES), BF16),
        in_specs=[SM] + [VM] * 4,
        out_specs=VM,
        scratch_shapes=[STAGE, STAGE],
        compiler_params=params(16),
        name="rows",
    )(*args)


def place_weights(meta_ref):
    sub, lane = iotas((24, 2 * LANES))
    target = jnp.full(sub.shape, -1, jnp.int32)
    for block in range(BLOCKS):
        at = global_row(meta_ref, block) - meta_ref[0] * LANES
        target = jnp.where(sub == slot(block), jnp.where((at >= 0) & (at < LANES), at, -1), target)
    target = jnp.where((sub == 16) | (sub == 18), LANES, target)
    target = jnp.where(sub == 17, 2 * LANES - 1, target)
    return jnp.where(lane == target, 1.0, 0.0).astype(BF16)


def smooth_all(weights, cells_ref, west_ref, east_ref, main_ref, rest_ref, smooth_ref, edge_ref, wind_ref):
    def placed(r):
        main = main_ref[pl.ds(r, 24, stride=ROWS), :].astype(BF16)
        rest = rest_ref[pl.ds(r, 24, stride=ROWS), :].astype(BF16)
        return dot_tn(main, weights), dot_tn(rest, weights)

    def store(r, base):
        main, rest = placed(r)
        base = base.astype(F32)
        smooth_ref[r, :LANES, :] = (base[:LANES] + main[:, :LANES]).astype(BF16).astype(F32)
        smooth_ref[r, LANES:, :] = (base[LANES:] + rest[:LEV, :LANES]).astype(BF16).astype(F32)
        return main, rest

    store(0, west_ref[:COLS, :])
    store(XS + 1, east_ref[...])

    def body(x, carry):
        main, rest = store(x + 1, cells_ref[x])
        edge_ref[x, :LANES, :] = main[:, LANES:]
        edge_ref[x, LANES:, :] = rest[:LEV, LANES:]
        wind_ref[x] = rest[LEV : 2 * LEV, LANES:]
        return carry

    lax.fori_loop(0, XS, body, 0, unroll=3)


def stencil(x, top, winds_ref, west_ref, smooth_ref, edge_ref, wind_ref):
    lane = lax.broadcasted_iota(jnp.int32, (LEV, LANES), 1)
    courant = winds_ref[x].astype(F32)
    before = winds_ref[jnp.maximum(x - 1, 0), :LEV, :].astype(F32)
    before = jnp.where(x == 0, west_ref[COLS:, :].astype(F32), before)
    across = courant[:LEV]
    along = jnp.where(top & (lane == LANES - 1), 0.0, courant[LEV:])
    south_along = jnp.where(lane == 0, wind_ref[x], pltpu.roll(along, 1, axis=1))
    east = jnp.maximum(across, 0.0)
    west = jnp.minimum(before, 0.0)
    north = jnp.maximum(along, 0.0)
    south = jnp.minimum(south_along, 0.0)
    centre = 1.0 - east + west - north + south
    made = []
    for v in range(VAR):
        span = slice(v * LEV, (v + 1) * LEV)
        here = smooth_ref[x + 1, span, :]
        edge = edge_ref[x, span, :]
        above = jnp.where(lane == LANES - 1, edge, pltpu.roll(here, LANES - 1, axis=1))
        below = jnp.where(lane == 0, edge, pltpu.roll(here, 1, axis=1))
        made.append(
            centre * here
            + (east * smooth_ref[x + 2, span, :] - west * smooth_ref[x, span, :])
            + (north * above - south * below)
        )
    return made


SCRATCH = [
    STAGE,
    STAGE,
    pltpu.VMEM((XS + 2, COLS, LANES), F32),
    pltpu.VMEM((XS, COLS, LANES), F32),
    pltpu.VMEM((XS, LEV, LANES), F32),
]


def first_kernel(
    meta_ref, cells_ref, winds_ref, west_ref, east_ref, recv_ref, halo_ref,
    out_ref, edges_ref, to_east_ref, to_west_ref, main_ref, rest_ref, smooth_ref, edge_ref, wind_ref,
):
    halos = [(halo_ref[2 * at], lanes_below(halo_ref[2 * at + 1], LEV)) for at in range(2)]
    stage_corrections(meta_ref, recv_ref, halos, halo_ref[1], main_ref, rest_ref)
    smooth_all(
        place_weights(meta_ref), cells_ref, west_ref, east_ref, main_ref, rest_ref, smooth_ref, edge_ref, wind_ref
    )
    clear_rims(main_ref, 2)
    clear_rims(rest_ref, 2)
    sub, lane = iotas((8, LANES))
    ends = jnp.where((lane == 0) & (sub == 0) | (lane == LANES - 1) & (sub == 1), 1.0, 0.0).astype(BF16)
    top = meta_ref[0] == BANDS - 1
    blank = jnp.zeros((3 * LEV, LANES), BF16)

    def body(x, carry):
        made = [m.astype(BF16) for m in stencil(x, top, winds_ref, west_ref, smooth_ref, edge_ref, wind_ref)]
        for v in range(VAR):
            out_ref[x, v * LEV : (v + 1) * LEV, :] = made[v]
        at = pl.ds(x + 1, 2, stride=ROWS)
        main_ref[at, :] = dot_nt(ends, jnp.concatenate(made[:4], axis=0))[:2]
        rest_ref[at, :] = dot_nt(ends, jnp.concatenate([made[4], blank], axis=0))[:2]
        return carry

    lax.fori_loop(0, XS, body, 0, unroll=3)
    for at in range(2):
        k = at * ROWS
        edges_ref[at, :ROWS, :] = main_ref[k : k + ROWS, :].astype(BF16)
        rest = rest_ref[k : k + ROWS, :]
        packed = rest[: ROWS // 2] + pltpu.roll(rest[ROWS // 2 :], LEV, axis=1)
        edges_ref[at, ROWS:, :] = packed.astype(BF16)
    to_east_ref[...] = out_ref[XS - 1]
    to_west_ref[...] = out_ref[0]


def first_substep(*args):
    return pl.pallas_call(
        first_kernel,
        out_shape=(
            shape((XS, COLS, LANES), BF16),
            shape((2, HALO, LANES), BF16),
            shape((COLS, LANES), BF16),
            shape((COLS, LANES), BF16),
        ),
        in_specs=[SM] + [VM] * 6,
        out_specs=(VM,) * 4,
        scratch_shapes=SCRATCH,
        compiler_params=params(32),
        name="first",
    )(*args)


def last_kernel(
    meta_ref, cells_ref, winds_ref, west_ref, east_ref, recv_ref, wind_halo_ref, wind_west_ref,
    out_ref, main_ref, rest_ref, smooth_ref, edge_ref, wind_ref,
):
    me = meta_ref[0]
    step = pl.program_id(0)

    @pl.when(step == 0)
    def _():
        halos = []
        for near, there in ((me - 1, me > 0), (me + 1, me < BANDS - 1)):
            source = jnp.clip(near, 0, BANDS - 1)
            main = recv_ref[source, PACK : PACK + ROWS, :].astype(F32)
            rest = recv_ref[source, PACK + ROWS :, :].astype(F32)
            rest = jnp.concatenate([pull(rest, 0), pull(rest, LEV)], axis=0)
            halos.append((jnp.where(there, main, 0.0), jnp.where(there, rest, 0.0)))
        stage_corrections(meta_ref, recv_ref, halos, wind_halo_ref[1], main_ref, rest_ref)
        smooth_all(
            place_weights(meta_ref), cells_ref, west_ref, east_ref, main_ref, rest_ref, smooth_ref, edge_ref, wind_ref
        )

    top = me == BANDS - 1

    def body(y, carry):
        x = step * CHUNK + y
        made = stencil(x, top, winds_ref, wind_west_ref, smooth_ref, edge_ref, wind_ref)
        for v in range(VAR):
            out_ref[y, v * LEV : (v + 1) * LEV, :] = made[v]
        return carry

    lax.fori_loop(0, CHUNK, body, 0, unroll=3)


def last_substep(*args):
    return pl.pallas_call(
        last_kernel,
        grid=(XS // CHUNK,),
        out_shape=shape((XS, COLS, LANES), F32),
        in_specs=[SM] + [VM] * 7,
        out_specs=pl.BlockSpec((CHUNK, COLS, LANES), lambda i: (i, 0, 0)),
        scratch_shapes=SCRATCH,
        compiler_params=params(32),
        name="last",
    )(*args)


SWAP = [(i, i ^ 1) for i in range(LON_DEV)]
EASTWARD = [(i, (i + 1) % LON_DEV) for i in range(LON_DEV)]
WESTWARD = [(i, (i - 1) % LON_DEV) for i in range(LON_DEV)]
SAME_CORE = [[2 * t + core for t in range(TARGETS)] for core in range(2)]


def by_lat(messages):
    return lax.all_to_all(messages, "lat", 0, 0, tiled=True)


def filtered(rows, own_ops, other_ops):
    other = lax.ppermute(rows, "lon", SWAP)
    partial = products(rows, other, own_ops, other_ops)
    return lax.all_to_all(partial, "lon", 0, 0, tiled=True, axis_index_groups=SAME_CORE)


def shards(cotangent, winds, filter_ops, block_band, block_row):
    me = lax.axis_index("lat").astype(jnp.int32).reshape(1)
    core = (lax.axis_index("lon") & 1).astype(jnp.int32).reshape(1)
    meta = jnp.concatenate([me, core, block_band, block_row])
    own_ops, send_ops = prepare_operators(meta, jnp.pad(filter_ops, ((0, 0), (1, 2), (0, 0))))
    other_ops = lax.ppermute(send_ops, "lon", SWAP)
    send, to_east, to_west = pick_rows(meta, cotangent, winds)
    west = lax.ppermute(to_east, "lon", EASTWARD)
    east = lax.ppermute(to_west, "lon", WESTWARD)
    rows, context, row_east, row_west, halo = unpack_rows(meta, by_lat(send))
    swapped = filtered(rows, own_ops, other_ops)
    row_from_west = lax.ppermute(row_east, "lon", EASTWARD)
    row_from_east = lax.ppermute(row_west, "lon", WESTWARD)
    given = by_lat(totals(meta, swapped))
    rows = next_rows(meta, context, row_from_west, row_from_east, given)
    swapped = filtered(rows, own_ops, other_ops)
    state, edges, to_east, to_west = first_substep(meta, cotangent, winds, west, east, given, halo)
    west2 = lax.ppermute(to_east, "lon", EASTWARD)
    east2 = lax.ppermute(to_west, "lon", WESTWARD)
    given = by_lat(totals(meta, swapped, edges))
    return last_substep(meta, state, winds, west2, east2, given, halo, west)


def solution(mesh):
    return jax.shard_map(
        shards,
        mesh=mesh,
        in_specs=(P("lon", None, "lat"), P("lon", None, "lat"), P("lat", "lon", None), P(), P()),
        out_specs=P("lon", None, "lat"),
        check_vma=False,
    )
```

```python
import jax
import jax.numpy as jnp
from jax import lax
from jax.experimental import pallas as pl
from jax.experimental.pallas import tpu as pltpu
from jax.sharding import PartitionSpec as P

VAR = 5
LEV = 32
COLS = VAR * LEV
XS = 45
ROWS = 48
LANES = 128
BANDS = 8
NLON = 1440
LON_DEV = 32
TARGETS = 16
BLOCKS = 16
PICKS = 56
WIRE = 6 * ROWS + 24
PACK = 120
HALO = 72
CHUNK = 9

F32 = jnp.float32
BF16 = jnp.bfloat16
VM = pl.BlockSpec(memory_space=pltpu.VMEM)
SM = pl.BlockSpec(memory_space=pltpu.SMEM)


def shape(dims, kind):
    return jax.ShapeDtypeStruct(dims, kind)


def params(mib):
    return pltpu.CompilerParams(vmem_limit_bytes=mib * 2**20)


def iotas(dims):
    return (
        lax.broadcasted_iota(jnp.int32, dims, 0),
        lax.broadcasted_iota(jnp.int32, dims, 1),
    )


def lanes_below(value, limit):
    lane = lax.broadcasted_iota(jnp.int32, value.shape, 1)
    return jnp.where(lane < limit, value, jnp.zeros_like(value))


def dot_nt(a, b):
    return lax.dot_general(a, b, (((1,), (1,)), ((), ())), preferred_element_type=F32)


def dot_tn(a, b):
    return lax.dot_general(a, b, (((0,), (0,)), ((), ())), preferred_element_type=F32)


def operator_kernel(meta_ref, ops_ref, own_ref, send_ref):
    core = meta_ref[1]
    for t in range(TARGETS):
        tiles = []
        for parity in range(2):
            start = XS * (2 * t + parity) - 1
            total = None
            first = max(start, 0) // LANES * LANES
            spans = [(first, min(first + 2 * LANES, NLON))]
            if start < 0:
                spans.append(((NLON - 1) // LANES * LANES, NLON))
            if start + XS + 2 > NLON:
                spans.append((0, LANES))
            for low, high in spans:
                row, lane = iotas((ROWS, high - low))
                wanted = start + row
                wanted = jnp.where(wanted < 0, wanted + NLON, wanted)
                wanted = jnp.where(wanted >= NLON, wanted - NLON, wanted)
                hit = (lane + low == wanted) & (row < XS + 2)
                pick = jnp.where(hit, 1.0, 0.0).astype(BF16)
                window = ops_ref[:, :, low:high].reshape(2 * ROWS, high - low)
                part = dot_nt(pick, window)
                total = part if total is None else total + part
            tiles.append(total)
        rows = slice(ROWS * t, ROWS * (t + 1))
        mine = core == 0
        own_ref[rows, :] = jnp.where(mine, tiles[0], tiles[1]).astype(BF16)
        send_ref[rows, :] = jnp.where(mine, tiles[1], tiles[0]).astype(BF16)


def prepare_operators(meta, ops):
    out = shape((TARGETS * ROWS, 2 * ROWS), BF16)
    return pl.pallas_call(
        operator_kernel,
        out_shape=(out, out),
        in_specs=[SM, VM],
        out_specs=(VM, VM),
        compiler_params=params(16),
        name="operators",
    )(meta, ops)


def slot(block):
    return (block % 2) * BANDS + block // 2


def global_row(meta_ref, block):
    return meta_ref[2 + block] * LANES + meta_ref[2 + BLOCKS + block]


def clear_rims(ref, count):
    blank = jnp.zeros((count, LANES), ref.dtype)
    for r in (0, XS + 1, XS + 2):
        ref[pl.ds(r, count, stride=ROWS), :] = blank


def pick_weights(meta_ref):
    me = meta_ref[0]
    sub, lane = iotas((PICKS, LANES))
    target = jnp.full(sub.shape, -1, jnp.int32)
    for block in range(BLOCKS):
        at = global_row(meta_ref, block) - me * LANES
        for near in range(3):
            k = near * BLOCKS + slot(block)
            target = jnp.where(sub == k, at + (near - 1), target)
    target = jnp.where(sub == 3 * BLOCKS, 0, target)
    target = jnp.where(sub == 3 * BLOCKS + 1, LANES - 1, target)
    return jnp.where(lane == target, 1.0, 0.0).astype(BF16)


def keep(value, *starts):
    lane = lax.broadcasted_iota(jnp.int32, value.shape, 1)
    hit = (lane >= starts[0]) & (lane < starts[0] + LEV)
    for start in starts[1:]:
        hit = hit | ((lane >= start) & (lane < start + LEV))
    return jnp.where(hit, value, jnp.zeros_like(value))


def pull(value, start):
    moved = pltpu.roll(value, LANES - start, axis=1) if start else value
    return lanes_below(moved, LEV)


def wide(value):
    value = value + pltpu.roll(value, LEV, axis=1)
    return value + pltpu.roll(value, 2 * LEV, axis=1)


def folded(value, width):
    half = ROWS // 2
    return value[:half] + pltpu.roll(value[half:], width, axis=1)


def unfolded(value, start, width, limit):
    low = pltpu.roll(value, LANES - start, axis=1) if start else value
    high = pltpu.roll(value, LANES - start - width, axis=1)
    return jnp.concatenate([lanes_below(low, limit), lanes_below(high, limit)], axis=0)


def pack_messages(meta_ref, main_ref, rest_ref, send_ref, edges_ref):
    me = meta_ref[0]

    def picked(ref, k):
        return ref[k * ROWS : (k + 1) * ROWS, :]

    for d in range(BANDS):
        tails, winds, souths = [], [], []
        for e in range(2):
            k = e * BANDS + d
            here = picked(rest_ref, BLOCKS + k)
            behind = picked(rest_ref, k)
            ahead = picked(rest_ref, 2 * BLOCKS + k)
            mine = meta_ref[2 + 2 * d + e] == me
            along = pull(here, 2 * LEV)
            before = pull(behind, 2 * LEV)
            north = jnp.where(mine, jnp.maximum(along, 0.0), lanes_below(jnp.ones_like(along), LEV))
            south = jnp.where(mine, jnp.minimum(before, 0.0), -lanes_below(jnp.ones_like(along), LEV))
            main = wide(north) * picked(main_ref, 2 * BLOCKS + k) - wide(south) * picked(main_ref, k)
            rest = north * ahead - south * behind
            send_ref[d, e * ROWS : (e + 1) * ROWS, :] = picked(main_ref, BLOCKS + k).astype(BF16)
            send_ref[d, (2 + e) * ROWS : (3 + e) * ROWS, :] = main.astype(BF16)
            tails.append((keep(here, 0), rest))
            winds.append(keep(here, LEV, 2 * LEV))
            souths.append(before)
        tail = tails[0][0] + pltpu.roll(tails[1][0], LEV, axis=1)
        tail = tail + pltpu.roll(tails[0][1], 2 * LEV, axis=1) + pltpu.roll(tails[1][1], 3 * LEV, axis=1)
        send_ref[d, 4 * ROWS : 5 * ROWS, :] = tail.astype(BF16)
        wind = pltpu.roll(winds[0], 3 * LEV, axis=1) + pltpu.roll(winds[1], LEV, axis=1)
        send_ref[d, 5 * ROWS : 6 * ROWS, :] = wind.astype(BF16)
        south = souths[0] + pltpu.roll(souths[1], LEV, axis=1)
        send_ref[d, 6 * ROWS :, :] = folded(south, 2 * LEV).astype(BF16)
    for at in range(2):
        k = 3 * BLOCKS + at
        edges_ref[at, :ROWS, :] = picked(main_ref, k).astype(BF16)
        rest = picked(rest_ref, k)
        rest = folded(keep(rest, 0), LEV) + folded(keep(rest, 2 * LEV), LEV)
        edges_ref[at, ROWS:, :] = rest.astype(BF16)


def clear(*refs):
    for ref in refs:
        ref[...] = jnp.zeros(ref.shape, ref.dtype)


def pick_kernel(meta_ref, cells_ref, winds_ref, send_ref, edges_ref, east_ref, west_ref, main_ref, rest_ref):
    step = pl.program_id(0)

    @pl.when(step == 0)
    def _():
        clear_rims(main_ref, PICKS)
        clear_rims(rest_ref, PICKS)
        west_ref[...] = cells_ref[0]

    weights = pick_weights(meta_ref)
    blank = jnp.zeros((LEV, LANES), BF16)
    for y in range(CHUNK):
        main = dot_nt(weights, cells_ref[y, :LANES, :])
        tail = jnp.concatenate([cells_ref[y, LANES:, :], winds_ref[y], blank], axis=0)
        rest = dot_nt(weights, tail)
        at = pl.ds(step * CHUNK + y + 1, PICKS, stride=ROWS)
        main_ref[at, :] = main
        rest_ref[at, :] = rest

    @pl.when(step == XS // CHUNK - 1)
    def _():
        pack_messages(meta_ref, main_ref, rest_ref, send_ref, edges_ref)
        east_ref[:COLS, :] = cells_ref[CHUNK - 1]
        east_ref[COLS:, :] = winds_ref[CHUNK - 1, :LEV, :]


STAGE = pltpu.VMEM((24 * ROWS, LANES), F32)
PICKED = pltpu.VMEM((PICKS * ROWS, LANES), F32)


def pick_rows(meta, cells, winds):
    return pl.pallas_call(
        pick_kernel,
        grid=(XS // CHUNK,),
        out_shape=(
            shape((BANDS, WIRE, LANES), BF16),
            shape((2, HALO, LANES), BF16),
            shape((COLS + LEV, LANES), BF16),
            shape((COLS, LANES), BF16),
        ),
        in_specs=[
            SM,
            pl.BlockSpec((CHUNK, COLS, LANES), lambda i: (i, 0, 0)),
            pl.BlockSpec((CHUNK, 2 * LEV, LANES), lambda i: (i, 0, 0)),
        ],
        out_specs=(VM,) * 4,
        scratch_shapes=[PICKED, PICKED],
        compiler_params=params(58),
        name="pick",
    )(meta, cells, winds)


def added(recv_ref, span):
    total = recv_ref[0, span, :].astype(F32)
    for s in range(1, BANDS):
        total = total + recv_ref[s, span, :].astype(F32)
    return total


def unpack_kernel(recv_ref, rows_ref):
    rows_ref[: 2 * ROWS, :] = added(recv_ref, slice(0, 2 * ROWS)).astype(BF16)
    tail = added(recv_ref, slice(4 * ROWS, 5 * ROWS))
    rows_ref[2 * ROWS :, :] = lanes_below(tail, 2 * LEV).astype(BF16)


def unpack_rows(recv):
    return pl.pallas_call(
        unpack_kernel,
        out_shape=shape((3 * ROWS, LANES), BF16),
        in_specs=[VM],
        out_specs=VM,
        compiler_params=params(8),
        name="unpack",
    )(recv)


def context_kernel(meta_ref, recv_ref, rows_ref, context_ref, to_east_ref, to_west_ref):
    me = meta_ref[0]
    winds = added(recv_ref, slice(5 * ROWS, 6 * ROWS))
    souths = unfolded(added(recv_ref, slice(6 * ROWS, WIRE)), 0, 2 * LEV, 2 * LEV)
    tails = None
    for e in range(2):
        band = meta_ref[2 + 2 * me + e]
        row = meta_ref[2 + BLOCKS + 2 * me + e]
        north = jnp.maximum(pull(winds, (2 * e + 1) * LEV), 0.0)
        south = jnp.minimum(pull(souths, e * LEV), 0.0)
        main = recv_ref[band, (2 + e) * ROWS : (3 + e) * ROWS, :].astype(F32)
        rest = pull(recv_ref[band, 4 * ROWS : 5 * ROWS, :].astype(F32), (2 + e) * LEV)
        for source, there, coef in (
            (jnp.minimum(band + 1, BANDS - 1), (row == LANES - 1) & (band < BANDS - 1), north),
            (jnp.maximum(band - 1, 0), (row == 0) & (band > 0), -south),
        ):
            share = jnp.where(there, coef, 0.0)
            main = main + wide(share) * recv_ref[source, (2 + e) * ROWS : (3 + e) * ROWS, :].astype(F32)
            rest = rest + share * pull(recv_ref[source, 4 * ROWS : 5 * ROWS, :].astype(F32), (2 + e) * LEV)
        context_ref[e] = main
        tails = rest if e == 0 else tails + pltpu.roll(rest, LEV, axis=1)
    context_ref[2] = tails
    context_ref[3] = winds
    context_ref[4] = souths
    clear(to_east_ref, to_west_ref)
    rims = [rows_ref[p * ROWS : (p + 1) * ROWS, :].astype(F32) for p in range(3)] + [winds]
    for at, tile in enumerate(rims):
        to_east_ref[at : at + 1, :] = tile[XS : XS + 1]
        to_west_ref[at : at + 1, :] = tile[1:2]


def unpack_context(meta, recv, rows):
    edge = shape((8, LANES), F32)
    return pl.pallas_call(
        context_kernel,
        out_shape=(shape((5, ROWS, LANES), F32), edge, edge),
        in_specs=[SM, VM, VM],
        out_specs=(VM,) * 3,
        compiler_params=params(8),
        name="context",
    )(meta, recv, rows)


def spread_blocks(rows_ref):
    first = rows_ref[:ROWS, :]
    second = rows_ref[ROWS : 2 * ROWS, :]
    rest = rows_ref[2 * ROWS :, :].astype(F32)
    lower = lanes_below(rest, LEV)
    upper = rest - lower
    blank = jnp.zeros_like(first)
    return jnp.concatenate(
        [
            jnp.concatenate([first, blank, lower.astype(BF16)], axis=1),
            jnp.concatenate([blank, second, upper.astype(BF16)], axis=1),
        ],
        axis=0,
    )


def product_kernel(rows_ref, other_ref, own_ops_ref, other_ops_ref, out_ref):
    mine = spread_blocks(rows_ref)
    theirs = spread_blocks(other_ref)
    for q in range(4):
        span = slice(4 * ROWS * q, 4 * ROWS * (q + 1))
        made = jnp.dot(own_ops_ref[span, :], mine, preferred_element_type=F32)
        made = made + jnp.dot(other_ops_ref[span, :], theirs, preferred_element_type=F32)
        for s in range(4):
            part = made[ROWS * s : ROWS * (s + 1)]
            rest = part[:, 2 * LANES :]
            t = 4 * q + s
            out_ref[t, :ROWS, :] = part[:, :LANES].astype(BF16)
            out_ref[t, ROWS : 2 * ROWS, :] = part[:, LANES : 2 * LANES].astype(BF16)
            packed = rest[: ROWS // 2] + pltpu.roll(rest[ROWS // 2 :], 2 * LEV, axis=1)
            out_ref[t, 2 * ROWS :, :] = packed.astype(BF16)


def products(rows, other, own_ops, other_ops):
    return pl.pallas_call(
        product_kernel,
        out_shape=shape((TARGETS, PACK, LANES), BF16),
        in_specs=[VM] * 4,
        out_specs=VM,
        compiler_params=params(12),
        name="product",
    )(rows, other, own_ops, other_ops)


def total_kernel(meta_ref, recv_ref, edges_ref, out_ref):
    total = recv_ref[0].astype(F32)
    for s in range(1, TARGETS):
        total = total + recv_ref[s].astype(F32)
    total = total.astype(BF16)
    me = meta_ref[0]
    for d in range(BANDS):
        out_ref[d, :PACK, :] = total
        edge = jnp.where(d == me + 1, edges_ref[1], jnp.zeros((HALO, LANES), BF16))
        out_ref[d, PACK:, :] = jnp.where(d == me - 1, edges_ref[0], edge)


def totals(meta, recv, edges):
    return pl.pallas_call(
        total_kernel,
        out_shape=shape((BANDS, PACK + HALO, LANES), BF16),
        in_specs=[SM, VM, VM],
        out_specs=VM,
        compiler_params=params(8),
        name="total",
    )(meta, recv, edges)


def halo_rows(meta_ref, recv_ref):
    me = meta_ref[0]
    halos = []
    for near, there in ((me - 1, me > 0), (me + 1, me < BANDS - 1)):
        source = jnp.clip(near, 0, BANDS - 1)
        main = recv_ref[source, PACK : PACK + ROWS, :].astype(F32)
        rest = recv_ref[source, PACK + ROWS :, :].astype(F32)
        found = (main, unfolded(rest, 0, LEV, LEV), unfolded(rest, 2 * LEV, LEV, LEV))
        halos.append([jnp.where(there, value, 0.0) for value in found])
    return halos[0][:2], halos[1][:2], halos[0][2]


def stage_blocks(recv_ref, main_ref, rest_ref):
    half = ROWS // 2
    for source in range(BANDS):
        packed = recv_ref[source, 2 * ROWS : PACK, :].astype(F32)
        for b in range(2):
            at = (b * BANDS + source) * ROWS
            main_ref[at : at + ROWS, :] = recv_ref[source, b * ROWS : (b + 1) * ROWS, :].astype(F32)
            rest_ref[at : at + half, :] = pull(packed, b * LEV)
            rest_ref[at + half : at + ROWS, :] = pull(packed, (2 + b) * LEV)


def block_sum(meta_ref, row, main_ref, rest_ref):
    main = jnp.zeros((ROWS, LANES), F32)
    rest = jnp.zeros((ROWS, LANES), F32)
    for block in range(BLOCKS):
        share = jnp.where(global_row(meta_ref, block) == row, 1.0, 0.0)
        k = slot(block) * ROWS
        main = main + share * main_ref[k : k + ROWS, :]
        rest = rest + share * rest_ref[k : k + ROWS, :]
    return main, rest


def stage_corrections(meta_ref, recv_ref, wind_recv_ref, main_ref, rest_ref):
    stage_blocks(recv_ref, main_ref, rest_ref)
    main_ref[18 * ROWS :, :] = jnp.zeros((6 * ROWS, LANES), F32)
    rest_ref[18 * ROWS :, :] = jnp.zeros((6 * ROWS, LANES), F32)
    me = meta_ref[0]
    halos = halo_rows(meta_ref, recv_ref)
    for at, row in enumerate((me * LANES - 1, (me + 1) * LANES)):
        main, rest = block_sum(meta_ref, row, main_ref, rest_ref)
        k = (16 + at) * ROWS
        main = (halos[at][0] + main).astype(BF16).astype(F32)
        rest = (halos[at][1] + rest).astype(BF16).astype(F32)
        main_ref[k : k + ROWS, :] = main
        rest_ref[k : k + ROWS, :] = rest
    wind = halo_rows(meta_ref, wind_recv_ref)[2]
    rest_ref[18 * ROWS : 19 * ROWS, :] = pltpu.roll(wind, LEV, axis=1)


def rows_kernel(meta_ref, before_ref, context_ref, west_ref, east_ref, recv_ref, out_ref, main_ref, rest_ref):
    stage_blocks(recv_ref, main_ref, rest_ref)
    me = meta_ref[0]
    sub = lax.broadcasted_iota(jnp.int32, (ROWS, LANES), 0)
    inner = (sub >= 1) & (sub <= XS)

    def rimmed(value, at):
        value = jnp.where(sub == 0, west_ref[at : at + 1, :], value)
        return jnp.where(sub == XS + 1, east_ref[at : at + 1, :], value)

    def known(p):
        return rimmed(before_ref[p * ROWS : (p + 1) * ROWS, :].astype(F32), p)

    last = None
    tail = known(2)
    winds = rimmed(context_ref[3], 3)
    for e in range(2):
        row = global_row(meta_ref, 2 * me + e)
        across = pull(winds, 2 * e * LEV)
        east = jnp.maximum(across, 0.0)
        west = jnp.minimum(pltpu.roll(across, 1, axis=0), 0.0)
        north = jnp.where(row == BANDS * LANES - 1, 0.0, jnp.maximum(pull(winds, (2 * e + 1) * LEV), 0.0))
        south = jnp.minimum(pull(context_ref[4], e * LEV), 0.0)
        coefs = (east, west, north, south)
        added = [block_sum(meta_ref, row + near, main_ref, rest_ref) for near in (-1, 0, 1)]

        def moved(coefs, here, aside, behind, ahead):
            east, west, north, south = coefs
            here = here.astype(BF16).astype(F32)
            centre = 1.0 - east + west - north + south
            made = (
                centre * here
                + (east * pltpu.roll(here, ROWS - 1, axis=0) - west * pltpu.roll(here, 1, axis=0))
                + (aside + (north * ahead - south * behind))
            )
            return jnp.where(inner, made, 0.0)

        main = moved([wide(c) for c in coefs], known(e) + added[1][0], context_ref[e], added[0][0], added[2][0])
        out_ref[e * ROWS : (e + 1) * ROWS, :] = main.astype(BF16)
        rest = pull(tail, e * LEV) + added[1][1]
        rest = moved(coefs, rest, pull(context_ref[2], e * LEV), added[0][1], added[2][1])
        rest = lanes_below(rest, LEV)
        last = rest if e == 0 else last + pltpu.roll(rest, LEV, axis=1)
    out_ref[2 * ROWS :, :] = last.astype(BF16)


def next_rows(*args):
    return pl.pallas_call(
        rows_kernel,
        out_shape=shape((3 * ROWS, LANES), BF16),
        in_specs=[SM] + [VM] * 5,
        out_specs=VM,
        scratch_shapes=[STAGE, STAGE],
        compiler_params=params(16),
        name="rows",
    )(*args)


def place_weights(meta_ref):
    sub, lane = iotas((24, 2 * LANES))
    target = jnp.full(sub.shape, -1, jnp.int32)
    for block in range(BLOCKS):
        at = global_row(meta_ref, block) - meta_ref[0] * LANES
        target = jnp.where(sub == slot(block), jnp.where((at >= 0) & (at < LANES), at, -1), target)
    target = jnp.where((sub == 16) | (sub == 18), LANES, target)
    target = jnp.where(sub == 17, 2 * LANES - 1, target)
    return jnp.where(lane == target, 1.0, 0.0).astype(BF16)


def smooth_all(weights, cells_ref, west_ref, east_ref, main_ref, rest_ref, smooth_ref, edge_ref, wind_ref):
    def placed(r):
        main = main_ref[pl.ds(r, 24, stride=ROWS), :].astype(BF16)
        rest = rest_ref[pl.ds(r, 24, stride=ROWS), :].astype(BF16)
        return dot_tn(main, weights), dot_tn(rest, weights)

    def store(r, base):
        main, rest = placed(r)
        base = base.astype(F32)
        smooth_ref[r, :LANES, :] = (base[:LANES] + main[:, :LANES]).astype(BF16).astype(F32)
        smooth_ref[r, LANES:, :] = (base[LANES:] + rest[:LEV, :LANES]).astype(BF16).astype(F32)
        return main, rest

    store(0, west_ref[:COLS, :])
    store(XS + 1, east_ref[...])

    def body(x, carry):
        main, rest = store(x + 1, cells_ref[x])
        edge_ref[x, :LANES, :] = main[:, LANES:]
        edge_ref[x, LANES:, :] = rest[:LEV, LANES:]
        wind_ref[x] = rest[LEV : 2 * LEV, LANES:]
        return carry

    lax.fori_loop(0, XS, body, 0, unroll=3)


def stencil(x, top, winds_ref, west_ref, smooth_ref, edge_ref, wind_ref):
    lane = lax.broadcasted_iota(jnp.int32, (LEV, LANES), 1)
    courant = winds_ref[x].astype(F32)
    before = winds_ref[jnp.maximum(x - 1, 0), :LEV, :].astype(F32)
    before = jnp.where(x == 0, west_ref[COLS:, :].astype(F32), before)
    across = courant[:LEV]
    along = jnp.where(top & (lane == LANES - 1), 0.0, courant[LEV:])
    south_along = jnp.where(lane == 0, wind_ref[x], pltpu.roll(along, 1, axis=1))
    east = jnp.maximum(across, 0.0)
    west = jnp.minimum(before, 0.0)
    north = jnp.maximum(along, 0.0)
    south = jnp.minimum(south_along, 0.0)
    centre = 1.0 - east + west - north + south
    made = []
    for v in range(VAR):
        span = slice(v * LEV, (v + 1) * LEV)
        here = smooth_ref[x + 1, span, :]
        edge = edge_ref[x, span, :]
        above = jnp.where(lane == LANES - 1, edge, pltpu.roll(here, LANES - 1, axis=1))
        below = jnp.where(lane == 0, edge, pltpu.roll(here, 1, axis=1))
        made.append(
            centre * here
            + (east * smooth_ref[x + 2, span, :] - west * smooth_ref[x, span, :])
            + (north * above - south * below)
        )
    return made


SCRATCH = [
    STAGE,
    STAGE,
    pltpu.VMEM((XS + 2, COLS, LANES), F32),
    pltpu.VMEM((XS, COLS, LANES), F32),
    pltpu.VMEM((XS, LEV, LANES), F32),
]


def first_kernel(
    meta_ref, cells_ref, winds_ref, west_ref, east_ref, recv_ref,
    out_ref, edges_ref, to_east_ref, to_west_ref, main_ref, rest_ref, smooth_ref, edge_ref, wind_ref,
):
    stage_corrections(meta_ref, recv_ref, recv_ref, main_ref, rest_ref)
    smooth_all(
        place_weights(meta_ref), cells_ref, west_ref, east_ref, main_ref, rest_ref, smooth_ref, edge_ref, wind_ref
    )
    clear_rims(main_ref, 2)
    clear_rims(rest_ref, 2)
    sub, lane = iotas((8, LANES))
    ends = jnp.where((lane == 0) & (sub == 0) | (lane == LANES - 1) & (sub == 1), 1.0, 0.0).astype(BF16)
    top = meta_ref[0] == BANDS - 1
    blank = jnp.zeros((3 * LEV, LANES), BF16)

    def body(x, carry):
        made = [m.astype(BF16) for m in stencil(x, top, winds_ref, west_ref, smooth_ref, edge_ref, wind_ref)]
        for v in range(VAR):
            out_ref[x, v * LEV : (v + 1) * LEV, :] = made[v]
        at = pl.ds(x + 1, 2, stride=ROWS)
        main_ref[at, :] = dot_nt(ends, jnp.concatenate(made[:4], axis=0))[:2]
        rest_ref[at, :] = dot_nt(ends, jnp.concatenate([made[4], blank], axis=0))[:2]
        return carry

    lax.fori_loop(0, XS, body, 0, unroll=3)
    for at in range(2):
        k = at * ROWS
        edges_ref[at, :ROWS, :] = main_ref[k : k + ROWS, :].astype(BF16)
        rest = rest_ref[k : k + ROWS, :]
        packed = rest[: ROWS // 2] + pltpu.roll(rest[ROWS // 2 :], LEV, axis=1)
        edges_ref[at, ROWS:, :] = packed.astype(BF16)
    to_east_ref[...] = out_ref[XS - 1]
    to_west_ref[...] = out_ref[0]


def first_substep(*args):
    return pl.pallas_call(
        first_kernel,
        out_shape=(
            shape((XS, COLS, LANES), BF16),
            shape((2, HALO, LANES), BF16),
            shape((COLS, LANES), BF16),
            shape((COLS, LANES), BF16),
        ),
        in_specs=[SM] + [VM] * 5,
        out_specs=(VM,) * 4,
        scratch_shapes=SCRATCH,
        compiler_params=params(16),
        name="first",
    )(*args)


def last_kernel(
    meta_ref, cells_ref, winds_ref, west_ref, east_ref, recv_ref, wind_recv_ref, wind_west_ref,
    out_ref, main_ref, rest_ref, smooth_ref, edge_ref, wind_ref,
):
    me = meta_ref[0]
    step = pl.program_id(0)

    @pl.when(step == 0)
    def _():
        stage_corrections(meta_ref, recv_ref, wind_recv_ref, main_ref, rest_ref)
        smooth_all(
            place_weights(meta_ref), cells_ref, west_ref, east_ref, main_ref, rest_ref, smooth_ref, edge_ref, wind_ref
        )

    top = me == BANDS - 1

    def body(y, carry):
        x = step * CHUNK + y
        made = stencil(x, top, winds_ref, wind_west_ref, smooth_ref, edge_ref, wind_ref)
        for v in range(VAR):
            out_ref[y, v * LEV : (v + 1) * LEV, :] = made[v]
        return carry

    lax.fori_loop(0, CHUNK, body, 0, unroll=3)


def last_substep(*args):
    return pl.pallas_call(
        last_kernel,
        grid=(XS // CHUNK,),
        out_shape=shape((XS, COLS, LANES), F32),
        in_specs=[SM] + [VM] * 7,
        out_specs=pl.BlockSpec((CHUNK, COLS, LANES), lambda i: (i, 0, 0)),
        scratch_shapes=SCRATCH,
        compiler_params=params(20),
        name="last",
    )(*args)


SWAP = [(i, i ^ 1) for i in range(LON_DEV)]
EASTWARD = [(i, (i + 1) % LON_DEV) for i in range(LON_DEV)]
WESTWARD = [(i, (i - 1) % LON_DEV) for i in range(LON_DEV)]
SAME_CORE = [[2 * t + core for t in range(TARGETS)] for core in range(2)]


def by_lat(messages):
    return lax.all_to_all(messages, "lat", 0, 0, tiled=True)


def filtered(rows, own_ops, other_ops):
    other = lax.ppermute(rows, "lon", SWAP)
    partial = products(rows, other, own_ops, other_ops)
    return lax.all_to_all(partial, "lon", 0, 0, tiled=True, axis_index_groups=SAME_CORE)


def shards(cotangent, winds, filter_ops, block_band, block_row):
    me = lax.axis_index("lat").astype(jnp.int32).reshape(1)
    core = (lax.axis_index("lon") & 1).astype(jnp.int32).reshape(1)
    meta = jnp.concatenate([me, core, block_band, block_row])
    own_ops, send_ops = prepare_operators(meta, jnp.pad(filter_ops, ((0, 0), (1, 2), (0, 0))))
    other_ops = lax.ppermute(send_ops, "lon", SWAP)
    send, edges, to_east, to_west = pick_rows(meta, cotangent, winds)
    west = lax.ppermute(to_east, "lon", EASTWARD)
    east = lax.ppermute(to_west, "lon", WESTWARD)
    recv, west, east = lax.optimization_barrier((by_lat(send), west, east))
    rows = unpack_rows(recv)
    swapped = filtered(rows, own_ops, other_ops)
    context, row_east, row_west = unpack_context(meta, recv, rows)
    row_from_west = lax.ppermute(row_east, "lon", EASTWARD)
    row_from_east = lax.ppermute(row_west, "lon", WESTWARD)
    given = by_lat(totals(meta, swapped, edges))
    rows = next_rows(meta, rows, context, row_from_west, row_from_east, given)
    swapped = filtered(rows, own_ops, other_ops)
    state, edges, to_east, to_west = first_substep(meta, cotangent, winds, west, east, given)
    west2 = lax.ppermute(to_east, "lon", EASTWARD)
    east2 = lax.ppermute(to_west, "lon", WESTWARD)
    given2 = by_lat(totals(meta, swapped, edges))
    return last_substep(meta, state, winds, west2, east2, given2, given, west)


def solution(mesh):
    return jax.shard_map(
        shards,
        mesh=mesh,
        in_specs=(P("lon", None, "lat"), P("lon", None, "lat"), P("lat", "lon", None), P(), P()),
        out_specs=P("lon", None, "lat"),
        check_vma=False,
    )
```

```python
import jax
import jax.numpy as jnp
from jax import lax
from jax.experimental import pallas as pl
from jax.experimental.pallas import tpu as pltpu
from jax.sharding import PartitionSpec as P

VAR = 5
LEV = 32
COLS = VAR * LEV
XS = 45
ROWS = 48
LANES = 128
BANDS = 8
NLON = 1440
LON_DEV = 32
TARGETS = 16
BLOCKS = 16
PICKS = 56
WIRE = 6 * ROWS + 24
PACK = 120
HALO = 72
CHUNK = 9

F32 = jnp.float32
BF16 = jnp.bfloat16
VM = pl.BlockSpec(memory_space=pltpu.VMEM)
SM = pl.BlockSpec(memory_space=pltpu.SMEM)
HB = pl.BlockSpec(memory_space=pl.ANY)
DMA = pltpu.SemaphoreType.DMA
SPANS = [(start, min(8, XS - start)) for start in range(0, XS, 8)]


def shape(dims, kind):
    return jax.ShapeDtypeStruct(dims, kind)


def params(mib):
    return pltpu.CompilerParams(vmem_limit_bytes=mib * 2**20)


def iotas(dims):
    return (
        lax.broadcasted_iota(jnp.int32, dims, 0),
        lax.broadcasted_iota(jnp.int32, dims, 1),
    )


def lanes_below(value, limit):
    lane = lax.broadcasted_iota(jnp.int32, value.shape, 1)
    return jnp.where(lane < limit, value, jnp.zeros_like(value))


def dot_nt(a, b):
    return lax.dot_general(a, b, (((1,), (1,)), ((), ())), preferred_element_type=F32)


def dot_tn(a, b):
    return lax.dot_general(a, b, (((0,), (0,)), ((), ())), preferred_element_type=F32)


def operator_kernel(meta_ref, ops_ref, own_ref, send_ref):
    core = meta_ref[1]
    for t in range(TARGETS):
        tiles = []
        for parity in range(2):
            start = XS * (2 * t + parity) - 1
            total = None
            first = max(start, 0) // LANES * LANES
            spans = [(first, min(first + 2 * LANES, NLON))]
            if start < 0:
                spans.append(((NLON - 1) // LANES * LANES, NLON))
            if start + XS + 2 > NLON:
                spans.append((0, LANES))
            for low, high in spans:
                row, lane = iotas((ROWS, high - low))
                wanted = start + row
                wanted = jnp.where(wanted < 0, wanted + NLON, wanted)
                wanted = jnp.where(wanted >= NLON, wanted - NLON, wanted)
                hit = (lane + low == wanted) & (row < XS + 2)
                pick = jnp.where(hit, 1.0, 0.0).astype(BF16)
                window = ops_ref[:, :, low:high].reshape(2 * ROWS, high - low)
                part = dot_nt(pick, window)
                total = part if total is None else total + part
            tiles.append(total)
        rows = slice(ROWS * t, ROWS * (t + 1))
        mine = core == 0
        own_ref[rows, :] = jnp.where(mine, tiles[0], tiles[1]).astype(BF16)
        send_ref[rows, :] = jnp.where(mine, tiles[1], tiles[0]).astype(BF16)


def prepare_operators(meta, ops):
    out = shape((TARGETS * ROWS, 2 * ROWS), BF16)
    return pl.pallas_call(
        operator_kernel,
        out_shape=(out, out),
        in_specs=[SM, VM],
        out_specs=(VM, VM),
        compiler_params=params(6),
        name="operators",
    )(meta, ops)


def slot(block):
    return (block % 2) * BANDS + block // 2


def global_row(meta_ref, block):
    return meta_ref[2 + block] * LANES + meta_ref[2 + BLOCKS + block]


def clear_rims(ref, count):
    blank = jnp.zeros((count, LANES), ref.dtype)
    for r in (0, XS + 1, XS + 2):
        ref[pl.ds(r, count, stride=ROWS), :] = blank


def pick_weights(meta_ref):
    me = meta_ref[0]
    lane = lax.broadcasted_iota(jnp.int32, (8, LANES), 1)
    pick = lane & 63
    target = jnp.full(lane.shape, -1, jnp.int32)
    for block in range(BLOCKS):
        at = global_row(meta_ref, block) - me * LANES
        for near in range(3):
            target = jnp.where(pick == near * BLOCKS + slot(block), at + (near - 1), target)
    target = jnp.where(pick == 3 * BLOCKS, 0, target)
    target = jnp.where(pick == 3 * BLOCKS + 1, LANES - 1, target)
    sub, lane = iotas((LANES, LANES))
    hit = sub == jnp.broadcast_to(target[:1], (LANES, LANES))
    halves = [jnp.where(hit & ((lane < 64) == side), 1.0, 0.0) for side in (True, False)]
    return jnp.concatenate(halves, axis=0).astype(BF16)


def keep(value, *starts):
    lane = lax.broadcasted_iota(jnp.int32, value.shape, 1)
    hit = (lane >= starts[0]) & (lane < starts[0] + LEV)
    for start in starts[1:]:
        hit = hit | ((lane >= start) & (lane < start + LEV))
    return jnp.where(hit, value, jnp.zeros_like(value))


def pull(value, start):
    moved = pltpu.roll(value, LANES - start, axis=1) if start else value
    return lanes_below(moved, LEV)


def wide(value):
    value = value + pltpu.roll(value, LEV, axis=1)
    return value + pltpu.roll(value, 2 * LEV, axis=1)


def folded(value, width):
    half = ROWS // 2
    return value[:half] + pltpu.roll(value[half:], width, axis=1)


def unfolded(value, start, width, limit):
    low = pltpu.roll(value, LANES - start, axis=1) if start else value
    high = pltpu.roll(value, LANES - start - width, axis=1)
    return jnp.concatenate([lanes_below(low, limit), lanes_below(high, limit)], axis=0)


def pack_messages(meta_ref, main_ref, rest_ref, send_ref, edges_ref, leaving):
    me = meta_ref[0]

    def picked(ref, k):
        return ref[k * ROWS : (k + 1) * ROWS, :]

    def add(d, start, count, value):
        span = slice(start, start + count)
        send_ref[d, span, :] = (send_ref[d, span, :].astype(F32) + value).astype(BF16)

    for block in range(BLOCKS):
        d, e = block // 2, block % 2
        k = slot(block)
        at = global_row(meta_ref, block) - me * LANES

        @pl.when((at >= -1) & (at <= LANES))
        def _():
            mine = (at >= 0) & (at < LANES)
            here = picked(rest_ref, BLOCKS + k)
            behind = picked(rest_ref, k)
            before = pull(behind, 2 * LEV)
            one = lanes_below(jnp.ones_like(here), LEV)
            north = jnp.where(mine, jnp.maximum(pull(here, 2 * LEV), 0.0), one)
            south = jnp.where(mine, jnp.minimum(before, 0.0), -one)
            main = wide(north) * picked(main_ref, 2 * BLOCKS + k) - wide(south) * picked(main_ref, k)
            rest = north * picked(rest_ref, 2 * BLOCKS + k) - south * behind
            send_ref[d, e * ROWS : (e + 1) * ROWS, :] = picked(main_ref, BLOCKS + k).astype(BF16)
            send_ref[d, (2 + e) * ROWS : (3 + e) * ROWS, :] = main.astype(BF16)
            tail = keep(here, 0) + pltpu.roll(rest, 2 * LEV, axis=1)
            add(d, 4 * ROWS, ROWS, pltpu.roll(tail, LEV, axis=1) if e else tail)
            add(d, 5 * ROWS, ROWS, pltpu.roll(keep(here, LEV, 2 * LEV), (1 if e else 3) * LEV, axis=1))
            add(d, 6 * ROWS, ROWS // 2, folded(pltpu.roll(before, LEV, axis=1) if e else before, 2 * LEV))

        if e:
            leaving[d].start()

    for at in range(2):
        k = 3 * BLOCKS + at
        edges_ref[at, :ROWS, :] = picked(main_ref, k).astype(BF16)
        rest = picked(rest_ref, k)
        rest = folded(keep(rest, 0), LEV) + folded(keep(rest, 2 * LEV), LEV)
        edges_ref[at, ROWS:, :] = rest.astype(BF16)


def clear(*refs):
    for ref in refs:
        ref[...] = jnp.zeros(ref.shape, ref.dtype)


def copies(source_ref, target_ref, sem_ref):
    return [
        pltpu.make_async_copy(source_ref.at[pl.ds(start, size)], target_ref.at[pl.ds(start, size)], sem_ref.at[n])
        for n, (start, size) in enumerate(SPANS)
    ]


def pick_kernel(
    meta_ref, cells_hbm, winds_hbm, send_hbm, edges_ref, east_ref, west_ref,
    main_ref, rest_ref, cells_ref, winds_ref, send_ref, cells_sem, winds_sem, send_sem,
):
    arriving = list(zip(copies(cells_hbm, cells_ref, cells_sem), copies(winds_hbm, winds_ref, winds_sem)))
    for pair in arriving:
        for copy in pair:
            copy.start()
    clear_rims(main_ref, PICKS)
    clear_rims(rest_ref, PICKS)
    weights = pick_weights(meta_ref)
    clear(send_ref)
    blank = jnp.zeros((LEV, 2 * LANES), BF16)
    for (start, size), pair in zip(SPANS, arriving):
        for copy in pair:
            copy.wait()
        for y in range(start, start + size, 2):
            both = (y, min(y + 1, XS - 1))
            main = jnp.concatenate([cells_ref[z, :LANES, :] for z in both], axis=1)
            rest = jnp.concatenate([cells_ref[z, LANES:, :] for z in both], axis=1)
            wind = jnp.concatenate([winds_ref[z] for z in both], axis=1)
            rest = jnp.concatenate([rest, wind, blank], axis=0)
            main = jnp.dot(main, weights, preferred_element_type=F32).astype(BF16).T.astype(F32)
            rest = jnp.dot(rest, weights, preferred_element_type=F32).astype(BF16).T.astype(F32)
            for side in range(min(2, XS - y)):
                at = pl.ds(y + side + 1, PICKS, stride=ROWS)
                main_ref[at, :] = main[64 * side : 64 * side + PICKS]
                rest_ref[at, :] = rest[64 * side : 64 * side + PICKS]
    east_ref[:COLS, :] = cells_ref[XS - 1]
    east_ref[COLS:, :] = winds_ref[XS - 1, :LEV, :]
    west_ref[...] = cells_ref[0]
    leaving = [pltpu.make_async_copy(send_ref.at[d], send_hbm.at[d], send_sem.at[d]) for d in range(BANDS)]
    pack_messages(meta_ref, main_ref, rest_ref, send_ref, edges_ref, leaving)
    for copy in leaving:
        copy.wait()


STAGE = pltpu.VMEM((24 * ROWS, LANES), F32)
PICKED = pltpu.VMEM((PICKS * ROWS, LANES), F32)


def pick_rows(meta, cells, winds):
    return pl.pallas_call(
        pick_kernel,
        out_shape=(
            shape((BANDS, WIRE, LANES), BF16),
            shape((2, HALO, LANES), BF16),
            shape((COLS + LEV, LANES), BF16),
            shape((COLS, LANES), BF16),
        ),
        in_specs=[SM, HB, HB],
        out_specs=(HB, VM, VM, VM),
        scratch_shapes=[
            PICKED,
            PICKED,
            pltpu.VMEM((XS, COLS, LANES), BF16),
            pltpu.VMEM((XS, 2 * LEV, LANES), BF16),
            pltpu.VMEM((BANDS, WIRE, LANES), BF16),
            DMA((len(SPANS),)),
            DMA((len(SPANS),)),
            DMA((BANDS,)),
        ],
        compiler_params=params(58),
        name="pick",
    )(meta, cells, winds)


def added(recv_ref, span):
    total = recv_ref[0, span, :].astype(F32)
    for s in range(1, BANDS):
        total = total + recv_ref[s, span, :].astype(F32)
    return total


def unpack_kernel(recv_ref, rows_ref):
    rows_ref[: 2 * ROWS, :] = added(recv_ref, slice(0, 2 * ROWS)).astype(BF16)
    tail = added(recv_ref, slice(4 * ROWS, 5 * ROWS))
    rows_ref[2 * ROWS :, :] = lanes_below(tail, 2 * LEV).astype(BF16)


def unpack_rows(recv):
    return pl.pallas_call(
        unpack_kernel,
        out_shape=shape((3 * ROWS, LANES), BF16),
        in_specs=[VM],
        out_specs=VM,
        compiler_params=params(8),
        name="unpack",
    )(recv)


def context_kernel(meta_ref, recv_ref, rows_ref, context_ref, to_east_ref, to_west_ref):
    me = meta_ref[0]
    winds = added(recv_ref, slice(5 * ROWS, 6 * ROWS))
    souths = unfolded(added(recv_ref, slice(6 * ROWS, WIRE)), 0, 2 * LEV, 2 * LEV)
    tails = None
    for e in range(2):
        band = meta_ref[2 + 2 * me + e]
        row = meta_ref[2 + BLOCKS + 2 * me + e]
        north = jnp.maximum(pull(winds, (2 * e + 1) * LEV), 0.0)
        south = jnp.minimum(pull(souths, e * LEV), 0.0)
        main = recv_ref[band, (2 + e) * ROWS : (3 + e) * ROWS, :].astype(F32)
        rest = pull(recv_ref[band, 4 * ROWS : 5 * ROWS, :].astype(F32), (2 + e) * LEV)
        for source, there, coef in (
            (jnp.minimum(band + 1, BANDS - 1), (row == LANES - 1) & (band < BANDS - 1), north),
            (jnp.maximum(band - 1, 0), (row == 0) & (band > 0), -south),
        ):
            share = jnp.where(there, coef, 0.0)
            main = main + wide(share) * recv_ref[source, (2 + e) * ROWS : (3 + e) * ROWS, :].astype(F32)
            rest = rest + share * pull(recv_ref[source, 4 * ROWS : 5 * ROWS, :].astype(F32), (2 + e) * LEV)
        context_ref[e] = main
        tails = rest if e == 0 else tails + pltpu.roll(rest, LEV, axis=1)
    context_ref[2] = tails
    context_ref[3] = winds
    context_ref[4] = souths
    clear(to_east_ref, to_west_ref)
    rims = [rows_ref[p * ROWS : (p + 1) * ROWS, :].astype(F32) for p in range(3)] + [winds]
    for at, tile in enumerate(rims):
        to_east_ref[at : at + 1, :] = tile[XS : XS + 1]
        to_west_ref[at : at + 1, :] = tile[1:2]


def unpack_context(meta, recv, rows):
    edge = shape((8, LANES), F32)
    return pl.pallas_call(
        context_kernel,
        out_shape=(shape((5, ROWS, LANES), F32), edge, edge),
        in_specs=[SM, VM, VM],
        out_specs=(VM,) * 3,
        compiler_params=params(8),
        name="context",
    )(meta, recv, rows)


def spread_blocks(rows_ref):
    first = rows_ref[:ROWS, :]
    second = rows_ref[ROWS : 2 * ROWS, :]
    rest = rows_ref[2 * ROWS :, :].astype(F32)
    lower = lanes_below(rest, LEV)
    upper = rest - lower
    blank = jnp.zeros_like(first)
    return jnp.concatenate(
        [
            jnp.concatenate([first, blank, lower.astype(BF16)], axis=1),
            jnp.concatenate([blank, second, upper.astype(BF16)], axis=1),
        ],
        axis=0,
    )


def product_kernel(rows_ref, other_ref, own_ops_ref, other_ops_ref, out_ref):
    mine = spread_blocks(rows_ref)
    theirs = spread_blocks(other_ref)
    for q in range(4):
        span = slice(4 * ROWS * q, 4 * ROWS * (q + 1))
        made = jnp.dot(own_ops_ref[span, :], mine, preferred_element_type=F32)
        made = made + jnp.dot(other_ops_ref[span, :], theirs, preferred_element_type=F32)
        for s in range(4):
            part = made[ROWS * s : ROWS * (s + 1)]
            rest = part[:, 2 * LANES :]
            t = 4 * q + s
            out_ref[t, :ROWS, :] = part[:, :LANES].astype(BF16)
            out_ref[t, ROWS : 2 * ROWS, :] = part[:, LANES : 2 * LANES].astype(BF16)
            packed = rest[: ROWS // 2] + pltpu.roll(rest[ROWS // 2 :], 2 * LEV, axis=1)
            out_ref[t, 2 * ROWS :, :] = packed.astype(BF16)


def products(rows, other, own_ops, other_ops):
    return pl.pallas_call(
        product_kernel,
        out_shape=shape((TARGETS, PACK, LANES), BF16),
        in_specs=[VM] * 4,
        out_specs=VM,
        compiler_params=params(6),
        name="product",
    )(rows, other, own_ops, other_ops)


def total_kernel(meta_ref, recv_ref, edges_ref, out_ref):
    total = recv_ref[0].astype(F32)
    for s in range(1, TARGETS):
        total = total + recv_ref[s].astype(F32)
    total = total.astype(BF16)
    me = meta_ref[0]
    for d in range(BANDS):
        out_ref[d, :PACK, :] = total
        edge = jnp.where(d == me + 1, edges_ref[1], jnp.zeros((HALO, LANES), BF16))
        out_ref[d, PACK:, :] = jnp.where(d == me - 1, edges_ref[0], edge)


def totals(meta, recv, edges):
    return pl.pallas_call(
        total_kernel,
        out_shape=shape((BANDS, PACK + HALO, LANES), BF16),
        in_specs=[SM, VM, VM],
        out_specs=VM,
        compiler_params=params(4),
        name="total",
    )(meta, recv, edges)


def halo_rows(meta_ref, recv_ref):
    me = meta_ref[0]
    halos = []
    for near, there in ((me - 1, me > 0), (me + 1, me < BANDS - 1)):
        source = jnp.clip(near, 0, BANDS - 1)
        main = recv_ref[source, PACK : PACK + ROWS, :].astype(F32)
        rest = recv_ref[source, PACK + ROWS :, :].astype(F32)
        found = (main, unfolded(rest, 0, LEV, LEV), unfolded(rest, 2 * LEV, LEV, LEV))
        halos.append([jnp.where(there, value, 0.0) for value in found])
    return halos[0][:2], halos[1][:2], halos[0][2]


def stage_blocks(recv_ref, main_ref, rest_ref):
    half = ROWS // 2
    for source in range(BANDS):
        packed = recv_ref[source, 2 * ROWS : PACK, :].astype(F32)
        for b in range(2):
            at = (b * BANDS + source) * ROWS
            main_ref[at : at + ROWS, :] = recv_ref[source, b * ROWS : (b + 1) * ROWS, :].astype(F32)
            rest_ref[at : at + half, :] = pull(packed, b * LEV)
            rest_ref[at + half : at + ROWS, :] = pull(packed, (2 + b) * LEV)


def block_sum(meta_ref, row, main_ref, rest_ref):
    main = jnp.zeros((ROWS, LANES), F32)
    rest = jnp.zeros((ROWS, LANES), F32)
    for block in range(BLOCKS):
        share = jnp.where(global_row(meta_ref, block) == row, 1.0, 0.0)
        k = slot(block) * ROWS
        main = main + share * main_ref[k : k + ROWS, :]
        rest = rest + share * rest_ref[k : k + ROWS, :]
    return main, rest


KEPT = 32
GROUP = LANES // KEPT
TALL = COLS + LEV


def stage_corrections(meta_ref, recv_ref, wind_recv_ref, main_ref, rest_ref, tall_ref):
    clear(main_ref, rest_ref)
    me = meta_ref[0]
    halos = halo_rows(meta_ref, recv_ref)
    sums = [list(halos[0]), list(halos[1])]
    for source in range(BANDS):
        packed = recv_ref[source, 2 * ROWS : PACK, :].astype(F32)
        for b in range(2):
            k = b * BANDS + source
            main = recv_ref[source, b * ROWS : (b + 1) * ROWS, :].astype(F32)
            rest = unfolded(packed, b * LEV, 2 * LEV, LEV)
            main_ref[pl.ds(k, ROWS, stride=KEPT), :] = main
            rest_ref[pl.ds(k, ROWS, stride=KEPT), :] = rest
            for at, row in enumerate((me * LANES - 1, (me + 1) * LANES)):
                share = jnp.where(global_row(meta_ref, 2 * source + b) == row, 1.0, 0.0)
                sums[at][0] = sums[at][0] + share * main
                sums[at][1] = sums[at][1] + share * rest
    for at in range(2):
        main_ref[pl.ds(16 + at, ROWS, stride=KEPT), :] = sums[at][0].astype(BF16).astype(F32)
        rest_ref[pl.ds(16 + at, ROWS, stride=KEPT), :] = sums[at][1].astype(BF16).astype(F32)
    wind = halo_rows(meta_ref, wind_recv_ref)[2]
    rest_ref[pl.ds(18, ROWS, stride=KEPT), :] = pltpu.roll(wind, LEV, axis=1)
    for t in range(ROWS // GROUP):
        span = slice(t * LANES, (t + 1) * LANES)
        tall_ref[t * TALL : t * TALL + LANES, :] = main_ref[span, :].T.astype(BF16)
        tall_ref[t * TALL + LANES : (t + 1) * TALL, :] = rest_ref[span, :].T[: 2 * LEV].astype(BF16)


def rows_kernel(meta_ref, before_ref, context_ref, west_ref, east_ref, recv_ref, out_ref, main_ref, rest_ref):
    stage_blocks(recv_ref, main_ref, rest_ref)
    me = meta_ref[0]
    sub = lax.broadcasted_iota(jnp.int32, (ROWS, LANES), 0)
    inner = (sub >= 1) & (sub <= XS)

    def rimmed(value, at):
        value = jnp.where(sub == 0, west_ref[at : at + 1, :], value)
        return jnp.where(sub == XS + 1, east_ref[at : at + 1, :], value)

    def known(p):
        return rimmed(before_ref[p * ROWS : (p + 1) * ROWS, :].astype(F32), p)

    last = None
    tail = known(2)
    winds = rimmed(context_ref[3], 3)
    for e in range(2):
        row = global_row(meta_ref, 2 * me + e)
        across = pull(winds, 2 * e * LEV)
        east = jnp.maximum(across, 0.0)
        west = jnp.minimum(pltpu.roll(across, 1, axis=0), 0.0)
        north = jnp.where(row == BANDS * LANES - 1, 0.0, jnp.maximum(pull(winds, (2 * e + 1) * LEV), 0.0))
        south = jnp.minimum(pull(context_ref[4], e * LEV), 0.0)
        coefs = (east, west, north, south)
        added = [block_sum(meta_ref, row + near, main_ref, rest_ref) for near in (-1, 0, 1)]

        def moved(coefs, here, aside, behind, ahead):
            east, west, north, south = coefs
            here = here.astype(BF16).astype(F32)
            centre = 1.0 - east + west - north + south
            made = (
                centre * here
                + (east * pltpu.roll(here, ROWS - 1, axis=0) - west * pltpu.roll(here, 1, axis=0))
                + (aside + (north * ahead - south * behind))
            )
            return jnp.where(inner, made, 0.0)

        main = moved([wide(c) for c in coefs], known(e) + added[1][0], context_ref[e], added[0][0], added[2][0])
        out_ref[e * ROWS : (e + 1) * ROWS, :] = main.astype(BF16)
        rest = pull(tail, e * LEV) + added[1][1]
        rest = moved(coefs, rest, pull(context_ref[2], e * LEV), added[0][1], added[2][1])
        rest = lanes_below(rest, LEV)
        last = rest if e == 0 else last + pltpu.roll(rest, LEV, axis=1)
    out_ref[2 * ROWS :, :] = last.astype(BF16)


def next_rows(*args):
    return pl.pallas_call(
        rows_kernel,
        out_shape=shape((3 * ROWS, LANES), BF16),
        in_specs=[SM] + [VM] * 5,
        out_specs=VM,
        scratch_shapes=[STAGE, STAGE],
        compiler_params=params(4),
        name="rows",
    )(*args)


def place_weights(meta_ref, q):
    sub, lane = iotas((LANES, 2 * LANES))
    kept = sub - q * KEPT
    target = jnp.full(sub.shape, -1, jnp.int32)
    for block in range(BLOCKS):
        at = global_row(meta_ref, block) - meta_ref[0] * LANES
        target = jnp.where(kept == slot(block), jnp.where((at >= 0) & (at < LANES), at, -1), target)
    target = jnp.where((kept == 16) | (kept == 18), LANES, target)
    target = jnp.where(kept == 17, 2 * LANES - 1, target)
    return jnp.where(lane == target, 1.0, 0.0).astype(BF16)


def smooth_all(meta_ref, cells_ref, west_ref, east_ref, tall_ref, placed_ref, smooth_ref, edge_ref, wind_ref):
    for q in range(GROUP):
        placed_ref[...] = jnp.dot(tall_ref[...], place_weights(meta_ref, q), preferred_element_type=F32)

        def store(t, r, base):
            at = pl.multiple_of(t * TALL, TALL)
            change = placed_ref[pl.ds(at, COLS), :LANES]
            smooth_ref[r] = (base.astype(F32) + change).astype(BF16).astype(F32)

        def body(t, carry):
            r = GROUP * t + q
            x = r - 1
            store(t, r, cells_ref[x])
            at = pl.multiple_of(t * TALL, TALL)
            edge_ref[x] = placed_ref[pl.ds(at, COLS), LANES:]
            wind_ref[x] = placed_ref[pl.ds(at + COLS, LEV), LANES:]
            return carry

        first = 1 if q == 0 else 0
        last = (XS - q) // GROUP + 1
        if q == 0:
            store(0, 0, west_ref[:COLS, :])
        if (XS + 1) % GROUP == q:
            store((XS + 1) // GROUP, XS + 1, east_ref[...])
        lax.fori_loop(first, last, body, 0, unroll=True)


def stencil(x, top, winds_ref, west_ref, smooth_ref, edge_ref, wind_ref):
    lane = lax.broadcasted_iota(jnp.int32, (LEV, LANES), 1)
    courant = winds_ref[x].astype(F32)
    before = winds_ref[jnp.maximum(x - 1, 0), :LEV, :].astype(F32)
    before = jnp.where(x == 0, west_ref[COLS:, :].astype(F32), before)
    across = courant[:LEV]
    along = jnp.where(top & (lane == LANES - 1), 0.0, courant[LEV:])
    south_along = jnp.where(lane == 0, wind_ref[x], pltpu.roll(along, 1, axis=1))
    east = jnp.maximum(across, 0.0)
    west = jnp.minimum(before, 0.0)
    north = jnp.maximum(along, 0.0)
    south = jnp.minimum(south_along, 0.0)
    centre = 1.0 - east + west - north + south
    made = []
    for v in range(VAR):
        span = slice(v * LEV, (v + 1) * LEV)
        here = smooth_ref[x + 1, span, :]
        edge = edge_ref[x, span, :]
        above = jnp.where(lane == LANES - 1, edge, pltpu.roll(here, LANES - 1, axis=1))
        below = jnp.where(lane == 0, edge, pltpu.roll(here, 1, axis=1))
        made.append(
            centre * here
            + (east * smooth_ref[x + 2, span, :] - west * smooth_ref[x, span, :])
            + (north * above - south * below)
        )
    return made


SCRATCH = [
    pltpu.VMEM((KEPT * ROWS, LANES), F32),
    pltpu.VMEM((KEPT * ROWS, LANES), F32),
    pltpu.VMEM((ROWS // GROUP * TALL, LANES), BF16),
    pltpu.VMEM((ROWS // GROUP * TALL, 2 * LANES), F32),
    pltpu.VMEM((XS + 2, COLS, LANES), F32),
    pltpu.VMEM((XS, COLS, LANES), F32),
    pltpu.VMEM((XS, LEV, LANES), F32),
]


def first_kernel(
    meta_ref, cells_hbm, winds_hbm, west_ref, east_ref, recv_ref,
    out_hbm, edges_ref, to_east_hbm, to_west_hbm,
    main_ref, rest_ref, tall_ref, placed_ref, smooth_ref, edge_ref, wind_ref, out_ref, out_sem, rim_sem,
    cells_ref, cells_sem, winds_ref, winds_sem,
):
    arriving = copies(cells_hbm, cells_ref, cells_sem) + copies(winds_hbm, winds_ref, winds_sem)
    for copy in arriving:
        copy.start()
    stage_corrections(meta_ref, recv_ref, recv_ref, main_ref, rest_ref, tall_ref)
    for copy in arriving:
        copy.wait()
    smooth_all(meta_ref, cells_ref, west_ref, east_ref, tall_ref, placed_ref, smooth_ref, edge_ref, wind_ref)
    top = meta_ref[0] == BANDS - 1

    def body(x, carry):
        made = stencil(x, top, winds_ref, west_ref, smooth_ref, edge_ref, wind_ref)
        for v in range(VAR):
            out_ref[x, v * LEV : (v + 1) * LEV, :] = made[v].astype(BF16)
        return carry

    leaving = copies(out_ref, out_hbm, out_sem)
    leaving.append(pltpu.make_async_copy(out_ref.at[0], to_west_hbm, rim_sem.at[0]))
    leaving.append(pltpu.make_async_copy(out_ref.at[XS - 1], to_east_hbm, rim_sem.at[1]))
    for (start, size), copy in zip(SPANS, leaving):
        lax.fori_loop(start, start + size, body, 0, unroll=4)
        copy.start()
    for copy in leaving[-2:]:
        copy.start()
    sub, lane = iotas((LANES, LANES))
    halves = [(sub == 0) & (lane == 2 * side) | (sub == LANES - 1) & (lane == 2 * side + 1) for side in range(2)]
    ends = jnp.concatenate([jnp.where(hit, 1.0, 0.0) for hit in halves], axis=0).astype(BF16)
    total = None
    for x in range(0, XS, 2):
        pair = jnp.concatenate([out_ref[min(x + side, XS - 1)] for side in range(2)], axis=1)
        found = jnp.dot(pair, ends, preferred_element_type=F32)
        if x == XS - 1:
            found = jnp.where(lax.broadcasted_iota(jnp.int32, found.shape, 1) < 2, found, 0.0)
        found = pltpu.roll(found, 2 * x + 2, axis=1)
        total = found if total is None else total + found
    main_ref[:LANES, :] = total[:LANES].T
    rest = jnp.concatenate([total[LANES:], jnp.zeros((LANES - LEV, LANES), F32)], axis=0)
    rest_ref[:LANES, :] = rest.T
    for at in range(2):
        edges_ref[at, :ROWS, :] = main_ref[pl.ds(at, ROWS, stride=2), :].astype(BF16)
        edges_ref[at, ROWS:, :] = folded(rest_ref[pl.ds(at, ROWS, stride=2), :], LEV).astype(BF16)
    for copy in leaving:
        copy.wait()


def first_substep(*args):
    return pl.pallas_call(
        first_kernel,
        out_shape=(
            shape((XS, COLS, LANES), BF16),
            shape((2, HALO, LANES), BF16),
            shape((COLS, LANES), BF16),
            shape((COLS, LANES), BF16),
        ),
        in_specs=[SM, HB, HB] + [VM] * 3,
        out_specs=(HB, VM, HB, HB),
        scratch_shapes=SCRATCH
        + [
            pltpu.VMEM((XS, COLS, LANES), BF16),
            DMA((len(SPANS),)),
            DMA((2,)),
            pltpu.VMEM((XS, COLS, LANES), BF16),
            DMA((len(SPANS),)),
            pltpu.VMEM((XS, 2 * LEV, LANES), BF16),
            DMA((len(SPANS),)),
        ],
        compiler_params=params(58),
        name="first",
    )(*args)


def last_kernel(
    meta_ref, cells_ref, winds_ref, west_ref, east_ref, recv_ref, wind_recv_ref, wind_west_ref,
    out_ref, main_ref, rest_ref, tall_ref, placed_ref, smooth_ref, edge_ref, wind_ref,
):
    me = meta_ref[0]
    step = pl.program_id(0)

    @pl.when(step == 0)
    def _():
        stage_corrections(meta_ref, recv_ref, wind_recv_ref, main_ref, rest_ref, tall_ref)
        smooth_all(meta_ref, cells_ref, west_ref, east_ref, tall_ref, placed_ref, smooth_ref, edge_ref, wind_ref)

    top = me == BANDS - 1

    def body(y, carry):
        x = step * CHUNK + y
        made = stencil(x, top, winds_ref, wind_west_ref, smooth_ref, edge_ref, wind_ref)
        for v in range(VAR):
            out_ref[y, v * LEV : (v + 1) * LEV, :] = made[v]
        return carry

    lax.fori_loop(0, CHUNK, body, 0, unroll=3)


def last_substep(*args):
    return pl.pallas_call(
        last_kernel,
        grid=(XS // CHUNK,),
        out_shape=shape((XS, COLS, LANES), F32),
        in_specs=[SM] + [VM] * 7,
        out_specs=pl.BlockSpec((CHUNK, COLS, LANES), lambda i: (i, 0, 0)),
        scratch_shapes=SCRATCH,
        compiler_params=params(16),
        name="last",
    )(*args)


SWAP = [(i, i ^ 1) for i in range(LON_DEV)]
EASTWARD = [(i, (i + 1) % LON_DEV) for i in range(LON_DEV)]
WESTWARD = [(i, (i - 1) % LON_DEV) for i in range(LON_DEV)]
SAME_CORE = [[2 * t + core for t in range(TARGETS)] for core in range(2)]


def by_lat(messages):
    return lax.all_to_all(messages, "lat", 0, 0, tiled=True)


def filtered(rows, own_ops, other_ops):
    other = lax.ppermute(rows, "lon", SWAP)
    partial = products(rows, other, own_ops, other_ops)
    return lax.all_to_all(partial, "lon", 0, 0, tiled=True, axis_index_groups=SAME_CORE)


def shards(cotangent, winds, filter_ops, block_band, block_row):
    me = lax.axis_index("lat").astype(jnp.int32).reshape(1)
    core = (lax.axis_index("lon") & 1).astype(jnp.int32).reshape(1)
    meta = jnp.concatenate([me, core, block_band, block_row])
    own_ops, send_ops = prepare_operators(meta, jnp.pad(filter_ops, ((0, 0), (1, 2), (0, 0))))
    other_ops = lax.ppermute(send_ops, "lon", SWAP)
    send, edges, to_east, to_west = pick_rows(meta, cotangent, winds)
    west = lax.ppermute(to_east, "lon", EASTWARD)
    east = lax.ppermute(to_west, "lon", WESTWARD)
    recv, west, east = lax.optimization_barrier((by_lat(send), west, east))
    rows = unpack_rows(recv)
    swapped = filtered(rows, own_ops, other_ops)
    context, row_east, row_west = unpack_context(meta, recv, rows)
    row_from_west = lax.ppermute(row_east, "lon", EASTWARD)
    row_from_east = lax.ppermute(row_west, "lon", WESTWARD)
    swapped, row_from_west, row_from_east = lax.optimization_barrier((swapped, row_from_west, row_from_east))
    given = by_lat(totals(meta, swapped, edges))
    rows = next_rows(meta, rows, context, row_from_west, row_from_east, given)
    swapped = filtered(rows, own_ops, other_ops)
    state, edges, to_east, to_west = first_substep(meta, cotangent, winds, west, east, given)
    west2 = lax.ppermute(to_east, "lon", EASTWARD)
    east2 = lax.ppermute(to_west, "lon", WESTWARD)
    given2 = by_lat(totals(meta, swapped, edges))
    return last_substep(meta, state, winds, west2, east2, given2, given, west)


def solution(mesh):
    return jax.shard_map(
        shards,
        mesh=mesh,
        in_specs=(P("lon", None, "lat"), P("lon", None, "lat"), P("lat", "lon", None), P(), P()),
        out_specs=P("lon", None, "lat"),
        check_vma=False,
    )
```

```python
import jax
import jax.numpy as jnp
from jax import lax
from jax.experimental import pallas as pl
from jax.experimental.pallas import tpu as pltpu
from jax.sharding import PartitionSpec as P

VAR = 5
LEV = 32
COLS = VAR * LEV
XS = 45
ROWS = 48
LANES = 128
BANDS = 8
NLON = 1440
LON_DEV = 32
TARGETS = 8
TEAM = 4
BLOCKS = 16
PICKS = 56
WIRE = 6 * ROWS + 24
PACK = 120
HALO = 72
CHUNK = 9

F32 = jnp.float32
BF16 = jnp.bfloat16
VM = pl.BlockSpec(memory_space=pltpu.VMEM)
SM = pl.BlockSpec(memory_space=pltpu.SMEM)
HB = pl.BlockSpec(memory_space=pl.ANY)
DMA = pltpu.SemaphoreType.DMA
SPANS = [(start, min(8, XS - start)) for start in range(0, XS, 8)]


def shape(dims, kind):
    return jax.ShapeDtypeStruct(dims, kind)


def params(mib):
    return pltpu.CompilerParams(vmem_limit_bytes=mib * 2**20)


def iotas(dims):
    return (
        lax.broadcasted_iota(jnp.int32, dims, 0),
        lax.broadcasted_iota(jnp.int32, dims, 1),
    )


def lanes_below(value, limit):
    lane = lax.broadcasted_iota(jnp.int32, value.shape, 1)
    return jnp.where(lane < limit, value, jnp.zeros_like(value))


def dot_nt(a, b):
    return lax.dot_general(a, b, (((1,), (1,)), ((), ())), preferred_element_type=F32)


def dot_tn(a, b):
    return lax.dot_general(a, b, (((0,), (0,)), ((), ())), preferred_element_type=F32)


def operator_kernel(meta_ref, ops_ref, *out_refs):
    place = meta_ref[1]
    for t in range(TARGETS):
        tiles = []
        for member in range(TEAM):
            start = XS * ((member // 2) * 2 * TARGETS + 2 * t + member % 2) - 1
            total = None
            first = max(start, 0) // LANES * LANES
            spans = [(first, min(first + 2 * LANES, NLON))]
            if start < 0:
                spans.append(((NLON - 1) // LANES * LANES, NLON))
            if start + XS + 2 > NLON:
                spans.append((0, LANES))
            for low, high in spans:
                row, lane = iotas((ROWS, high - low))
                wanted = start + row
                wanted = jnp.where(wanted < 0, wanted + NLON, wanted)
                wanted = jnp.where(wanted >= NLON, wanted - NLON, wanted)
                hit = (lane + low == wanted) & (row < XS + 2)
                pick = jnp.where(hit, 1.0, 0.0).astype(BF16)
                window = ops_ref[:, :, low:high].reshape(2 * ROWS, high - low)
                part = dot_nt(pick, window)
                total = part if total is None else total + part
            tiles.append(total)
        rows = slice(ROWS * t, ROWS * (t + 1))
        for other in range(TEAM):
            value = tiles[other]
            for member in range(1, TEAM):
                value = jnp.where(place == member, tiles[member ^ other], value)
            out_refs[other][rows, :] = value.astype(BF16)


def prepare_operators(meta, ops):
    out = shape((TARGETS * ROWS, 2 * ROWS), BF16)
    return pl.pallas_call(
        operator_kernel,
        out_shape=(out,) * TEAM,
        in_specs=[SM, VM],
        out_specs=(VM,) * TEAM,
        compiler_params=params(6),
        name="operators",
    )(meta, ops)


def slot(block):
    return (block % 2) * BANDS + block // 2


def global_row(meta_ref, block):
    return meta_ref[2 + block] * LANES + meta_ref[2 + BLOCKS + block]


def clear_rims(ref, count):
    blank = jnp.zeros((count, LANES), ref.dtype)
    for r in (0, XS + 1, XS + 2):
        ref[pl.ds(r, count, stride=ROWS), :] = blank


def pick_weights(meta_ref):
    me = meta_ref[0]
    lane = lax.broadcasted_iota(jnp.int32, (8, LANES), 1)
    pick = lane & 63
    target = jnp.full(lane.shape, -1, jnp.int32)
    for block in range(BLOCKS):
        at = global_row(meta_ref, block) - me * LANES
        for near in range(3):
            target = jnp.where(pick == near * BLOCKS + slot(block), at + (near - 1), target)
    target = jnp.where(pick == 3 * BLOCKS, 0, target)
    target = jnp.where(pick == 3 * BLOCKS + 1, LANES - 1, target)
    sub, lane = iotas((LANES, LANES))
    hit = sub == jnp.broadcast_to(target[:1], (LANES, LANES))
    halves = [jnp.where(hit & ((lane < 64) == side), 1.0, 0.0) for side in (True, False)]
    return jnp.concatenate(halves, axis=0).astype(BF16)


def keep(value, *starts):
    lane = lax.broadcasted_iota(jnp.int32, value.shape, 1)
    hit = (lane >= starts[0]) & (lane < starts[0] + LEV)
    for start in starts[1:]:
        hit = hit | ((lane >= start) & (lane < start + LEV))
    return jnp.where(hit, value, jnp.zeros_like(value))


def pull(value, start):
    moved = pltpu.roll(value, LANES - start, axis=1) if start else value
    return lanes_below(moved, LEV)


def wide(value):
    value = value + pltpu.roll(value, LEV, axis=1)
    return value + pltpu.roll(value, 2 * LEV, axis=1)


def folded(value, width):
    half = ROWS // 2
    return value[:half] + pltpu.roll(value[half:], width, axis=1)


def unfolded(value, start, width, limit):
    low = pltpu.roll(value, LANES - start, axis=1) if start else value
    high = pltpu.roll(value, LANES - start - width, axis=1)
    return jnp.concatenate([lanes_below(low, limit), lanes_below(high, limit)], axis=0)


def pack_messages(meta_ref, main_ref, rest_ref, send_ref, edges_ref, leaving):
    me = meta_ref[0]

    def picked(ref, k):
        return ref[k * ROWS : (k + 1) * ROWS, :]

    def add(d, start, count, value):
        span = slice(start, start + count)
        send_ref[d, span, :] = (send_ref[d, span, :].astype(F32) + value).astype(BF16)

    for block in range(BLOCKS):
        d, e = block // 2, block % 2
        k = slot(block)
        at = global_row(meta_ref, block) - me * LANES

        @pl.when((at >= -1) & (at <= LANES))
        def _():
            mine = (at >= 0) & (at < LANES)
            here = picked(rest_ref, BLOCKS + k)
            behind = picked(rest_ref, k)
            before = pull(behind, 2 * LEV)
            one = lanes_below(jnp.ones_like(here), LEV)
            north = jnp.where(mine, jnp.maximum(pull(here, 2 * LEV), 0.0), one)
            south = jnp.where(mine, jnp.minimum(before, 0.0), -one)
            main = wide(north) * picked(main_ref, 2 * BLOCKS + k) - wide(south) * picked(main_ref, k)
            rest = north * picked(rest_ref, 2 * BLOCKS + k) - south * behind
            send_ref[d, e * ROWS : (e + 1) * ROWS, :] = picked(main_ref, BLOCKS + k).astype(BF16)
            send_ref[d, (2 + e) * ROWS : (3 + e) * ROWS, :] = main.astype(BF16)
            tail = keep(here, 0) + pltpu.roll(rest, 2 * LEV, axis=1)
            add(d, 4 * ROWS, ROWS, pltpu.roll(tail, LEV, axis=1) if e else tail)
            add(d, 5 * ROWS, ROWS, pltpu.roll(keep(here, LEV, 2 * LEV), (1 if e else 3) * LEV, axis=1))
            add(d, 6 * ROWS, ROWS // 2, folded(pltpu.roll(before, LEV, axis=1) if e else before, 2 * LEV))

        if e:
            leaving[d].start()

    for at in range(2):
        k = 3 * BLOCKS + at
        edges_ref[at, :ROWS, :] = picked(main_ref, k).astype(BF16)
        rest = picked(rest_ref, k)
        rest = folded(keep(rest, 0), LEV) + folded(keep(rest, 2 * LEV), LEV)
        edges_ref[at, ROWS:, :] = rest.astype(BF16)


def clear(*refs):
    for ref in refs:
        ref[...] = jnp.zeros(ref.shape, ref.dtype)


def copies(source_ref, target_ref, sem_ref):
    return [
        pltpu.make_async_copy(source_ref.at[pl.ds(start, size)], target_ref.at[pl.ds(start, size)], sem_ref.at[n])
        for n, (start, size) in enumerate(SPANS)
    ]


class Scalars:
    def __init__(self, me, band_ref, row_ref):
        self.me, self.band_ref, self.row_ref = me, band_ref, row_ref

    def __getitem__(self, at):
        if at == 0:
            return self.me
        return self.band_ref[at - 2] if at < 2 + BLOCKS else self.row_ref[at - 2 - BLOCKS]


def pick_kernel(
    band_ref, row_ref, cells_hbm, winds_hbm, send_hbm, edges_ref, east_ref, west_ref,
    main_ref, rest_ref, cells_ref, winds_ref, send_ref, cells_sem, winds_sem, send_sem,
):
    meta_ref = Scalars(lax.axis_index("lat").astype(jnp.int32), band_ref, row_ref)
    arriving = list(zip(copies(cells_hbm, cells_ref, cells_sem), copies(winds_hbm, winds_ref, winds_sem)))
    for pair in arriving:
        for copy in pair:
            copy.start()
    clear_rims(main_ref, PICKS)
    clear_rims(rest_ref, PICKS)
    weights = pick_weights(meta_ref)
    clear(send_ref)
    blank = jnp.zeros((LEV, 2 * LANES), BF16)
    for (start, size), pair in zip(SPANS, arriving):
        for copy in pair:
            copy.wait()
        for y in range(start, start + size, 2):
            both = (y, min(y + 1, XS - 1))
            main = jnp.concatenate([cells_ref[z, :LANES, :] for z in both], axis=1)
            rest = jnp.concatenate([cells_ref[z, LANES:, :] for z in both], axis=1)
            wind = jnp.concatenate([winds_ref[z] for z in both], axis=1)
            rest = jnp.concatenate([rest, wind, blank], axis=0)
            main = jnp.dot(main, weights, preferred_element_type=F32).astype(BF16).T.astype(F32)
            rest = jnp.dot(rest, weights, preferred_element_type=F32).astype(BF16).T.astype(F32)
            for side in range(min(2, XS - y)):
                at = pl.ds(y + side + 1, PICKS, stride=ROWS)
                main_ref[at, :] = main[64 * side : 64 * side + PICKS]
                rest_ref[at, :] = rest[64 * side : 64 * side + PICKS]
    east_ref[:COLS, :] = cells_ref[XS - 1]
    east_ref[COLS:, :] = winds_ref[XS - 1, :LEV, :]
    west_ref[...] = cells_ref[0]
    leaving = [pltpu.make_async_copy(send_ref.at[d], send_hbm.at[d], send_sem.at[d]) for d in range(BANDS)]
    pack_messages(meta_ref, main_ref, rest_ref, send_ref, edges_ref, leaving)
    for copy in leaving:
        copy.wait()


STAGE = pltpu.VMEM((24 * ROWS, LANES), F32)
PICKED = pltpu.VMEM((PICKS * ROWS, LANES), F32)


def pick_rows(band, row, cells, winds):
    return pl.pallas_call(
        pick_kernel,
        out_shape=(
            shape((BANDS, WIRE, LANES), BF16),
            shape((2, HALO, LANES), BF16),
            shape((COLS + LEV, LANES), BF16),
            shape((COLS, LANES), BF16),
        ),
        in_specs=[SM, SM, HB, HB],
        out_specs=(HB, VM, VM, VM),
        scratch_shapes=[
            PICKED,
            PICKED,
            pltpu.VMEM((XS, COLS, LANES), BF16),
            pltpu.VMEM((XS, 2 * LEV, LANES), BF16),
            pltpu.VMEM((BANDS, WIRE, LANES), BF16),
            DMA((len(SPANS),)),
            DMA((len(SPANS),)),
            DMA((BANDS,)),
        ],
        compiler_params=params(58),
        name="pick",
    )(band, row, cells, winds)


def added(recv_ref, span):
    total = recv_ref[0, span, :].astype(F32)
    for s in range(1, BANDS):
        total = total + recv_ref[s, span, :].astype(F32)
    return total


def unpack_kernel(recv_ref, rows_ref):
    rows_ref[: 2 * ROWS, :] = added(recv_ref, slice(0, 2 * ROWS)).astype(BF16)
    tail = added(recv_ref, slice(4 * ROWS, 5 * ROWS))
    rows_ref[2 * ROWS :, :] = lanes_below(tail, 2 * LEV).astype(BF16)


def unpack_rows(recv):
    return pl.pallas_call(
        unpack_kernel,
        out_shape=shape((3 * ROWS, LANES), BF16),
        in_specs=[VM],
        out_specs=VM,
        compiler_params=params(8),
        name="unpack",
    )(recv)


def context_kernel(meta_ref, recv_ref, rows_ref, context_ref, to_east_ref, to_west_ref):
    me = meta_ref[0]
    winds = added(recv_ref, slice(5 * ROWS, 6 * ROWS))
    souths = unfolded(added(recv_ref, slice(6 * ROWS, WIRE)), 0, 2 * LEV, 2 * LEV)
    tails = None
    for e in range(2):
        band = meta_ref[2 + 2 * me + e]
        row = meta_ref[2 + BLOCKS + 2 * me + e]
        north = jnp.maximum(pull(winds, (2 * e + 1) * LEV), 0.0)
        south = jnp.minimum(pull(souths, e * LEV), 0.0)
        main = recv_ref[band, (2 + e) * ROWS : (3 + e) * ROWS, :].astype(F32)
        rest = pull(recv_ref[band, 4 * ROWS : 5 * ROWS, :].astype(F32), (2 + e) * LEV)
        for source, there, coef in (
            (jnp.minimum(band + 1, BANDS - 1), (row == LANES - 1) & (band < BANDS - 1), north),
            (jnp.maximum(band - 1, 0), (row == 0) & (band > 0), -south),
        ):
            share = jnp.where(there, coef, 0.0)
            main = main + wide(share) * recv_ref[source, (2 + e) * ROWS : (3 + e) * ROWS, :].astype(F32)
            rest = rest + share * pull(recv_ref[source, 4 * ROWS : 5 * ROWS, :].astype(F32), (2 + e) * LEV)
        context_ref[e] = main
        tails = rest if e == 0 else tails + pltpu.roll(rest, LEV, axis=1)
    context_ref[2] = tails
    context_ref[3] = winds
    context_ref[4] = souths
    clear(to_east_ref, to_west_ref)
    rims = [rows_ref[p * ROWS : (p + 1) * ROWS, :].astype(F32) for p in range(3)] + [winds]
    for at, tile in enumerate(rims):
        to_east_ref[at : at + 1, :] = tile[XS : XS + 1]
        to_west_ref[at : at + 1, :] = tile[1:2]


def unpack_context(meta, recv, rows):
    edge = shape((8, LANES), F32)
    return pl.pallas_call(
        context_kernel,
        out_shape=(shape((5, ROWS, LANES), F32), edge, edge),
        in_specs=[SM, VM, VM],
        out_specs=(VM,) * 3,
        compiler_params=params(8),
        name="context",
    )(meta, recv, rows)


def spread_blocks(rows_ref):
    first = rows_ref[:ROWS, :]
    second = rows_ref[ROWS : 2 * ROWS, :]
    rest = rows_ref[2 * ROWS :, :].astype(F32)
    lower = lanes_below(rest, LEV)
    upper = rest - lower
    blank = jnp.zeros_like(first)
    return jnp.concatenate(
        [
            jnp.concatenate([first, blank, lower.astype(BF16)], axis=1),
            jnp.concatenate([blank, second, upper.astype(BF16)], axis=1),
        ],
        axis=0,
    )


def product_kernel(*refs):
    out_ref = refs[-1]
    rows = [spread_blocks(ref) for ref in refs[:TEAM]]
    for q in range(2):
        span = slice(4 * ROWS * q, 4 * ROWS * (q + 1))
        made = None
        for ops_ref, values in zip(refs[TEAM : 2 * TEAM], rows):
            part = jnp.dot(ops_ref[span, :], values, preferred_element_type=F32)
            made = part if made is None else made + part
        for s in range(4):
            part = made[ROWS * s : ROWS * (s + 1)]
            t = 4 * q + s
            out_ref[t, :ROWS, :] = part[:, :LANES].astype(BF16)
            out_ref[t, ROWS : 2 * ROWS, :] = part[:, LANES : 2 * LANES].astype(BF16)
            out_ref[t, 2 * ROWS :, :] = folded(part[:, 2 * LANES :], 2 * LEV).astype(BF16)


def products(rows, ops):
    return pl.pallas_call(
        product_kernel,
        out_shape=shape((TARGETS, PACK, LANES), BF16),
        in_specs=[VM] * (2 * TEAM),
        out_specs=VM,
        compiler_params=params(6),
        name="product",
    )(*rows, *ops)


def total_kernel(meta_ref, recv_ref, edges_hbm, out_ref, edges_ref, sem_ref):
    arriving = pltpu.make_async_copy(edges_hbm, edges_ref, sem_ref.at[0])
    arriving.start()
    total = recv_ref[0].astype(F32)
    for s in range(1, TARGETS):
        total = total + recv_ref[s].astype(F32)
    total = total.astype(BF16)
    me = meta_ref[0]
    for d in range(BANDS):
        out_ref[d, :PACK, :] = total
    arriving.wait()
    for d in range(BANDS):
        edge = jnp.where(d == me + 1, edges_ref[1], jnp.zeros((HALO, LANES), BF16))
        out_ref[d, PACK:, :] = jnp.where(d == me - 1, edges_ref[0], edge)


def totals(meta, recv, edges):
    return pl.pallas_call(
        total_kernel,
        out_shape=shape((BANDS, PACK + HALO, LANES), BF16),
        in_specs=[SM, VM, HB],
        out_specs=VM,
        scratch_shapes=[pltpu.VMEM((2, HALO, LANES), BF16), DMA((1,))],
        compiler_params=params(4),
        name="total",
    )(meta, recv, edges)


def halo_rows(meta_ref, recv_ref):
    me = meta_ref[0]
    halos = []
    for near, there in ((me - 1, me > 0), (me + 1, me < BANDS - 1)):
        source = jnp.clip(near, 0, BANDS - 1)
        main = recv_ref[source, PACK : PACK + ROWS, :].astype(F32)
        rest = recv_ref[source, PACK + ROWS :, :].astype(F32)
        found = (main, unfolded(rest, 0, LEV, LEV), unfolded(rest, 2 * LEV, LEV, LEV))
        halos.append([jnp.where(there, value, 0.0) for value in found])
    return halos[0][:2], halos[1][:2], halos[0][2]


def stage_blocks(recv_ref, main_ref, rest_ref):
    half = ROWS // 2
    for source in range(BANDS):
        packed = recv_ref[source, 2 * ROWS : PACK, :].astype(F32)
        for b in range(2):
            at = (b * BANDS + source) * ROWS
            main_ref[at : at + ROWS, :] = recv_ref[source, b * ROWS : (b + 1) * ROWS, :].astype(F32)
            rest_ref[at : at + half, :] = pull(packed, b * LEV)
            rest_ref[at + half : at + ROWS, :] = pull(packed, (2 + b) * LEV)


def block_sum(meta_ref, row, main_ref, rest_ref):
    main = jnp.zeros((ROWS, LANES), F32)
    rest = jnp.zeros((ROWS, LANES), F32)
    for block in range(BLOCKS):
        share = jnp.where(global_row(meta_ref, block) == row, 1.0, 0.0)
        k = slot(block) * ROWS
        main = main + share * main_ref[k : k + ROWS, :]
        rest = rest + share * rest_ref[k : k + ROWS, :]
    return main, rest


KEPT = 32
GROUP = LANES // KEPT
TALL = COLS + LEV


def stage_corrections(meta_ref, recv_ref, wind_recv_ref, main_ref, rest_ref, tall_ref):
    clear(main_ref, rest_ref)
    me = meta_ref[0]
    halos = halo_rows(meta_ref, recv_ref)
    sums = [list(halos[0]), list(halos[1])]
    for source in range(BANDS):
        packed = recv_ref[source, 2 * ROWS : PACK, :].astype(F32)
        for b in range(2):
            k = b * BANDS + source
            main = recv_ref[source, b * ROWS : (b + 1) * ROWS, :].astype(F32)
            rest = unfolded(packed, b * LEV, 2 * LEV, LEV)
            main_ref[pl.ds(k, ROWS, stride=KEPT), :] = main
            rest_ref[pl.ds(k, ROWS, stride=KEPT), :] = rest
            for at, row in enumerate((me * LANES - 1, (me + 1) * LANES)):
                share = jnp.where(global_row(meta_ref, 2 * source + b) == row, 1.0, 0.0)
                sums[at][0] = sums[at][0] + share * main
                sums[at][1] = sums[at][1] + share * rest
    for at in range(2):
        main_ref[pl.ds(16 + at, ROWS, stride=KEPT), :] = sums[at][0].astype(BF16).astype(F32)
        rest_ref[pl.ds(16 + at, ROWS, stride=KEPT), :] = sums[at][1].astype(BF16).astype(F32)
    wind = halo_rows(meta_ref, wind_recv_ref)[2]
    rest_ref[pl.ds(18, ROWS, stride=KEPT), :] = pltpu.roll(wind, LEV, axis=1)
    for t in range(ROWS // GROUP):
        span = slice(t * LANES, (t + 1) * LANES)
        tall_ref[t * TALL : t * TALL + LANES, :] = main_ref[span, :].T.astype(BF16)
        tall_ref[t * TALL + LANES : (t + 1) * TALL, :] = rest_ref[span, :].T[: 2 * LEV].astype(BF16)


def rows_kernel(meta_ref, before_ref, context_ref, west_ref, east_ref, recv_ref, out_ref, main_ref, rest_ref):
    stage_blocks(recv_ref, main_ref, rest_ref)
    me = meta_ref[0]
    sub = lax.broadcasted_iota(jnp.int32, (ROWS, LANES), 0)
    inner = (sub >= 1) & (sub <= XS)

    def rimmed(value, at):
        value = jnp.where(sub == 0, west_ref[at : at + 1, :], value)
        return jnp.where(sub == XS + 1, east_ref[at : at + 1, :], value)

    def known(p):
        return rimmed(before_ref[p * ROWS : (p + 1) * ROWS, :].astype(F32), p)

    last = None
    tail = known(2)
    winds = rimmed(context_ref[3], 3)
    for e in range(2):
        row = global_row(meta_ref, 2 * me + e)
        across = pull(winds, 2 * e * LEV)
        east = jnp.maximum(across, 0.0)
        west = jnp.minimum(pltpu.roll(across, 1, axis=0), 0.0)
        north = jnp.where(row == BANDS * LANES - 1, 0.0, jnp.maximum(pull(winds, (2 * e + 1) * LEV), 0.0))
        south = jnp.minimum(pull(context_ref[4], e * LEV), 0.0)
        coefs = (east, west, north, south)
        added = [block_sum(meta_ref, row + near, main_ref, rest_ref) for near in (-1, 0, 1)]

        def moved(coefs, here, aside, behind, ahead):
            east, west, north, south = coefs
            here = here.astype(BF16).astype(F32)
            centre = 1.0 - east + west - north + south
            made = (
                centre * here
                + (east * pltpu.roll(here, ROWS - 1, axis=0) - west * pltpu.roll(here, 1, axis=0))
                + (aside + (north * ahead - south * behind))
            )
            return jnp.where(inner, made, 0.0)

        main = moved([wide(c) for c in coefs], known(e) + added[1][0], context_ref[e], added[0][0], added[2][0])
        out_ref[e * ROWS : (e + 1) * ROWS, :] = main.astype(BF16)
        rest = pull(tail, e * LEV) + added[1][1]
        rest = moved(coefs, rest, pull(context_ref[2], e * LEV), added[0][1], added[2][1])
        rest = lanes_below(rest, LEV)
        last = rest if e == 0 else last + pltpu.roll(rest, LEV, axis=1)
    out_ref[2 * ROWS :, :] = last.astype(BF16)


def next_rows(*args):
    return pl.pallas_call(
        rows_kernel,
        out_shape=shape((3 * ROWS, LANES), BF16),
        in_specs=[SM] + [VM] * 5,
        out_specs=VM,
        scratch_shapes=[STAGE, STAGE],
        compiler_params=params(4),
        name="rows",
    )(*args)


def place_weights(meta_ref, q):
    sub, lane = iotas((LANES, 2 * LANES))
    kept = sub - q * KEPT
    target = jnp.full(sub.shape, -1, jnp.int32)
    for block in range(BLOCKS):
        at = global_row(meta_ref, block) - meta_ref[0] * LANES
        target = jnp.where(kept == slot(block), jnp.where((at >= 0) & (at < LANES), at, -1), target)
    target = jnp.where((kept == 16) | (kept == 18), LANES, target)
    target = jnp.where(kept == 17, 2 * LANES - 1, target)
    return jnp.where(lane == target, 1.0, 0.0).astype(BF16)


def advance(meta_ref, cells_ref, winds_ref, west_ref, east_ref, wind_west_ref, tall_ref, placed_ref, smooth_ref, emit):
    for q in range(GROUP):
        placed_ref[q] = jnp.dot(tall_ref[...], place_weights(meta_ref, q), preferred_element_type=F32)
    top = meta_ref[0] == BANDS - 1

    def smooth(r, base):
        at = pl.multiple_of((r // GROUP) * TALL, TALL)
        change = placed_ref[r % GROUP, pl.ds(at, COLS), :LANES]
        smooth_ref[r] = (base.astype(F32) + change).astype(BF16).astype(F32)

    smooth(0, west_ref[:COLS, :])
    smooth(1, cells_ref[0])
    smooth(XS + 1, east_ref[...])

    def body(x, carry):
        r = jnp.minimum(x + 2, XS)
        smooth(r, cells_ref[r - 1])
        made = stencil(x, top, winds_ref, wind_west_ref, smooth_ref, placed_ref)
        emit(x, made)
        return carry

    return body


def stencil(x, top, winds_ref, west_ref, smooth_ref, placed_ref):
    at = pl.multiple_of(((x + 1) // GROUP) * TALL, TALL)
    q = (x + 1) % GROUP
    lane = lax.broadcasted_iota(jnp.int32, (LEV, LANES), 1)
    courant = winds_ref[x].astype(F32)
    before = winds_ref[jnp.maximum(x - 1, 0), :LEV, :].astype(F32)
    before = jnp.where(x == 0, west_ref[COLS:, :].astype(F32), before)
    across = courant[:LEV]
    along = jnp.where(top & (lane == LANES - 1), 0.0, courant[LEV:])
    south_along = jnp.where(lane == 0, placed_ref[q, pl.ds(at + COLS, LEV), LANES:], pltpu.roll(along, 1, axis=1))
    east = jnp.maximum(across, 0.0)
    west = jnp.minimum(before, 0.0)
    north = jnp.maximum(along, 0.0)
    south = jnp.minimum(south_along, 0.0)
    centre = 1.0 - east + west - north + south
    made = []
    for v in range(VAR):
        span = slice(v * LEV, (v + 1) * LEV)
        here = smooth_ref[x + 1, span, :]
        edge = placed_ref[q, pl.ds(at + v * LEV, LEV), LANES:]
        above = jnp.where(lane == LANES - 1, edge, pltpu.roll(here, LANES - 1, axis=1))
        below = jnp.where(lane == 0, edge, pltpu.roll(here, 1, axis=1))
        made.append(
            centre * here
            + (east * smooth_ref[x + 2, span, :] - west * smooth_ref[x, span, :])
            + (north * above - south * below)
        )
    return made


SCRATCH = [
    pltpu.VMEM((KEPT * ROWS, LANES), F32),
    pltpu.VMEM((KEPT * ROWS, LANES), F32),
    pltpu.VMEM((ROWS // GROUP * TALL, LANES), BF16),
    pltpu.VMEM((GROUP, ROWS // GROUP * TALL, 2 * LANES), F32),
    pltpu.VMEM((XS + 2, COLS, LANES), F32),
]


def first_kernel(
    meta_ref, cells_hbm, winds_hbm, west_ref, east_ref, recv_ref,
    out_hbm, edges_ref, to_east_hbm, to_west_hbm,
    main_ref, rest_ref, tall_ref, placed_ref, smooth_ref, out_ref, out_sem, rim_sem,
    cells_ref, cells_sem, winds_ref, winds_sem,
):
    arriving = copies(cells_hbm, cells_ref, cells_sem) + copies(winds_hbm, winds_ref, winds_sem)
    for copy in arriving:
        copy.start()
    stage_corrections(meta_ref, recv_ref, recv_ref, main_ref, rest_ref, tall_ref)
    for copy in arriving:
        copy.wait()

    def emit(x, made):
        for v in range(VAR):
            out_ref[x, v * LEV : (v + 1) * LEV, :] = made[v].astype(BF16)

    body = advance(
        meta_ref, cells_ref, winds_ref, west_ref, east_ref, west_ref, tall_ref, placed_ref, smooth_ref, emit
    )
    leaving = copies(out_ref, out_hbm, out_sem)
    leaving.append(pltpu.make_async_copy(out_ref.at[0], to_west_hbm, rim_sem.at[0]))
    leaving.append(pltpu.make_async_copy(out_ref.at[XS - 1], to_east_hbm, rim_sem.at[1]))
    for (start, size), copy in zip(SPANS, leaving):
        lax.fori_loop(start, start + size, body, 0, unroll=4)
        copy.start()
    for copy in leaving[-2:]:
        copy.start()
    sub, lane = iotas((LANES, LANES))
    halves = [(sub == 0) & (lane == 2 * side) | (sub == LANES - 1) & (lane == 2 * side + 1) for side in range(2)]
    ends = jnp.concatenate([jnp.where(hit, 1.0, 0.0) for hit in halves], axis=0).astype(BF16)
    total = None
    for x in range(0, XS, 2):
        pair = jnp.concatenate([out_ref[min(x + side, XS - 1)] for side in range(2)], axis=1)
        found = jnp.dot(pair, ends, preferred_element_type=F32)
        if x == XS - 1:
            found = jnp.where(lax.broadcasted_iota(jnp.int32, found.shape, 1) < 2, found, 0.0)
        found = pltpu.roll(found, 2 * x + 2, axis=1)
        total = found if total is None else total + found
    main_ref[:LANES, :] = total[:LANES].T
    rest = jnp.concatenate([total[LANES:], jnp.zeros((LANES - LEV, LANES), F32)], axis=0)
    rest_ref[:LANES, :] = rest.T
    for at in range(2):
        edges_ref[at, :ROWS, :] = main_ref[pl.ds(at, ROWS, stride=2), :].astype(BF16)
        edges_ref[at, ROWS:, :] = folded(rest_ref[pl.ds(at, ROWS, stride=2), :], LEV).astype(BF16)
    for copy in leaving:
        copy.wait()


def first_substep(*args):
    return pl.pallas_call(
        first_kernel,
        out_shape=(
            shape((XS, COLS, LANES), BF16),
            shape((2, HALO, LANES), BF16),
            shape((COLS, LANES), BF16),
            shape((COLS, LANES), BF16),
        ),
        in_specs=[SM, HB, HB] + [VM] * 3,
        out_specs=(HB, VM, HB, HB),
        scratch_shapes=SCRATCH
        + [
            pltpu.VMEM((XS, COLS, LANES), BF16),
            DMA((len(SPANS),)),
            DMA((2,)),
            pltpu.VMEM((XS, COLS, LANES), BF16),
            DMA((len(SPANS),)),
            pltpu.VMEM((XS, 2 * LEV, LANES), BF16),
            DMA((len(SPANS),)),
        ],
        compiler_params=params(58),
        name="first",
    )(*args)


def last_kernel(
    meta_ref, cells_ref, winds_ref, west_ref, east_ref, recv_ref, wind_recv_ref, wind_west_ref,
    out_hbm, main_ref, rest_ref, tall_ref, placed_ref, smooth_ref, out_ref, out_sem,
):
    stage_corrections(meta_ref, recv_ref, wind_recv_ref, main_ref, rest_ref, tall_ref)

    def emit(x, made):
        for v in range(VAR):
            out_ref[x, v * LEV : (v + 1) * LEV, :] = made[v]

    body = advance(
        meta_ref, cells_ref, winds_ref, west_ref, east_ref, wind_west_ref, tall_ref, placed_ref, smooth_ref, emit
    )
    leaving = copies(out_ref, out_hbm, out_sem)
    for (start, size), copy in zip(SPANS, leaving):
        lax.fori_loop(start, start + size, body, 0, unroll=4)
        copy.start()
    for copy in leaving:
        copy.wait()


def last_substep(*args):
    return pl.pallas_call(
        last_kernel,
        out_shape=shape((XS, COLS, LANES), F32),
        in_specs=[SM] + [VM] * 7,
        out_specs=HB,
        scratch_shapes=SCRATCH + [pltpu.VMEM((XS, COLS, LANES), F32), DMA((len(SPANS),))],
        compiler_params=params(24),
        name="last",
    )(*args)


def stay_kernel(cells_hbm, message_hbm, cells_ref, sem_ref):
    arriving = copies(cells_hbm, cells_ref, sem_ref)
    for copy in arriving:
        copy.start()
    for copy in arriving:
        copy.wait()


def bring_back(cells, message):
    return pl.pallas_call(
        stay_kernel,
        out_shape=shape((XS, COLS, LANES), BF16),
        in_specs=[HB, HB],
        out_specs=VM,
        scratch_shapes=[DMA((len(SPANS),))],
        compiler_params=params(4),
        name="stay",
    )(cells, message)


TEAMMATES = [[(i, i ^ (16 * (other // 2) + other % 2)) for i in range(LON_DEV)] for other in range(1, TEAM)]
EASTWARD = [(i, (i + 1) % LON_DEV) for i in range(LON_DEV)]
WESTWARD = [(i, (i - 1) % LON_DEV) for i in range(LON_DEV)]
ALONG_Z = [[16 * (place // 2) + 2 * t + place % 2 for t in range(TARGETS)] for place in range(TEAM)]


def by_lat(messages):
    return lax.all_to_all(messages, "lat", 0, 0, tiled=True)


def filtered(rows, ops):
    team = [rows] + [lax.ppermute(rows, "lon", mates) for mates in TEAMMATES]
    partial = products(team, ops)
    return lax.all_to_all(partial, "lon", 0, 0, tiled=True, axis_index_groups=ALONG_Z)


def shards(cotangent, winds, filter_ops, block_band, block_row):
    me = lax.axis_index("lat").astype(jnp.int32).reshape(1)
    at = lax.axis_index("lon").astype(jnp.int32)
    place = ((at >> 4) * 2 + (at & 1)).reshape(1)
    meta = jnp.concatenate([me, place, block_band, block_row])
    made = prepare_operators(meta, jnp.pad(filter_ops, ((0, 0), (1, 2), (0, 0))))
    ops = [made[0]] + [lax.ppermute(part, "lon", mates) for part, mates in zip(made[1:], TEAMMATES)]
    send, edges, to_east, to_west = pick_rows(block_band, block_row, cotangent, winds)
    west = lax.ppermute(to_east, "lon", EASTWARD)
    east = lax.ppermute(to_west, "lon", WESTWARD)
    recv, west, east = lax.optimization_barrier((by_lat(send), west, east))
    rows = unpack_rows(recv)
    swapped = filtered(rows, ops)
    context, row_east, row_west = unpack_context(meta, recv, rows)
    row_from_west = lax.ppermute(row_east, "lon", EASTWARD)
    row_from_east = lax.ppermute(row_west, "lon", WESTWARD)
    swapped, row_from_west, row_from_east = lax.optimization_barrier((swapped, row_from_west, row_from_east))
    given = by_lat(totals(meta, swapped, edges))
    rows = next_rows(meta, rows, context, row_from_west, row_from_east, given)
    swapped = filtered(rows, ops)
    state, edges, to_east, to_west = first_substep(meta, cotangent, winds, west, east, given)
    west2 = lax.ppermute(to_east, "lon", EASTWARD)
    east2 = lax.ppermute(to_west, "lon", WESTWARD)
    message = totals(meta, swapped, edges)
    given2 = by_lat(message)
    return last_substep(meta, bring_back(state, message), winds, west2, east2, given2, given, west)


def solution(mesh):
    return jax.shard_map(
        shards,
        mesh=mesh,
        in_specs=(P("lon", None, "lat"), P("lon", None, "lat"), P("lat", "lon", None), P(), P()),
        out_specs=P("lon", None, "lat"),
        check_vma=False,
    )
```

```python
import jax
import jax.numpy as jnp
from jax import lax
from jax.experimental import pallas as pl
from jax.experimental.pallas import tpu as pltpu
from jax.sharding import PartitionSpec as P

VAR = 5
LEV = 32
COLS = VAR * LEV
XS = 45
ROWS = 48
LANES = 128
BANDS = 8
NLON = 1440
LON_DEV = 32
TARGETS = 8
TEAM = 4
BLOCKS = 16
PICKS = 56
WIRE = 6 * ROWS + 24
PACK = 120
HALO = 72
CHUNK = 9

F32 = jnp.float32
BF16 = jnp.bfloat16
VM = pl.BlockSpec(memory_space=pltpu.VMEM)
SM = pl.BlockSpec(memory_space=pltpu.SMEM)
HB = pl.BlockSpec(memory_space=pl.ANY)
DMA = pltpu.SemaphoreType.DMA
SPANS = [(start, min(8, XS - start)) for start in range(0, XS, 8)]


def shape(dims, kind):
    return jax.ShapeDtypeStruct(dims, kind)


def params(mib):
    return pltpu.CompilerParams(vmem_limit_bytes=mib * 2**20)


def iotas(dims):
    return (
        lax.broadcasted_iota(jnp.int32, dims, 0),
        lax.broadcasted_iota(jnp.int32, dims, 1),
    )


def lanes_below(value, limit):
    lane = lax.broadcasted_iota(jnp.int32, value.shape, 1)
    return jnp.where(lane < limit, value, jnp.zeros_like(value))


def dot_nt(a, b):
    return lax.dot_general(a, b, (((1,), (1,)), ((), ())), preferred_element_type=F32)


def dot_tn(a, b):
    return lax.dot_general(a, b, (((0,), (0,)), ((), ())), preferred_element_type=F32)


def operator_kernel(meta_ref, ops_ref, *out_refs):
    place = meta_ref[1]
    for t in range(TARGETS):
        tiles = []
        for member in range(TEAM):
            start = XS * ((member // 2) * 2 * TARGETS + 2 * t + member % 2) - 1
            total = None
            first = max(start, 0) // LANES * LANES
            spans = [(first, min(first + 2 * LANES, NLON))]
            if start < 0:
                spans.append(((NLON - 1) // LANES * LANES, NLON))
            if start + XS + 2 > NLON:
                spans.append((0, LANES))
            for low, high in spans:
                row, lane = iotas((ROWS, high - low))
                wanted = start + row
                wanted = jnp.where(wanted < 0, wanted + NLON, wanted)
                wanted = jnp.where(wanted >= NLON, wanted - NLON, wanted)
                hit = (lane + low == wanted) & (row < XS + 2)
                pick = jnp.where(hit, 1.0, 0.0).astype(BF16)
                window = ops_ref[:, :, low:high].reshape(2 * ROWS, high - low)
                part = dot_nt(pick, window)
                total = part if total is None else total + part
            tiles.append(total)
        rows = slice(ROWS * t, ROWS * (t + 1))
        for other in range(TEAM):
            value = tiles[other]
            for member in range(1, TEAM):
                value = jnp.where(place == member, tiles[member ^ other], value)
            out_refs[other][rows, :] = value.astype(BF16)


def prepare_operators(meta, ops):
    out = shape((TARGETS * ROWS, 2 * ROWS), BF16)
    return pl.pallas_call(
        operator_kernel,
        out_shape=(out,) * TEAM,
        in_specs=[SM, VM],
        out_specs=(VM,) * TEAM,
        compiler_params=params(6),
        name="operators",
    )(meta, ops)


def slot(block):
    return (block % 2) * BANDS + block // 2


def global_row(meta_ref, block):
    return meta_ref[2 + block] * LANES + meta_ref[2 + BLOCKS + block]


def clear_rims(ref, count):
    blank = jnp.zeros((count, LANES), ref.dtype)
    for r in (0, XS + 1, XS + 2):
        ref[pl.ds(r, count, stride=ROWS), :] = blank


def pick_weights(meta_ref):
    me = meta_ref[0]
    lane = lax.broadcasted_iota(jnp.int32, (8, LANES), 1)
    pick = lane & 63
    target = jnp.full(lane.shape, -1, jnp.int32)
    for block in range(BLOCKS):
        at = global_row(meta_ref, block) - me * LANES
        for near in range(3):
            target = jnp.where(pick == near * BLOCKS + slot(block), at + (near - 1), target)
    target = jnp.where(pick == 3 * BLOCKS, 0, target)
    target = jnp.where(pick == 3 * BLOCKS + 1, LANES - 1, target)
    sub, lane = iotas((LANES, LANES))
    hit = sub == jnp.broadcast_to(target[:1], (LANES, LANES))
    halves = [jnp.where(hit & ((lane < 64) == side), 1.0, 0.0) for side in (True, False)]
    return jnp.concatenate(halves, axis=0).astype(BF16)


def keep(value, *starts):
    lane = lax.broadcasted_iota(jnp.int32, value.shape, 1)
    hit = (lane >= starts[0]) & (lane < starts[0] + LEV)
    for start in starts[1:]:
        hit = hit | ((lane >= start) & (lane < start + LEV))
    return jnp.where(hit, value, jnp.zeros_like(value))


def pull(value, start):
    moved = pltpu.roll(value, LANES - start, axis=1) if start else value
    return lanes_below(moved, LEV)


def wide(value):
    value = value + pltpu.roll(value, LEV, axis=1)
    return value + pltpu.roll(value, 2 * LEV, axis=1)


def folded(value, width):
    half = ROWS // 2
    return value[:half] + pltpu.roll(value[half:], width, axis=1)


def unfolded(value, start, width, limit):
    low = pltpu.roll(value, LANES - start, axis=1) if start else value
    high = pltpu.roll(value, LANES - start - width, axis=1)
    return jnp.concatenate([lanes_below(low, limit), lanes_below(high, limit)], axis=0)


def pack_messages(meta_ref, main_ref, rest_ref, send_ref, edges_ref, leaving):
    me = meta_ref[0]

    def picked(ref, k):
        return ref[k * ROWS : (k + 1) * ROWS, :]

    def add(d, start, count, value):
        span = slice(start, start + count)
        send_ref[d, span, :] = (send_ref[d, span, :].astype(F32) + value).astype(BF16)

    for block in range(BLOCKS):
        d, e = block // 2, block % 2
        k = slot(block)
        at = global_row(meta_ref, block) - me * LANES

        @pl.when((at >= -1) & (at <= LANES))
        def _():
            mine = (at >= 0) & (at < LANES)
            here = picked(rest_ref, BLOCKS + k)
            behind = picked(rest_ref, k)
            before = pull(behind, 2 * LEV)
            one = lanes_below(jnp.ones_like(here), LEV)
            north = jnp.where(mine, jnp.maximum(pull(here, 2 * LEV), 0.0), one)
            south = jnp.where(mine, jnp.minimum(before, 0.0), -one)
            main = wide(north) * picked(main_ref, 2 * BLOCKS + k) - wide(south) * picked(main_ref, k)
            rest = north * picked(rest_ref, 2 * BLOCKS + k) - south * behind
            send_ref[d, e * ROWS : (e + 1) * ROWS, :] = picked(main_ref, BLOCKS + k).astype(BF16)
            send_ref[d, (2 + e) * ROWS : (3 + e) * ROWS, :] = main.astype(BF16)
            tail = keep(here, 0) + pltpu.roll(rest, 2 * LEV, axis=1)
            add(d, 4 * ROWS, ROWS, pltpu.roll(tail, LEV, axis=1) if e else tail)
            add(d, 5 * ROWS, ROWS, pltpu.roll(keep(here, LEV, 2 * LEV), (1 if e else 3) * LEV, axis=1))
            add(d, 6 * ROWS, ROWS // 2, folded(pltpu.roll(before, LEV, axis=1) if e else before, 2 * LEV))

        if e:
            leaving[d].start()

    for at in range(2):
        k = 3 * BLOCKS + at
        edges_ref[at, :ROWS, :] = picked(main_ref, k).astype(BF16)
        rest = picked(rest_ref, k)
        rest = folded(keep(rest, 0), LEV) + folded(keep(rest, 2 * LEV), LEV)
        edges_ref[at, ROWS:, :] = rest.astype(BF16)


def clear(*refs):
    for ref in refs:
        ref[...] = jnp.zeros(ref.shape, ref.dtype)


def copies(source_ref, target_ref, sem_ref):
    return [
        pltpu.make_async_copy(source_ref.at[pl.ds(start, size)], target_ref.at[pl.ds(start, size)], sem_ref.at[n])
        for n, (start, size) in enumerate(SPANS)
    ]


class Scalars:
    def __init__(self, me, band_ref, row_ref):
        self.me, self.band_ref, self.row_ref = me, band_ref, row_ref

    def __getitem__(self, at):
        if at == 0:
            return self.me
        return self.band_ref[at - 2] if at < 2 + BLOCKS else self.row_ref[at - 2 - BLOCKS]


def pick_kernel(
    band_ref, row_ref, cells_hbm, winds_hbm, send_hbm, edges_ref, east_ref, west_ref,
    main_ref, rest_ref, cells_ref, winds_ref, send_ref, cells_sem, winds_sem, send_sem,
):
    meta_ref = Scalars(lax.axis_index("lat").astype(jnp.int32), band_ref, row_ref)
    arriving = list(zip(copies(cells_hbm, cells_ref, cells_sem), copies(winds_hbm, winds_ref, winds_sem)))
    for pair in arriving:
        for copy in pair:
            copy.start()
    clear_rims(main_ref, PICKS)
    clear_rims(rest_ref, PICKS)
    weights = pick_weights(meta_ref)
    clear(send_ref)
    blank = jnp.zeros((LEV, 2 * LANES), BF16)
    for (start, size), pair in zip(SPANS, arriving):
        for copy in pair:
            copy.wait()
        for y in range(start, start + size, 2):
            both = (y, min(y + 1, XS - 1))
            main = jnp.concatenate([cells_ref[z, :LANES, :] for z in both], axis=1)
            rest = jnp.concatenate([cells_ref[z, LANES:, :] for z in both], axis=1)
            wind = jnp.concatenate([winds_ref[z] for z in both], axis=1)
            rest = jnp.concatenate([rest, wind, blank], axis=0)
            main = jnp.dot(main, weights, preferred_element_type=F32).astype(BF16).T.astype(F32)
            rest = jnp.dot(rest, weights, preferred_element_type=F32).astype(BF16).T.astype(F32)
            for side in range(min(2, XS - y)):
                at = pl.ds(y + side + 1, PICKS, stride=ROWS)
                main_ref[at, :] = main[64 * side : 64 * side + PICKS]
                rest_ref[at, :] = rest[64 * side : 64 * side + PICKS]
    east_ref[:COLS, :] = cells_ref[XS - 1]
    east_ref[COLS:, :] = winds_ref[XS - 1, :LEV, :]
    west_ref[...] = cells_ref[0]
    leaving = [pltpu.make_async_copy(send_ref.at[d], send_hbm.at[d], send_sem.at[d]) for d in range(BANDS)]
    pack_messages(meta_ref, main_ref, rest_ref, send_ref, edges_ref, leaving)
    for copy in leaving:
        copy.wait()


STAGE = pltpu.VMEM((24 * ROWS, LANES), F32)
PICKED = pltpu.VMEM((PICKS * ROWS, LANES), F32)


def pick_rows(band, row, cells, winds):
    return pl.pallas_call(
        pick_kernel,
        out_shape=(
            shape((BANDS, WIRE, LANES), BF16),
            shape((2, HALO, LANES), BF16),
            shape((COLS + LEV, LANES), BF16),
            shape((COLS, LANES), BF16),
        ),
        in_specs=[SM, SM, HB, HB],
        out_specs=(HB, VM, VM, VM),
        scratch_shapes=[
            PICKED,
            PICKED,
            pltpu.VMEM((XS, COLS, LANES), BF16),
            pltpu.VMEM((XS, 2 * LEV, LANES), BF16),
            pltpu.VMEM((BANDS, WIRE, LANES), BF16),
            DMA((len(SPANS),)),
            DMA((len(SPANS),)),
            DMA((BANDS,)),
        ],
        compiler_params=params(58),
        name="pick",
    )(band, row, cells, winds)


def added(recv_ref, span):
    total = recv_ref[0, span, :].astype(F32)
    for s in range(1, BANDS):
        total = total + recv_ref[s, span, :].astype(F32)
    return total


def unpack_kernel(recv_ref, rows_ref):
    rows_ref[: 2 * ROWS, :] = added(recv_ref, slice(0, 2 * ROWS)).astype(BF16)
    tail = added(recv_ref, slice(4 * ROWS, 5 * ROWS))
    rows_ref[2 * ROWS :, :] = lanes_below(tail, 2 * LEV).astype(BF16)


def unpack_rows(recv):
    return pl.pallas_call(
        unpack_kernel,
        out_shape=shape((3 * ROWS, LANES), BF16),
        in_specs=[VM],
        out_specs=VM,
        compiler_params=params(8),
        name="unpack",
    )(recv)


def context_kernel(meta_ref, recv_ref, rows_ref, context_ref, to_east_ref, to_west_ref):
    me = meta_ref[0]
    winds = added(recv_ref, slice(5 * ROWS, 6 * ROWS))
    souths = unfolded(added(recv_ref, slice(6 * ROWS, WIRE)), 0, 2 * LEV, 2 * LEV)
    tails = None
    for e in range(2):
        band = meta_ref[2 + 2 * me + e]
        row = meta_ref[2 + BLOCKS + 2 * me + e]
        north = jnp.maximum(pull(winds, (2 * e + 1) * LEV), 0.0)
        south = jnp.minimum(pull(souths, e * LEV), 0.0)
        main = recv_ref[band, (2 + e) * ROWS : (3 + e) * ROWS, :].astype(F32)
        rest = pull(recv_ref[band, 4 * ROWS : 5 * ROWS, :].astype(F32), (2 + e) * LEV)
        for source, there, coef in (
            (jnp.minimum(band + 1, BANDS - 1), (row == LANES - 1) & (band < BANDS - 1), north),
            (jnp.maximum(band - 1, 0), (row == 0) & (band > 0), -south),
        ):
            share = jnp.where(there, coef, 0.0)
            main = main + wide(share) * recv_ref[source, (2 + e) * ROWS : (3 + e) * ROWS, :].astype(F32)
            rest = rest + share * pull(recv_ref[source, 4 * ROWS : 5 * ROWS, :].astype(F32), (2 + e) * LEV)
        context_ref[e] = main
        tails = rest if e == 0 else tails + pltpu.roll(rest, LEV, axis=1)
    context_ref[2] = tails
    context_ref[3] = winds
    context_ref[4] = souths
    clear(to_east_ref, to_west_ref)
    rims = [rows_ref[p * ROWS : (p + 1) * ROWS, :].astype(F32) for p in range(3)] + [winds]
    for at, tile in enumerate(rims):
        to_east_ref[at : at + 1, :] = tile[XS : XS + 1]
        to_west_ref[at : at + 1, :] = tile[1:2]


def unpack_context(meta, recv, rows):
    edge = shape((8, LANES), F32)
    return pl.pallas_call(
        context_kernel,
        out_shape=(shape((5, ROWS, LANES), F32), edge, edge),
        in_specs=[SM, VM, VM],
        out_specs=(VM,) * 3,
        compiler_params=params(8),
        name="context",
    )(meta, recv, rows)


def spread_blocks(rows_ref):
    first = rows_ref[:ROWS, :]
    second = rows_ref[ROWS : 2 * ROWS, :]
    rest = rows_ref[2 * ROWS :, :].astype(F32)
    lower = lanes_below(rest, LEV)
    upper = rest - lower
    blank = jnp.zeros_like(first)
    return jnp.concatenate(
        [
            jnp.concatenate([first, blank, lower.astype(BF16)], axis=1),
            jnp.concatenate([blank, second, upper.astype(BF16)], axis=1),
        ],
        axis=0,
    )


def product_kernel(*refs):
    out_ref = refs[-1]
    rows = [spread_blocks(ref) for ref in refs[:TEAM]]
    for q in range(2):
        span = slice(4 * ROWS * q, 4 * ROWS * (q + 1))
        made = None
        for ops_ref, values in zip(refs[TEAM : 2 * TEAM], rows):
            part = jnp.dot(ops_ref[span, :], values, preferred_element_type=F32)
            made = part if made is None else made + part
        for s in range(4):
            part = made[ROWS * s : ROWS * (s + 1)]
            t = 4 * q + s
            out_ref[t, :ROWS, :] = part[:, :LANES].astype(BF16)
            out_ref[t, ROWS : 2 * ROWS, :] = part[:, LANES : 2 * LANES].astype(BF16)
            out_ref[t, 2 * ROWS :, :] = folded(part[:, 2 * LANES :], 2 * LEV).astype(BF16)


def products(rows, ops):
    return pl.pallas_call(
        product_kernel,
        out_shape=shape((TARGETS, PACK, LANES), BF16),
        in_specs=[VM] * (2 * TEAM),
        out_specs=VM,
        compiler_params=params(6),
        name="product",
    )(*rows, *ops)


def total_kernel(meta_ref, recv_ref, edges_hbm, out_ref, edges_ref, sem_ref):
    arriving = pltpu.make_async_copy(edges_hbm, edges_ref, sem_ref.at[0])
    arriving.start()
    total = recv_ref[0].astype(F32)
    for s in range(1, TARGETS):
        total = total + recv_ref[s].astype(F32)
    total = total.astype(BF16)
    me = meta_ref[0]
    for d in range(BANDS):
        out_ref[d, :PACK, :] = total
    arriving.wait()
    for d in range(BANDS):
        edge = jnp.where(d == me + 1, edges_ref[1], jnp.zeros((HALO, LANES), BF16))
        out_ref[d, PACK:, :] = jnp.where(d == me - 1, edges_ref[0], edge)


def totals(meta, recv, edges):
    return pl.pallas_call(
        total_kernel,
        out_shape=shape((BANDS, PACK + HALO, LANES), BF16),
        in_specs=[SM, VM, HB],
        out_specs=VM,
        scratch_shapes=[pltpu.VMEM((2, HALO, LANES), BF16), DMA((1,))],
        compiler_params=params(4),
        name="total",
    )(meta, recv, edges)


def halo_rows(meta_ref, recv_ref):
    me = meta_ref[0]
    halos = []
    for near, there in ((me - 1, me > 0), (me + 1, me < BANDS - 1)):
        source = jnp.clip(near, 0, BANDS - 1)
        main = recv_ref[source, PACK : PACK + ROWS, :].astype(F32)
        rest = recv_ref[source, PACK + ROWS :, :].astype(F32)
        found = (main, unfolded(rest, 0, LEV, LEV), unfolded(rest, 2 * LEV, LEV, LEV))
        halos.append([jnp.where(there, value, 0.0) for value in found])
    return halos[0][:2], halos[1][:2], halos[0][2]


def stage_blocks(recv_ref, main_ref, rest_ref):
    half = ROWS // 2
    for source in range(BANDS):
        packed = recv_ref[source, 2 * ROWS : PACK, :].astype(F32)
        for b in range(2):
            at = (b * BANDS + source) * ROWS
            main_ref[at : at + ROWS, :] = recv_ref[source, b * ROWS : (b + 1) * ROWS, :].astype(F32)
            rest_ref[at : at + half, :] = pull(packed, b * LEV)
            rest_ref[at + half : at + ROWS, :] = pull(packed, (2 + b) * LEV)


def block_sum(meta_ref, row, main_ref, rest_ref):
    main = jnp.zeros((ROWS, LANES), F32)
    rest = jnp.zeros((ROWS, LANES), F32)
    for block in range(BLOCKS):
        share = jnp.where(global_row(meta_ref, block) == row, 1.0, 0.0)
        k = slot(block) * ROWS
        main = main + share * main_ref[k : k + ROWS, :]
        rest = rest + share * rest_ref[k : k + ROWS, :]
    return main, rest


KEPT = 32
GROUP = LANES // KEPT
TALL = COLS + LEV


def stage_corrections(meta_ref, recv_ref, wind_recv_ref, main_ref, rest_ref, tall_ref):
    clear(main_ref, rest_ref)
    me = meta_ref[0]
    halos = halo_rows(meta_ref, recv_ref)
    sums = [list(halos[0]), list(halos[1])]
    for source in range(BANDS):
        packed = recv_ref[source, 2 * ROWS : PACK, :].astype(F32)
        for b in range(2):
            k = b * BANDS + source
            main = recv_ref[source, b * ROWS : (b + 1) * ROWS, :].astype(F32)
            rest = unfolded(packed, b * LEV, 2 * LEV, LEV)
            main_ref[pl.ds(k, ROWS, stride=KEPT), :] = main
            rest_ref[pl.ds(k, ROWS, stride=KEPT), :] = rest
            for at, row in enumerate((me * LANES - 1, (me + 1) * LANES)):
                share = jnp.where(global_row(meta_ref, 2 * source + b) == row, 1.0, 0.0)
                sums[at][0] = sums[at][0] + share * main
                sums[at][1] = sums[at][1] + share * rest
    for at in range(2):
        main_ref[pl.ds(16 + at, ROWS, stride=KEPT), :] = sums[at][0].astype(BF16).astype(F32)
        rest_ref[pl.ds(16 + at, ROWS, stride=KEPT), :] = sums[at][1].astype(BF16).astype(F32)
    wind = halo_rows(meta_ref, wind_recv_ref)[2]
    rest_ref[pl.ds(18, ROWS, stride=KEPT), :] = pltpu.roll(wind, LEV, axis=1)
    for t in range(ROWS // GROUP):
        span = slice(t * LANES, (t + 1) * LANES)
        tall_ref[t * TALL : t * TALL + LANES, :] = main_ref[span, :].T.astype(BF16)
        tall_ref[t * TALL + LANES : (t + 1) * TALL, :] = rest_ref[span, :].T[: 2 * LEV].astype(BF16)


def rows_kernel(meta_ref, before_ref, context_ref, west_ref, east_ref, recv_ref, out_ref, main_ref, rest_ref):
    stage_blocks(recv_ref, main_ref, rest_ref)
    me = meta_ref[0]
    sub = lax.broadcasted_iota(jnp.int32, (ROWS, LANES), 0)
    inner = (sub >= 1) & (sub <= XS)

    def rimmed(value, at):
        value = jnp.where(sub == 0, west_ref[at : at + 1, :], value)
        return jnp.where(sub == XS + 1, east_ref[at : at + 1, :], value)

    def known(p):
        return rimmed(before_ref[p * ROWS : (p + 1) * ROWS, :].astype(F32), p)

    last = None
    tail = known(2)
    winds = rimmed(context_ref[3], 3)
    for e in range(2):
        row = global_row(meta_ref, 2 * me + e)
        across = pull(winds, 2 * e * LEV)
        east = jnp.maximum(across, 0.0)
        west = jnp.minimum(pltpu.roll(across, 1, axis=0), 0.0)
        north = jnp.where(row == BANDS * LANES - 1, 0.0, jnp.maximum(pull(winds, (2 * e + 1) * LEV), 0.0))
        south = jnp.minimum(pull(context_ref[4], e * LEV), 0.0)
        coefs = (east, west, north, south)
        added = [block_sum(meta_ref, row + near, main_ref, rest_ref) for near in (-1, 0, 1)]

        def moved(coefs, here, aside, behind, ahead):
            east, west, north, south = coefs
            here = here.astype(BF16).astype(F32)
            centre = 1.0 - east + west - north + south
            made = (
                centre * here
                + (east * pltpu.roll(here, ROWS - 1, axis=0) - west * pltpu.roll(here, 1, axis=0))
                + (aside + (north * ahead - south * behind))
            )
            return jnp.where(inner, made, 0.0)

        main = moved([wide(c) for c in coefs], known(e) + added[1][0], context_ref[e], added[0][0], added[2][0])
        out_ref[e * ROWS : (e + 1) * ROWS, :] = main.astype(BF16)
        rest = pull(tail, e * LEV) + added[1][1]
        rest = moved(coefs, rest, pull(context_ref[2], e * LEV), added[0][1], added[2][1])
        rest = lanes_below(rest, LEV)
        last = rest if e == 0 else last + pltpu.roll(rest, LEV, axis=1)
    out_ref[2 * ROWS :, :] = last.astype(BF16)


def next_rows(*args):
    return pl.pallas_call(
        rows_kernel,
        out_shape=shape((3 * ROWS, LANES), BF16),
        in_specs=[SM] + [VM] * 5,
        out_specs=VM,
        scratch_shapes=[STAGE, STAGE],
        compiler_params=params(4),
        name="rows",
    )(*args)


def place_weights(meta_ref, q):
    sub, lane = iotas((LANES, 2 * LANES))
    kept = sub - q * KEPT
    target = jnp.full(sub.shape, -1, jnp.int32)
    for block in range(BLOCKS):
        at = global_row(meta_ref, block) - meta_ref[0] * LANES
        target = jnp.where(kept == slot(block), jnp.where((at >= 0) & (at < LANES), at, -1), target)
    target = jnp.where((kept == 16) | (kept == 18), LANES, target)
    target = jnp.where(kept == 17, 2 * LANES - 1, target)
    return jnp.where(lane == target, 1.0, 0.0).astype(BF16)


def advance(
    meta_ref, cells_ref, winds_ref, west_ref, east_ref, wind_west_ref, tall_ref, placed_ref, smooth_ref, emit, leaving,
    rounded,
):
    for q in range(GROUP):
        placed_ref[q] = jnp.dot(tall_ref[...], place_weights(meta_ref, q), preferred_element_type=F32)
    top = meta_ref[0] == BANDS - 1

    def smooth(r, base):
        at = (r // GROUP) * TALL
        value = base.astype(F32) + placed_ref[r % GROUP, pl.ds(at, COLS), :LANES]
        if rounded:
            value = value.astype(BF16).astype(F32)
        smooth_ref[r] = value
        return value

    def step(x, ahead):
        ahead = smooth(x + 2, ahead)
        emit(x, stencil(x, top, winds_ref, wind_west_ref, smooth_ref, ahead, placed_ref))

    def body(x, carry):
        step(x, cells_ref[x + 1])
        return carry

    smooth(0, west_ref[:COLS, :])
    smooth(1, cells_ref[0])
    for (start, size), copy in zip(SPANS, leaving):
        for x in range(start, min(start + size, XS - 1)):
            body(x, 0)
        if start + size == XS:
            step(XS - 1, east_ref[...])
        copy.start()


def stencil(x, top, winds_ref, west_ref, smooth_ref, ahead, placed_ref):
    at = ((x + 1) // GROUP) * TALL
    q = (x + 1) % GROUP
    lane = lax.broadcasted_iota(jnp.int32, (LEV, LANES), 1)
    courant = winds_ref[x].astype(F32)
    before = winds_ref[jnp.maximum(x - 1, 0), :LEV, :].astype(F32)
    before = jnp.where(x == 0, west_ref[COLS:, :].astype(F32), before)
    across = courant[:LEV]
    along = jnp.where(top & (lane == LANES - 1), 0.0, courant[LEV:])
    south_along = jnp.where(lane == 0, placed_ref[q, pl.ds(at + COLS, LEV), LANES:], pltpu.roll(along, 1, axis=1))
    east = jnp.maximum(across, 0.0)
    west = jnp.minimum(before, 0.0)
    north = jnp.maximum(along, 0.0)
    south = jnp.minimum(south_along, 0.0)
    centre = 1.0 - east + west - north + south
    made = []
    for v in range(VAR):
        span = slice(v * LEV, (v + 1) * LEV)
        here = smooth_ref[x + 1, span, :]
        edge = placed_ref[q, pl.ds(at + v * LEV, LEV), LANES:]
        above = jnp.where(lane == LANES - 1, edge, pltpu.roll(here, LANES - 1, axis=1))
        below = jnp.where(lane == 0, edge, pltpu.roll(here, 1, axis=1))
        made.append(
            centre * here
            + (east * ahead[span] - west * smooth_ref[x, span, :])
            + (north * above - south * below)
        )
    return made


SCRATCH = [
    pltpu.VMEM((KEPT * ROWS, LANES), F32),
    pltpu.VMEM((KEPT * ROWS, LANES), F32),
    pltpu.VMEM((ROWS // GROUP * TALL, LANES), BF16),
    pltpu.VMEM((GROUP, ROWS // GROUP * TALL, 2 * LANES), F32),
    pltpu.VMEM((XS + 2, COLS, LANES), F32),
]


def first_kernel(
    meta_ref, cells_hbm, winds_hbm, west_ref, east_ref, recv_ref,
    out_hbm, edges_ref, to_east_hbm, to_west_hbm,
    main_ref, rest_ref, tall_ref, placed_ref, smooth_ref, out_ref, out_sem, rim_sem,
    cells_ref, cells_sem, winds_ref, winds_sem,
):
    arriving = copies(cells_hbm, cells_ref, cells_sem) + copies(winds_hbm, winds_ref, winds_sem)
    for copy in arriving:
        copy.start()
    stage_corrections(meta_ref, recv_ref, recv_ref, main_ref, rest_ref, tall_ref)
    for copy in arriving:
        copy.wait()

    def emit(x, made):
        for v in range(VAR):
            out_ref[x, v * LEV : (v + 1) * LEV, :] = made[v].astype(BF16)

    leaving = copies(out_ref, out_hbm, out_sem)
    advance(
        meta_ref, cells_ref, winds_ref, west_ref, east_ref, west_ref, tall_ref, placed_ref, smooth_ref, emit, leaving,
        True,
    )
    rims = [
        pltpu.make_async_copy(out_ref.at[0], to_west_hbm, rim_sem.at[0]),
        pltpu.make_async_copy(out_ref.at[XS - 1], to_east_hbm, rim_sem.at[1]),
    ]
    for copy in rims:
        copy.start()
    sub, lane = iotas((LANES, LANES))
    halves = [(sub == 0) & (lane == 2 * side) | (sub == LANES - 1) & (lane == 2 * side + 1) for side in range(2)]
    ends = jnp.concatenate([jnp.where(hit, 1.0, 0.0) for hit in halves], axis=0).astype(BF16)
    total = None
    for x in range(0, XS, 2):
        pair = jnp.concatenate([out_ref[min(x + side, XS - 1)] for side in range(2)], axis=1)
        found = jnp.dot(pair, ends, preferred_element_type=F32)
        if x == XS - 1:
            found = jnp.where(lax.broadcasted_iota(jnp.int32, found.shape, 1) < 2, found, 0.0)
        found = pltpu.roll(found, 2 * x + 2, axis=1)
        total = found if total is None else total + found
    main_ref[:LANES, :] = total[:LANES].T
    rest = jnp.concatenate([total[LANES:], jnp.zeros((LANES - LEV, LANES), F32)], axis=0)
    rest_ref[:LANES, :] = rest.T
    for at in range(2):
        edges_ref[at, :ROWS, :] = main_ref[pl.ds(at, ROWS, stride=2), :].astype(BF16)
        edges_ref[at, ROWS:, :] = folded(rest_ref[pl.ds(at, ROWS, stride=2), :], LEV).astype(BF16)
    for copy in leaving + rims:
        copy.wait()


def first_substep(*args):
    return pl.pallas_call(
        first_kernel,
        out_shape=(
            shape((XS, COLS, LANES), BF16),
            shape((2, HALO, LANES), BF16),
            shape((COLS, LANES), BF16),
            shape((COLS, LANES), BF16),
        ),
        in_specs=[SM, HB, HB] + [VM] * 3,
        out_specs=(HB, VM, HB, HB),
        scratch_shapes=SCRATCH
        + [
            pltpu.VMEM((XS, COLS, LANES), BF16),
            DMA((len(SPANS),)),
            DMA((2,)),
            pltpu.VMEM((XS, COLS, LANES), BF16),
            DMA((len(SPANS),)),
            pltpu.VMEM((XS, 2 * LEV, LANES), BF16),
            DMA((len(SPANS),)),
        ],
        compiler_params=params(58),
        name="first",
    )(*args)


def last_kernel(
    meta_ref, cells_ref, winds_ref, west_ref, east_ref, recv_ref, wind_recv_ref, wind_west_ref,
    out_hbm, main_ref, rest_ref, tall_ref, placed_ref, smooth_ref, out_ref, out_sem,
):
    stage_corrections(meta_ref, recv_ref, wind_recv_ref, main_ref, rest_ref, tall_ref)

    def emit(x, made):
        for v in range(VAR):
            out_ref[x, v * LEV : (v + 1) * LEV, :] = made[v]

    leaving = copies(out_ref, out_hbm, out_sem)
    advance(
        meta_ref, cells_ref, winds_ref, west_ref, east_ref, wind_west_ref, tall_ref, placed_ref, smooth_ref, emit,
        leaving, False,
    )
    for copy in leaving:
        copy.wait()


def last_substep(*args):
    return pl.pallas_call(
        last_kernel,
        out_shape=shape((XS, COLS, LANES), F32),
        in_specs=[SM] + [VM] * 7,
        out_specs=HB,
        scratch_shapes=SCRATCH + [pltpu.VMEM((XS, COLS, LANES), F32), DMA((len(SPANS),))],
        compiler_params=params(30),
        name="last",
    )(*args)


def stay_kernel(cells_hbm, message_hbm, cells_ref, sem_ref):
    arriving = copies(cells_hbm, cells_ref, sem_ref)
    for copy in arriving:
        copy.start()
    for copy in arriving:
        copy.wait()


def bring_back(cells, message):
    return pl.pallas_call(
        stay_kernel,
        out_shape=shape((XS, COLS, LANES), BF16),
        in_specs=[HB, HB],
        out_specs=VM,
        scratch_shapes=[DMA((len(SPANS),))],
        compiler_params=params(4),
        name="stay",
    )(cells, message)


TEAMMATES = [[(i, i ^ (16 * (other // 2) + other % 2)) for i in range(LON_DEV)] for other in range(1, TEAM)]
EASTWARD = [(i, (i + 1) % LON_DEV) for i in range(LON_DEV)]
WESTWARD = [(i, (i - 1) % LON_DEV) for i in range(LON_DEV)]
ALONG_Z = [[16 * (place // 2) + 2 * t + place % 2 for t in range(TARGETS)] for place in range(TEAM)]


def by_lat(messages):
    return lax.all_to_all(messages, "lat", 0, 0, tiled=True)


def filtered(rows, ops):
    team = [rows] + [lax.ppermute(rows, "lon", mates) for mates in TEAMMATES]
    partial = products(team, ops)
    return lax.all_to_all(partial, "lon", 0, 0, tiled=True, axis_index_groups=ALONG_Z)


def shards(cotangent, winds, filter_ops, block_band, block_row):
    me = lax.axis_index("lat").astype(jnp.int32).reshape(1)
    at = lax.axis_index("lon").astype(jnp.int32)
    place = ((at >> 4) * 2 + (at & 1)).reshape(1)
    meta = jnp.concatenate([me, place, block_band, block_row])
    made = prepare_operators(meta, jnp.pad(filter_ops, ((0, 0), (1, 2), (0, 0))))
    ops = [made[0]] + [lax.ppermute(part, "lon", mates) for part, mates in zip(made[1:], TEAMMATES)]
    send, edges, to_east, to_west = pick_rows(block_band, block_row, cotangent, winds)
    west = lax.ppermute(to_east, "lon", EASTWARD)
    east = lax.ppermute(to_west, "lon", WESTWARD)
    recv, west, east = lax.optimization_barrier((by_lat(send), west, east))
    rows = unpack_rows(recv)
    swapped = filtered(rows, ops)
    context, row_east, row_west = unpack_context(meta, recv, rows)
    row_from_west = lax.ppermute(row_east, "lon", EASTWARD)
    row_from_east = lax.ppermute(row_west, "lon", WESTWARD)
    swapped, row_from_west, row_from_east = lax.optimization_barrier((swapped, row_from_west, row_from_east))
    given = by_lat(totals(meta, swapped, edges))
    rows = next_rows(meta, rows, context, row_from_west, row_from_east, given)
    swapped = filtered(rows, ops)
    state, edges, to_east, to_west = first_substep(meta, cotangent, winds, west, east, given)
    west2 = lax.ppermute(to_east, "lon", EASTWARD)
    east2 = lax.ppermute(to_west, "lon", WESTWARD)
    message = totals(meta, swapped, edges)
    given2 = by_lat(message)
    return last_substep(meta, bring_back(state, message), winds, west2, east2, given2, given, west)


def solution(mesh):
    return jax.shard_map(
        shards,
        mesh=mesh,
        in_specs=(P("lon", None, "lat"), P("lon", None, "lat"), P("lat", "lon", None), P(), P()),
        out_specs=P("lon", None, "lat"),
        check_vma=False,
    )
```

```python
import jax
import jax.numpy as jnp
from jax import lax
from jax.experimental import pallas as pl
from jax.experimental.pallas import tpu as pltpu
from jax.sharding import PartitionSpec as P

VAR = 5
LEV = 32
COLS = VAR * LEV
XS = 45
ROWS = 48
LANES = 128
BANDS = 8
NLON = 1440
LON_DEV = 32
TARGETS = 8
TEAM = 4
BLOCKS = 16
PICKS = 56
WIRE = 6 * ROWS + 24
PACK = 120
HALO = 72
CHUNK = 9

F32 = jnp.float32
BF16 = jnp.bfloat16
VM = pl.BlockSpec(memory_space=pltpu.VMEM)
SM = pl.BlockSpec(memory_space=pltpu.SMEM)
HB = pl.BlockSpec(memory_space=pl.ANY)
DMA = pltpu.SemaphoreType.DMA
SPANS = [(start, min(8, XS - start)) for start in range(0, XS, 8)]


def shape(dims, kind):
    return jax.ShapeDtypeStruct(dims, kind)


def params(mib):
    return pltpu.CompilerParams(vmem_limit_bytes=mib * 2**20)


def iotas(dims):
    return (
        lax.broadcasted_iota(jnp.int32, dims, 0),
        lax.broadcasted_iota(jnp.int32, dims, 1),
    )


def lanes_below(value, limit):
    lane = lax.broadcasted_iota(jnp.int32, value.shape, 1)
    return jnp.where(lane < limit, value, jnp.zeros_like(value))


def dot_nt(a, b):
    return lax.dot_general(a, b, (((1,), (1,)), ((), ())), preferred_element_type=F32)


def dot_tn(a, b):
    return lax.dot_general(a, b, (((0,), (0,)), ((), ())), preferred_element_type=F32)


def operator_kernel(meta_ref, ops_ref, *out_refs):
    place = meta_ref[1]
    for t in range(TARGETS):
        tiles = []
        for member in range(TEAM):
            start = XS * ((member // 2) * 2 * TARGETS + 2 * t + member % 2) - 1
            total = None
            first = max(start, 0) // LANES * LANES
            spans = [(first, min(first + 2 * LANES, NLON))]
            if start < 0:
                spans.append(((NLON - 1) // LANES * LANES, NLON))
            if start + XS + 2 > NLON:
                spans.append((0, LANES))
            for low, high in spans:
                row, lane = iotas((ROWS, high - low))
                wanted = start + row
                wanted = jnp.where(wanted < 0, wanted + NLON, wanted)
                wanted = jnp.where(wanted >= NLON, wanted - NLON, wanted)
                hit = (lane + low == wanted) & (row < XS + 2)
                pick = jnp.where(hit, 1.0, 0.0).astype(BF16)
                window = ops_ref[:, :, low:high].reshape(2 * ROWS, high - low)
                part = dot_nt(pick, window)
                total = part if total is None else total + part
            tiles.append(total)
        rows = slice(ROWS * t, ROWS * (t + 1))
        for other in range(TEAM):
            value = tiles[other]
            for member in range(1, TEAM):
                value = jnp.where(place == member, tiles[member ^ other], value)
            out_refs[other][rows, :] = value.astype(BF16)


def prepare_operators(meta, ops):
    out = shape((TARGETS * ROWS, 2 * ROWS), BF16)
    return pl.pallas_call(
        operator_kernel,
        out_shape=(out,) * TEAM,
        in_specs=[SM, VM],
        out_specs=(VM,) * TEAM,
        compiler_params=params(6),
        name="operators",
    )(meta, ops)


def slot(block):
    return (block % 2) * BANDS + block // 2


def global_row(meta_ref, block):
    return meta_ref[2 + block] * LANES + meta_ref[2 + BLOCKS + block]


def clear_rims(ref, count):
    blank = jnp.zeros((count, LANES), ref.dtype)
    for r in (0, XS + 1, XS + 2):
        ref[pl.ds(r, count, stride=ROWS), :] = blank


def pick_weights(meta_ref):
    me = meta_ref[0]
    lane = lax.broadcasted_iota(jnp.int32, (8, LANES), 1)
    pick = lane & 63
    target = jnp.full(lane.shape, -1, jnp.int32)
    for block in range(BLOCKS):
        at = global_row(meta_ref, block) - me * LANES
        for near in range(3):
            target = jnp.where(pick == near * BLOCKS + slot(block), at + (near - 1), target)
    target = jnp.where(pick == 3 * BLOCKS, 0, target)
    target = jnp.where(pick == 3 * BLOCKS + 1, LANES - 1, target)
    sub, lane = iotas((LANES, LANES))
    hit = sub == jnp.broadcast_to(target[:1], (LANES, LANES))
    halves = [jnp.where(hit & ((lane < 64) == side), 1.0, 0.0) for side in (True, False)]
    return jnp.concatenate(halves, axis=0).astype(BF16)


def keep(value, *starts):
    lane = lax.broadcasted_iota(jnp.int32, value.shape, 1)
    hit = (lane >= starts[0]) & (lane < starts[0] + LEV)
    for start in starts[1:]:
        hit = hit | ((lane >= start) & (lane < start + LEV))
    return jnp.where(hit, value, jnp.zeros_like(value))


def pull(value, start):
    moved = pltpu.roll(value, LANES - start, axis=1) if start else value
    return lanes_below(moved, LEV)


def wide(value):
    value = value + pltpu.roll(value, LEV, axis=1)
    return value + pltpu.roll(value, 2 * LEV, axis=1)


def folded(value, width):
    half = ROWS // 2
    return value[:half] + pltpu.roll(value[half:], width, axis=1)


def unfolded(value, start, width, limit):
    low = pltpu.roll(value, LANES - start, axis=1) if start else value
    high = pltpu.roll(value, LANES - start - width, axis=1)
    return jnp.concatenate([lanes_below(low, limit), lanes_below(high, limit)], axis=0)


def pack_messages(meta_ref, main_ref, rest_ref, send_ref, edges_ref, leaving):
    me = meta_ref[0]

    def picked(ref, k):
        return ref[k * ROWS : (k + 1) * ROWS, :]

    def add(d, start, count, value):
        span = slice(start, start + count)
        send_ref[d, span, :] = (send_ref[d, span, :].astype(F32) + value).astype(BF16)

    for block in range(BLOCKS):
        d, e = block // 2, block % 2
        k = slot(block)
        at = global_row(meta_ref, block) - me * LANES

        @pl.when((at >= -1) & (at <= LANES))
        def _():
            mine = (at >= 0) & (at < LANES)
            here = picked(rest_ref, BLOCKS + k)
            behind = picked(rest_ref, k)
            before = pull(behind, 2 * LEV)
            one = lanes_below(jnp.ones_like(here), LEV)
            north = jnp.where(mine, jnp.maximum(pull(here, 2 * LEV), 0.0), one)
            south = jnp.where(mine, jnp.minimum(before, 0.0), -one)
            main = wide(north) * picked(main_ref, 2 * BLOCKS + k) - wide(south) * picked(main_ref, k)
            rest = north * picked(rest_ref, 2 * BLOCKS + k) - south * behind
            send_ref[d, e * ROWS : (e + 1) * ROWS, :] = picked(main_ref, BLOCKS + k).astype(BF16)
            send_ref[d, (2 + e) * ROWS : (3 + e) * ROWS, :] = main.astype(BF16)
            tail = keep(here, 0) + pltpu.roll(rest, 2 * LEV, axis=1)
            add(d, 4 * ROWS, ROWS, pltpu.roll(tail, LEV, axis=1) if e else tail)
            add(d, 5 * ROWS, ROWS, pltpu.roll(keep(here, LEV, 2 * LEV), (1 if e else 3) * LEV, axis=1))
            add(d, 6 * ROWS, ROWS // 2, folded(pltpu.roll(before, LEV, axis=1) if e else before, 2 * LEV))

        if e:
            leaving[d].start()

    for at in range(2):
        k = 3 * BLOCKS + at
        edges_ref[at][:ROWS, :] = picked(main_ref, k).astype(BF16)
        rest = picked(rest_ref, k)
        rest = folded(keep(rest, 0), LEV) + folded(keep(rest, 2 * LEV), LEV)
        edges_ref[at][ROWS:, :] = rest.astype(BF16)


def clear(*refs):
    for ref in refs:
        ref[...] = jnp.zeros(ref.shape, ref.dtype)


def copies(source_ref, target_ref, sem_ref):
    return [
        pltpu.make_async_copy(source_ref.at[pl.ds(start, size)], target_ref.at[pl.ds(start, size)], sem_ref.at[n])
        for n, (start, size) in enumerate(SPANS)
    ]


class Scalars:
    def __init__(self, me, band_ref, row_ref):
        self.me, self.band_ref, self.row_ref = me, band_ref, row_ref

    def __getitem__(self, at):
        if at == 0:
            return self.me
        return self.band_ref[at - 2] if at < 2 + BLOCKS else self.row_ref[at - 2 - BLOCKS]


def pick_kernel(
    band_ref, row_ref, cells_hbm, winds_hbm, send_hbm, south_ref, north_ref, east_ref, west_ref,
    main_ref, rest_ref, cells_ref, winds_ref, send_ref, cells_sem, winds_sem, send_sem,
):
    meta_ref = Scalars(lax.axis_index("lat").astype(jnp.int32), band_ref, row_ref)
    arriving = list(zip(copies(cells_hbm, cells_ref, cells_sem), copies(winds_hbm, winds_ref, winds_sem)))
    for pair in arriving:
        for copy in pair:
            copy.start()
    clear_rims(main_ref, PICKS)
    clear_rims(rest_ref, PICKS)
    weights = pick_weights(meta_ref)
    clear(send_ref)
    blank = jnp.zeros((LEV, 2 * LANES), BF16)
    for (start, size), pair in zip(SPANS, arriving):
        for copy in pair:
            copy.wait()
        for y in range(start, start + size, 2):
            both = (y, min(y + 1, XS - 1))
            main = jnp.concatenate([cells_ref[z, :LANES, :] for z in both], axis=1)
            rest = jnp.concatenate([cells_ref[z, LANES:, :] for z in both], axis=1)
            wind = jnp.concatenate([winds_ref[z] for z in both], axis=1)
            rest = jnp.concatenate([rest, wind, blank], axis=0)
            main = jnp.dot(main, weights, preferred_element_type=F32).astype(BF16).T.astype(F32)
            rest = jnp.dot(rest, weights, preferred_element_type=F32).astype(BF16).T.astype(F32)
            for side in range(min(2, XS - y)):
                at = pl.ds(y + side + 1, PICKS, stride=ROWS)
                main_ref[at, :] = main[64 * side : 64 * side + PICKS]
                rest_ref[at, :] = rest[64 * side : 64 * side + PICKS]
    east_ref[:COLS, :] = cells_ref[XS - 1]
    east_ref[COLS:, :] = winds_ref[XS - 1, :LEV, :]
    west_ref[...] = cells_ref[0]
    leaving = [pltpu.make_async_copy(send_ref.at[d], send_hbm.at[d], send_sem.at[d]) for d in range(BANDS)]
    pack_messages(meta_ref, main_ref, rest_ref, send_ref, (south_ref, north_ref), leaving)
    for copy in leaving:
        copy.wait()


STAGE = pltpu.VMEM((24 * ROWS, LANES), F32)
PICKED = pltpu.VMEM((PICKS * ROWS, LANES), F32)


def pick_rows(band, row, cells, winds):
    return pl.pallas_call(
        pick_kernel,
        out_shape=(
            shape((BANDS, WIRE, LANES), BF16),
            shape((HALO, LANES), BF16),
            shape((HALO, LANES), BF16),
            shape((COLS + LEV, LANES), BF16),
            shape((COLS, LANES), BF16),
        ),
        in_specs=[SM, SM, HB, HB],
        out_specs=(HB, VM, VM, VM, VM),
        scratch_shapes=[
            PICKED,
            PICKED,
            pltpu.VMEM((XS, COLS, LANES), BF16),
            pltpu.VMEM((XS, 2 * LEV, LANES), BF16),
            pltpu.VMEM((BANDS, WIRE, LANES), BF16),
            DMA((len(SPANS),)),
            DMA((len(SPANS),)),
            DMA((BANDS,)),
        ],
        compiler_params=params(58),
        name="pick",
    )(band, row, cells, winds)


def added(recv_ref, span):
    total = recv_ref[0, span, :].astype(F32)
    for s in range(1, BANDS):
        total = total + recv_ref[s, span, :].astype(F32)
    return total


def unpack_kernel(recv_ref, rows_ref):
    rows_ref[: 2 * ROWS, :] = added(recv_ref, slice(0, 2 * ROWS)).astype(BF16)
    tail = added(recv_ref, slice(4 * ROWS, 5 * ROWS))
    rows_ref[2 * ROWS :, :] = lanes_below(tail, 2 * LEV).astype(BF16)


def unpack_rows(recv):
    return pl.pallas_call(
        unpack_kernel,
        out_shape=shape((3 * ROWS, LANES), BF16),
        in_specs=[VM],
        out_specs=VM,
        compiler_params=params(8),
        name="unpack",
    )(recv)


def context_kernel(meta_ref, recv_ref, rows_ref, context_ref, to_east_ref, to_west_ref):
    me = meta_ref[0]
    winds = added(recv_ref, slice(5 * ROWS, 6 * ROWS))
    souths = unfolded(added(recv_ref, slice(6 * ROWS, WIRE)), 0, 2 * LEV, 2 * LEV)
    tails = None
    for e in range(2):
        band = meta_ref[2 + 2 * me + e]
        row = meta_ref[2 + BLOCKS + 2 * me + e]
        north = jnp.maximum(pull(winds, (2 * e + 1) * LEV), 0.0)
        south = jnp.minimum(pull(souths, e * LEV), 0.0)
        main = recv_ref[band, (2 + e) * ROWS : (3 + e) * ROWS, :].astype(F32)
        rest = pull(recv_ref[band, 4 * ROWS : 5 * ROWS, :].astype(F32), (2 + e) * LEV)
        for source, there, coef in (
            (jnp.minimum(band + 1, BANDS - 1), (row == LANES - 1) & (band < BANDS - 1), north),
            (jnp.maximum(band - 1, 0), (row == 0) & (band > 0), -south),
        ):
            share = jnp.where(there, coef, 0.0)
            main = main + wide(share) * recv_ref[source, (2 + e) * ROWS : (3 + e) * ROWS, :].astype(F32)
            rest = rest + share * pull(recv_ref[source, 4 * ROWS : 5 * ROWS, :].astype(F32), (2 + e) * LEV)
        context_ref[e] = main
        tails = rest if e == 0 else tails + pltpu.roll(rest, LEV, axis=1)
    context_ref[2] = tails
    context_ref[3] = winds
    context_ref[4] = souths
    clear(to_east_ref, to_west_ref)
    rims = [rows_ref[p * ROWS : (p + 1) * ROWS, :].astype(F32) for p in range(3)] + [winds]
    for at, tile in enumerate(rims):
        to_east_ref[at : at + 1, :] = tile[XS : XS + 1]
        to_west_ref[at : at + 1, :] = tile[1:2]


def unpack_context(meta, recv, rows):
    edge = shape((8, LANES), F32)
    return pl.pallas_call(
        context_kernel,
        out_shape=(shape((5, ROWS, LANES), F32), edge, edge),
        in_specs=[SM, VM, VM],
        out_specs=(VM,) * 3,
        compiler_params=params(8),
        name="context",
    )(meta, recv, rows)


def spread_blocks(rows_ref):
    first = rows_ref[:ROWS, :]
    second = rows_ref[ROWS : 2 * ROWS, :]
    rest = rows_ref[2 * ROWS :, :].astype(F32)
    lower = lanes_below(rest, LEV)
    upper = rest - lower
    blank = jnp.zeros_like(first)
    return jnp.concatenate(
        [
            jnp.concatenate([first, blank, lower.astype(BF16)], axis=1),
            jnp.concatenate([blank, second, upper.astype(BF16)], axis=1),
        ],
        axis=0,
    )


def product_kernel(*refs):
    out_ref = refs[-1]
    rows = [spread_blocks(ref) for ref in refs[:TEAM]]
    for q in range(2):
        span = slice(4 * ROWS * q, 4 * ROWS * (q + 1))
        made = None
        for ops_ref, values in zip(refs[TEAM : 2 * TEAM], rows):
            part = jnp.dot(ops_ref[span, :], values, preferred_element_type=F32)
            made = part if made is None else made + part
        for s in range(4):
            part = made[ROWS * s : ROWS * (s + 1)]
            t = 4 * q + s
            out_ref[t, :ROWS, :] = part[:, :LANES].astype(BF16)
            out_ref[t, ROWS : 2 * ROWS, :] = part[:, LANES : 2 * LANES].astype(BF16)
            out_ref[t, 2 * ROWS :, :] = folded(part[:, 2 * LANES :], 2 * LEV).astype(BF16)


def products(rows, ops):
    return pl.pallas_call(
        product_kernel,
        out_shape=shape((TARGETS, PACK, LANES), BF16),
        in_specs=[VM] * (2 * TEAM),
        out_specs=VM,
        compiler_params=params(6),
        name="product",
    )(*rows, *ops)


def total_kernel(recv_ref, out_ref):
    total = recv_ref[0].astype(F32)
    for s in range(1, TARGETS):
        total = total + recv_ref[s].astype(F32)
    total = total.astype(BF16)
    for d in range(BANDS):
        out_ref[d] = total


def totals(recv):
    return pl.pallas_call(
        total_kernel,
        out_shape=shape((BANDS, PACK, LANES), BF16),
        in_specs=[VM],
        out_specs=VM,
        compiler_params=params(4),
        name="total",
    )(recv)


def total_with_edges_kernel(meta_ref, recv_ref, edges_hbm, out_ref, edges_ref, sem_ref):
    arriving = pltpu.make_async_copy(edges_hbm, edges_ref, sem_ref.at[0])
    arriving.start()
    total = recv_ref[0].astype(F32)
    for s in range(1, TARGETS):
        total = total + recv_ref[s].astype(F32)
    total = total.astype(BF16)
    me = meta_ref[0]
    for d in range(BANDS):
        out_ref[d, :PACK, :] = total
    arriving.wait()
    for d in range(BANDS):
        edge = jnp.where(d == me + 1, edges_ref[1], jnp.zeros((HALO, LANES), BF16))
        out_ref[d, PACK:, :] = jnp.where(d == me - 1, edges_ref[0], edge)


def totals_with_edges(meta, recv, edges):
    return pl.pallas_call(
        total_with_edges_kernel,
        out_shape=shape((BANDS, PACK + HALO, LANES), BF16),
        in_specs=[SM, VM, HB],
        out_specs=VM,
        scratch_shapes=[pltpu.VMEM((2, HALO, LANES), BF16), DMA((1,))],
        compiler_params=params(4),
        name="edged",
    )(meta, recv, edges)


def halo_rows(meta_ref, recv_ref):
    me = meta_ref[0]
    halos = []
    for near, there in ((me - 1, me > 0), (me + 1, me < BANDS - 1)):
        source = jnp.clip(near, 0, BANDS - 1)
        main = recv_ref[source, PACK : PACK + ROWS, :].astype(F32)
        rest = unfolded(recv_ref[source, PACK + ROWS :, :].astype(F32), 0, LEV, LEV)
        halos.append([jnp.where(there, value, 0.0) for value in (main, rest)])
    return halos


def halo_row(edge_ref):
    rest = edge_ref[ROWS:, :].astype(F32)
    return edge_ref[:ROWS, :].astype(F32), unfolded(rest, 0, LEV, LEV), unfolded(rest, 2 * LEV, LEV, LEV)


def stage_blocks(recv_ref, main_ref, rest_ref):
    half = ROWS // 2
    for source in range(BANDS):
        packed = recv_ref[source, 2 * ROWS : PACK, :].astype(F32)
        for b in range(2):
            at = (b * BANDS + source) * ROWS
            main_ref[at : at + ROWS, :] = recv_ref[source, b * ROWS : (b + 1) * ROWS, :].astype(F32)
            rest_ref[at : at + half, :] = pull(packed, b * LEV)
            rest_ref[at + half : at + ROWS, :] = pull(packed, (2 + b) * LEV)


def block_sum(meta_ref, row, main_ref, rest_ref):
    main = jnp.zeros((ROWS, LANES), F32)
    rest = jnp.zeros((ROWS, LANES), F32)
    for block in range(BLOCKS):
        share = jnp.where(global_row(meta_ref, block) == row, 1.0, 0.0)
        k = slot(block) * ROWS
        main = main + share * main_ref[k : k + ROWS, :]
        rest = rest + share * rest_ref[k : k + ROWS, :]
    return main, rest


KEPT = 32
GROUP = LANES // KEPT
TALL = COLS + LEV


def stage_corrections(meta_ref, recv_ref, halos, wind_ref, main_ref, rest_ref, tall_ref):
    clear(main_ref, rest_ref)
    me = meta_ref[0]
    sums = [list(halo) for halo in halos]
    for source in range(BANDS):
        packed = recv_ref[source, 2 * ROWS : PACK, :].astype(F32)
        for b in range(2):
            k = b * BANDS + source
            main = recv_ref[source, b * ROWS : (b + 1) * ROWS, :].astype(F32)
            rest = unfolded(packed, b * LEV, 2 * LEV, LEV)
            main_ref[pl.ds(k, ROWS, stride=KEPT), :] = main
            rest_ref[pl.ds(k, ROWS, stride=KEPT), :] = rest
            for at, row in enumerate((me * LANES - 1, (me + 1) * LANES)):
                share = jnp.where(global_row(meta_ref, 2 * source + b) == row, 1.0, 0.0)
                sums[at][0] = sums[at][0] + share * main
                sums[at][1] = sums[at][1] + share * rest
    for at in range(2):
        main_ref[pl.ds(16 + at, ROWS, stride=KEPT), :] = sums[at][0].astype(BF16).astype(F32)
        rest_ref[pl.ds(16 + at, ROWS, stride=KEPT), :] = sums[at][1].astype(BF16).astype(F32)
    wind = halo_row(wind_ref)[2]
    rest_ref[pl.ds(18, ROWS, stride=KEPT), :] = pltpu.roll(wind, LEV, axis=1)
    for t in range(ROWS // GROUP):
        span = slice(t * LANES, (t + 1) * LANES)
        tall_ref[t * TALL : t * TALL + LANES, :] = main_ref[span, :].T.astype(BF16)
        tall_ref[t * TALL + LANES : (t + 1) * TALL, :] = rest_ref[span, :].T[: 2 * LEV].astype(BF16)


def rows_kernel(meta_ref, before_ref, context_ref, west_ref, east_ref, recv_ref, out_ref, main_ref, rest_ref):
    stage_blocks(recv_ref, main_ref, rest_ref)
    me = meta_ref[0]
    sub = lax.broadcasted_iota(jnp.int32, (ROWS, LANES), 0)
    inner = (sub >= 1) & (sub <= XS)

    def rimmed(value, at):
        value = jnp.where(sub == 0, west_ref[at : at + 1, :], value)
        return jnp.where(sub == XS + 1, east_ref[at : at + 1, :], value)

    def known(p):
        return rimmed(before_ref[p * ROWS : (p + 1) * ROWS, :].astype(F32), p)

    last = None
    tail = known(2)
    winds = rimmed(context_ref[3], 3)
    for e in range(2):
        row = global_row(meta_ref, 2 * me + e)
        across = pull(winds, 2 * e * LEV)
        east = jnp.maximum(across, 0.0)
        west = jnp.minimum(pltpu.roll(across, 1, axis=0), 0.0)
        north = jnp.where(row == BANDS * LANES - 1, 0.0, jnp.maximum(pull(winds, (2 * e + 1) * LEV), 0.0))
        south = jnp.minimum(pull(context_ref[4], e * LEV), 0.0)
        coefs = (east, west, north, south)
        added = [block_sum(meta_ref, row + near, main_ref, rest_ref) for near in (-1, 0, 1)]

        def moved(coefs, here, aside, behind, ahead):
            east, west, north, south = coefs
            here = here.astype(BF16).astype(F32)
            centre = 1.0 - east + west - north + south
            made = (
                centre * here
                + (east * pltpu.roll(here, ROWS - 1, axis=0) - west * pltpu.roll(here, 1, axis=0))
                + (aside + (north * ahead - south * behind))
            )
            return jnp.where(inner, made, 0.0)

        main = moved([wide(c) for c in coefs], known(e) + added[1][0], context_ref[e], added[0][0], added[2][0])
        out_ref[e * ROWS : (e + 1) * ROWS, :] = main.astype(BF16)
        rest = pull(tail, e * LEV) + added[1][1]
        rest = moved(coefs, rest, pull(context_ref[2], e * LEV), added[0][1], added[2][1])
        rest = lanes_below(rest, LEV)
        last = rest if e == 0 else last + pltpu.roll(rest, LEV, axis=1)
    out_ref[2 * ROWS :, :] = last.astype(BF16)


def next_rows(*args):
    return pl.pallas_call(
        rows_kernel,
        out_shape=shape((3 * ROWS, LANES), BF16),
        in_specs=[SM] + [VM] * 5,
        out_specs=VM,
        scratch_shapes=[STAGE, STAGE],
        compiler_params=params(4),
        name="rows",
    )(*args)


def place_weights(meta_ref, q):
    sub, lane = iotas((LANES, 2 * LANES))
    kept = sub - q * KEPT
    target = jnp.full(sub.shape, -1, jnp.int32)
    for block in range(BLOCKS):
        at = global_row(meta_ref, block) - meta_ref[0] * LANES
        target = jnp.where(kept == slot(block), jnp.where((at >= 0) & (at < LANES), at, -1), target)
    target = jnp.where((kept == 16) | (kept == 18), LANES, target)
    target = jnp.where(kept == 17, 2 * LANES - 1, target)
    return jnp.where(lane == target, 1.0, 0.0).astype(BF16)


def advance(
    meta_ref, cells_ref, winds_ref, west_ref, east_ref, wind_west_ref, tall_ref, placed_ref, smooth_ref, emit, leaving,
    rounded,
):
    for q in range(GROUP):
        placed_ref[q] = jnp.dot(tall_ref[...], place_weights(meta_ref, q), preferred_element_type=F32)
    top = meta_ref[0] == BANDS - 1

    def smooth(r, base):
        at = (r // GROUP) * TALL
        value = base.astype(F32) + placed_ref[r % GROUP, pl.ds(at, COLS), :LANES]
        if rounded:
            value = value.astype(BF16).astype(F32)
        smooth_ref[r] = value
        return value

    def step(x, ahead):
        ahead = smooth(x + 2, ahead)
        emit(x, stencil(x, top, winds_ref, wind_west_ref, smooth_ref, ahead, placed_ref))

    def body(x, carry):
        step(x, cells_ref[x + 1])
        return carry

    smooth(0, west_ref[:COLS, :])
    smooth(1, cells_ref[0])
    for (start, size), copy in zip(SPANS, leaving):
        for x in range(start, min(start + size, XS - 1)):
            body(x, 0)
        if start + size == XS:
            step(XS - 1, east_ref[...])
        copy.start()


def stencil(x, top, winds_ref, west_ref, smooth_ref, ahead, placed_ref):
    at = ((x + 1) // GROUP) * TALL
    q = (x + 1) % GROUP
    lane = lax.broadcasted_iota(jnp.int32, (LEV, LANES), 1)
    courant = winds_ref[x].astype(F32)
    before = winds_ref[jnp.maximum(x - 1, 0), :LEV, :].astype(F32)
    before = jnp.where(x == 0, west_ref[COLS:, :].astype(F32), before)
    across = courant[:LEV]
    along = jnp.where(top & (lane == LANES - 1), 0.0, courant[LEV:])
    south_along = jnp.where(lane == 0, placed_ref[q, pl.ds(at + COLS, LEV), LANES:], pltpu.roll(along, 1, axis=1))
    east = jnp.maximum(across, 0.0)
    west = jnp.minimum(before, 0.0)
    north = jnp.maximum(along, 0.0)
    south = jnp.minimum(south_along, 0.0)
    centre = 1.0 - east + west - north + south
    made = []
    for v in range(VAR):
        span = slice(v * LEV, (v + 1) * LEV)
        here = smooth_ref[x + 1, span, :]
        edge = placed_ref[q, pl.ds(at + v * LEV, LEV), LANES:]
        above = jnp.where(lane == LANES - 1, edge, pltpu.roll(here, LANES - 1, axis=1))
        below = jnp.where(lane == 0, edge, pltpu.roll(here, 1, axis=1))
        made.append(
            centre * here
            + (east * ahead[span] - west * smooth_ref[x, span, :])
            + (north * above - south * below)
        )
    return made


SCRATCH = [
    pltpu.VMEM((KEPT * ROWS, LANES), F32),
    pltpu.VMEM((KEPT * ROWS, LANES), F32),
    pltpu.VMEM((ROWS // GROUP * TALL, LANES), BF16),
    pltpu.VMEM((GROUP, ROWS // GROUP * TALL, 2 * LANES), F32),
    pltpu.VMEM((XS + 2, COLS, LANES), F32),
]


def first_kernel(
    meta_ref, cells_hbm, winds_hbm, west_ref, east_ref, recv_ref, south_ref, north_ref,
    out_hbm, edges_ref, to_east_hbm, to_west_hbm,
    main_ref, rest_ref, tall_ref, placed_ref, smooth_ref, out_ref, out_sem, rim_sem,
    cells_ref, cells_sem, winds_ref, winds_sem,
):
    arriving = copies(cells_hbm, cells_ref, cells_sem) + copies(winds_hbm, winds_ref, winds_sem)
    for copy in arriving:
        copy.start()
    halos = [halo_row(ref)[:2] for ref in (south_ref, north_ref)]
    stage_corrections(meta_ref, recv_ref, halos, south_ref, main_ref, rest_ref, tall_ref)
    for copy in arriving:
        copy.wait()

    def emit(x, made):
        for v in range(VAR):
            out_ref[x, v * LEV : (v + 1) * LEV, :] = made[v].astype(BF16)

    leaving = copies(out_ref, out_hbm, out_sem)
    advance(
        meta_ref, cells_ref, winds_ref, west_ref, east_ref, west_ref, tall_ref, placed_ref, smooth_ref, emit, leaving,
        True,
    )
    rims = [
        pltpu.make_async_copy(out_ref.at[0], to_west_hbm, rim_sem.at[0]),
        pltpu.make_async_copy(out_ref.at[XS - 1], to_east_hbm, rim_sem.at[1]),
    ]
    for copy in rims:
        copy.start()
    sub, lane = iotas((LANES, LANES))
    halves = [(sub == 0) & (lane == 2 * side) | (sub == LANES - 1) & (lane == 2 * side + 1) for side in range(2)]
    ends = jnp.concatenate([jnp.where(hit, 1.0, 0.0) for hit in halves], axis=0).astype(BF16)
    total = None
    for x in range(0, XS, 2):
        pair = jnp.concatenate([out_ref[min(x + side, XS - 1)] for side in range(2)], axis=1)
        found = jnp.dot(pair, ends, preferred_element_type=F32)
        if x == XS - 1:
            found = jnp.where(lax.broadcasted_iota(jnp.int32, found.shape, 1) < 2, found, 0.0)
        found = pltpu.roll(found, 2 * x + 2, axis=1)
        total = found if total is None else total + found
    main_ref[:LANES, :] = total[:LANES].T
    rest = jnp.concatenate([total[LANES:], jnp.zeros((LANES - LEV, LANES), F32)], axis=0)
    rest_ref[:LANES, :] = rest.T
    for at in range(2):
        edges_ref[at, :ROWS, :] = main_ref[pl.ds(at, ROWS, stride=2), :].astype(BF16)
        edges_ref[at, ROWS:, :] = folded(rest_ref[pl.ds(at, ROWS, stride=2), :], LEV).astype(BF16)
    for copy in leaving + rims:
        copy.wait()


def first_substep(*args):
    return pl.pallas_call(
        first_kernel,
        out_shape=(
            shape((XS, COLS, LANES), BF16),
            shape((2, HALO, LANES), BF16),
            shape((COLS, LANES), BF16),
            shape((COLS, LANES), BF16),
        ),
        in_specs=[SM, HB, HB] + [VM] * 5,
        out_specs=(HB, VM, HB, HB),
        scratch_shapes=SCRATCH
        + [
            pltpu.VMEM((XS, COLS, LANES), BF16),
            DMA((len(SPANS),)),
            DMA((2,)),
            pltpu.VMEM((XS, COLS, LANES), BF16),
            DMA((len(SPANS),)),
            pltpu.VMEM((XS, 2 * LEV, LANES), BF16),
            DMA((len(SPANS),)),
        ],
        compiler_params=params(58),
        name="first",
    )(*args)


def last_kernel(
    meta_ref, cells_ref, winds_ref, west_ref, east_ref, recv_ref, wind_ref, wind_west_ref,
    out_hbm, main_ref, rest_ref, tall_ref, placed_ref, smooth_ref, out_ref, out_sem,
):
    stage_corrections(meta_ref, recv_ref, halo_rows(meta_ref, recv_ref), wind_ref, main_ref, rest_ref, tall_ref)

    def emit(x, made):
        for v in range(VAR):
            out_ref[x, v * LEV : (v + 1) * LEV, :] = made[v]

    leaving = copies(out_ref, out_hbm, out_sem)
    advance(
        meta_ref, cells_ref, winds_ref, west_ref, east_ref, wind_west_ref, tall_ref, placed_ref, smooth_ref, emit,
        leaving, False,
    )
    for copy in leaving:
        copy.wait()


def last_substep(*args):
    return pl.pallas_call(
        last_kernel,
        out_shape=shape((XS, COLS, LANES), F32),
        in_specs=[SM] + [VM] * 7,
        out_specs=HB,
        scratch_shapes=SCRATCH + [pltpu.VMEM((XS, COLS, LANES), F32), DMA((len(SPANS),))],
        compiler_params=params(30),
        name="last",
    )(*args)


def stay_kernel(cells_hbm, message_hbm, cells_ref, sem_ref):
    arriving = copies(cells_hbm, cells_ref, sem_ref)
    for copy in arriving:
        copy.start()
    for copy in arriving:
        copy.wait()


def bring_back(cells, message):
    return pl.pallas_call(
        stay_kernel,
        out_shape=shape((XS, COLS, LANES), BF16),
        in_specs=[HB, HB],
        out_specs=VM,
        scratch_shapes=[DMA((len(SPANS),))],
        compiler_params=params(4),
        name="stay",
    )(cells, message)


TEAMMATES = [[(i, i ^ (16 * (other // 2) + other % 2)) for i in range(LON_DEV)] for other in range(1, TEAM)]
SOUTHWARD = [(i + 1, i) for i in range(BANDS - 1)]
NORTHWARD = [(i, i + 1) for i in range(BANDS - 1)]
EASTWARD = [(i, (i + 1) % LON_DEV) for i in range(LON_DEV)]
WESTWARD = [(i, (i - 1) % LON_DEV) for i in range(LON_DEV)]
ALONG_Z = [[16 * (place // 2) + 2 * t + place % 2 for t in range(TARGETS)] for place in range(TEAM)]


def by_lat(messages):
    return lax.all_to_all(messages, "lat", 0, 0, tiled=True)


def filtered(rows, ops):
    team = [rows] + [lax.ppermute(rows, "lon", mates) for mates in TEAMMATES]
    partial = products(team, ops)
    return lax.all_to_all(partial, "lon", 0, 0, tiled=True, axis_index_groups=ALONG_Z)


def shards(cotangent, winds, filter_ops, block_band, block_row):
    me = lax.axis_index("lat").astype(jnp.int32).reshape(1)
    at = lax.axis_index("lon").astype(jnp.int32)
    place = ((at >> 4) * 2 + (at & 1)).reshape(1)
    meta = jnp.concatenate([me, place, block_band, block_row])
    made = prepare_operators(meta, jnp.pad(filter_ops, ((0, 0), (1, 2), (0, 0))))
    ops = [made[0]] + [lax.ppermute(part, "lon", mates) for part, mates in zip(made[1:], TEAMMATES)]
    send, to_south, to_north, to_east, to_west = pick_rows(block_band, block_row, cotangent, winds)
    west = lax.ppermute(to_east, "lon", EASTWARD)
    east = lax.ppermute(to_west, "lon", WESTWARD)
    recv, west, east, to_south, to_north = lax.optimization_barrier((by_lat(send), west, east, to_south, to_north))
    rows = unpack_rows(recv)
    swapped = filtered(rows, ops)
    context, row_east, row_west = unpack_context(meta, recv, rows)
    row_from_west = lax.ppermute(row_east, "lon", EASTWARD)
    row_from_east = lax.ppermute(row_west, "lon", WESTWARD)
    south = lax.ppermute(to_north, "lat", NORTHWARD)
    north = lax.ppermute(to_south, "lat", SOUTHWARD)
    swapped, row_from_west, row_from_east, south, north = lax.optimization_barrier(
        (swapped, row_from_west, row_from_east, south, north)
    )
    given = by_lat(totals(swapped))
    rows = next_rows(meta, rows, context, row_from_west, row_from_east, given)
    swapped = filtered(rows, ops)
    state, edges, to_east, to_west = first_substep(meta, cotangent, winds, west, east, given, south, north)
    message = totals_with_edges(meta, swapped, edges)
    given2 = by_lat(message)
    west2 = lax.ppermute(to_east, "lon", EASTWARD)
    east2 = lax.ppermute(to_west, "lon", WESTWARD)
    return last_substep(meta, bring_back(state, message), winds, west2, east2, given2, south, west)


def solution(mesh):
    return jax.shard_map(
        shards,
        mesh=mesh,
        in_specs=(P("lon", None, "lat"), P("lon", None, "lat"), P("lat", "lon", None), P(), P()),
        out_specs=P("lon", None, "lat"),
        check_vma=False,
    )
```

```python
import jax
import jax.numpy as jnp
from jax import lax
from jax.experimental import pallas as pl
from jax.experimental.pallas import tpu as pltpu
from jax.sharding import PartitionSpec as P

VAR = 5
LEV = 32
COLS = VAR * LEV
XS = 45
ROWS = 48
LANES = 128
BANDS = 8
NLON = 1440
LON_DEV = 32
TARGETS = 8
TEAM = 4
BLOCKS = 16
PICKS = 56
WIRE = 6 * ROWS + 24
PACK = 120
HALO = 72
CHUNK = 9

F32 = jnp.float32
BF16 = jnp.bfloat16
VM = pl.BlockSpec(memory_space=pltpu.VMEM)
SM = pl.BlockSpec(memory_space=pltpu.SMEM)
HB = pl.BlockSpec(memory_space=pl.ANY)
DMA = pltpu.SemaphoreType.DMA
SPANS = [(0, 6), (6, 8), (14, 10), (24, 10), (34, 8), (42, 3)]


def shape(dims, kind):
    return jax.ShapeDtypeStruct(dims, kind)


def params(mib):
    return pltpu.CompilerParams(vmem_limit_bytes=mib * 2**20)


def iotas(dims):
    return (
        lax.broadcasted_iota(jnp.int32, dims, 0),
        lax.broadcasted_iota(jnp.int32, dims, 1),
    )


def lanes_below(value, limit):
    lane = lax.broadcasted_iota(jnp.int32, value.shape, 1)
    return jnp.where(lane < limit, value, jnp.zeros_like(value))


def dot_nt(a, b):
    return lax.dot_general(a, b, (((1,), (1,)), ((), ())), preferred_element_type=F32)


def dot_tn(a, b):
    return lax.dot_general(a, b, (((0,), (0,)), ((), ())), preferred_element_type=F32)


def operator_kernel(meta_ref, ops_ref, *out_refs):
    place = meta_ref[1]
    for t in range(TARGETS):
        tiles = []
        for member in range(TEAM):
            start = XS * ((member // 2) * 2 * TARGETS + 2 * t + member % 2) - 1
            total = None
            first = max(start, 0) // LANES * LANES
            spans = [(first, min(first + 2 * LANES, NLON))]
            if start < 0:
                spans.append(((NLON - 1) // LANES * LANES, NLON))
            if start + XS + 2 > NLON:
                spans.append((0, LANES))
            for low, high in spans:
                row, lane = iotas((ROWS, high - low))
                wanted = start + row
                wanted = jnp.where(wanted < 0, wanted + NLON, wanted)
                wanted = jnp.where(wanted >= NLON, wanted - NLON, wanted)
                hit = (lane + low == wanted) & (row < XS + 2)
                pick = jnp.where(hit, 1.0, 0.0).astype(BF16)
                window = ops_ref[:, :, low:high].reshape(2 * ROWS, high - low)
                part = dot_nt(pick, window)
                total = part if total is None else total + part
            tiles.append(total)
        rows = slice(ROWS * t, ROWS * (t + 1))
        for other in range(TEAM):
            value = tiles[other]
            for member in range(1, TEAM):
                value = jnp.where(place == member, tiles[member ^ other], value)
            out_refs[other][rows, :] = value.astype(BF16)


def prepare_operators(meta, ops):
    out = shape((TARGETS * ROWS, 2 * ROWS), BF16)
    return pl.pallas_call(
        operator_kernel,
        out_shape=(out,) * TEAM,
        in_specs=[SM, VM],
        out_specs=(VM,) * TEAM,
        compiler_params=params(6),
        name="operators",
    )(meta, ops)


def slot(block):
    return (block % 2) * BANDS + block // 2


def global_row(meta_ref, block):
    return meta_ref[2 + block] * LANES + meta_ref[2 + BLOCKS + block]


def clear_rims(ref, count):
    blank = jnp.zeros((count, LANES), ref.dtype)
    for r in (0, XS + 1, XS + 2):
        ref[pl.ds(r, count, stride=ROWS), :] = blank


def pick_weights(meta_ref):
    me = meta_ref[0]
    lane = lax.broadcasted_iota(jnp.int32, (8, LANES), 1)
    pick = lane & 63
    target = jnp.full(lane.shape, -1, jnp.int32)
    for block in range(BLOCKS):
        at = global_row(meta_ref, block) - me * LANES
        for near in range(3):
            target = jnp.where(pick == near * BLOCKS + slot(block), at + (near - 1), target)
    target = jnp.where(pick == 3 * BLOCKS, 0, target)
    target = jnp.where(pick == 3 * BLOCKS + 1, LANES - 1, target)
    sub, lane = iotas((LANES, LANES))
    hit = sub == jnp.broadcast_to(target[:1], (LANES, LANES))
    halves = [jnp.where(hit & ((lane < 64) == side), 1.0, 0.0) for side in (True, False)]
    return jnp.concatenate(halves, axis=0).astype(BF16)


def keep(value, *starts):
    lane = lax.broadcasted_iota(jnp.int32, value.shape, 1)
    hit = (lane >= starts[0]) & (lane < starts[0] + LEV)
    for start in starts[1:]:
        hit = hit | ((lane >= start) & (lane < start + LEV))
    return jnp.where(hit, value, jnp.zeros_like(value))


def pull(value, start):
    moved = pltpu.roll(value, LANES - start, axis=1) if start else value
    return lanes_below(moved, LEV)


def wide(value):
    value = value + pltpu.roll(value, LEV, axis=1)
    return value + pltpu.roll(value, 2 * LEV, axis=1)


def folded(value, width):
    half = ROWS // 2
    return value[:half] + pltpu.roll(value[half:], width, axis=1)


def unfolded(value, start, width, limit):
    low = pltpu.roll(value, LANES - start, axis=1) if start else value
    high = pltpu.roll(value, LANES - start - width, axis=1)
    return jnp.concatenate([lanes_below(low, limit), lanes_below(high, limit)], axis=0)


def pack_messages(meta_ref, main_ref, rest_ref, send_ref, edges_ref, leaving):
    me = meta_ref[0]

    def picked(ref, k):
        return ref[k * ROWS : (k + 1) * ROWS, :]

    def add(d, start, count, value):
        span = slice(start, start + count)
        send_ref[d, span, :] = (send_ref[d, span, :].astype(F32) + value).astype(BF16)

    for block in range(BLOCKS):
        d, e = block // 2, block % 2
        k = slot(block)
        at = global_row(meta_ref, block) - me * LANES

        @pl.when((at >= -1) & (at <= LANES))
        def _():
            mine = (at >= 0) & (at < LANES)
            here = picked(rest_ref, BLOCKS + k)
            behind = picked(rest_ref, k)
            before = pull(behind, 2 * LEV)
            one = lanes_below(jnp.ones_like(here), LEV)
            north = jnp.where(mine, jnp.maximum(pull(here, 2 * LEV), 0.0), one)
            south = jnp.where(mine, jnp.minimum(before, 0.0), -one)
            main = wide(north) * picked(main_ref, 2 * BLOCKS + k) - wide(south) * picked(main_ref, k)
            rest = north * picked(rest_ref, 2 * BLOCKS + k) - south * behind
            send_ref[d, e * ROWS : (e + 1) * ROWS, :] = picked(main_ref, BLOCKS + k).astype(BF16)
            send_ref[d, (2 + e) * ROWS : (3 + e) * ROWS, :] = main.astype(BF16)
            tail = keep(here, 0) + pltpu.roll(rest, 2 * LEV, axis=1)
            add(d, 4 * ROWS, ROWS, pltpu.roll(tail, LEV, axis=1) if e else tail)
            add(d, 5 * ROWS, ROWS, pltpu.roll(keep(here, LEV, 2 * LEV), (1 if e else 3) * LEV, axis=1))
            add(d, 6 * ROWS, ROWS // 2, folded(pltpu.roll(before, LEV, axis=1) if e else before, 2 * LEV))

        if e:
            leaving[d].start()

    for at in range(2):
        k = 3 * BLOCKS + at
        edges_ref[at, :ROWS, :] = picked(main_ref, k).astype(BF16)
        rest = picked(rest_ref, k)
        rest = folded(keep(rest, 0), LEV) + folded(keep(rest, 2 * LEV), LEV)
        edges_ref[at, ROWS:, :] = rest.astype(BF16)


def clear(*refs):
    for ref in refs:
        ref[...] = jnp.zeros(ref.shape, ref.dtype)


def copies(source_ref, target_ref, sem_ref):
    return [
        pltpu.make_async_copy(source_ref.at[pl.ds(start, size)], target_ref.at[pl.ds(start, size)], sem_ref.at[n])
        for n, (start, size) in enumerate(SPANS)
    ]


class Scalars:
    def __init__(self, me, band_ref, row_ref):
        self.me, self.band_ref, self.row_ref = me, band_ref, row_ref

    def __getitem__(self, at):
        if at == 0:
            return self.me
        return self.band_ref[at - 2] if at < 2 + BLOCKS else self.row_ref[at - 2 - BLOCKS]


def pick_kernel(
    band_ref, row_ref, cells_hbm, winds_hbm, send_hbm, edges_ref, east_ref, west_ref,
    main_ref, rest_ref, cells_ref, winds_ref, send_ref, cells_sem, winds_sem, send_sem,
):
    meta_ref = Scalars(lax.axis_index("lat").astype(jnp.int32), band_ref, row_ref)
    arriving = list(zip(copies(cells_hbm, cells_ref, cells_sem), copies(winds_hbm, winds_ref, winds_sem)))
    for pair in arriving:
        for copy in pair:
            copy.start()
    clear_rims(main_ref, PICKS)
    clear_rims(rest_ref, PICKS)
    weights = pick_weights(meta_ref)
    clear(send_ref)
    blank = jnp.zeros((LEV, 2 * LANES), BF16)
    for (start, size), pair in zip(SPANS, arriving):
        for copy in pair:
            copy.wait()
        for y in range(start, start + size, 2):
            both = (y, min(y + 1, XS - 1))
            main = jnp.concatenate([cells_ref[z, :LANES, :] for z in both], axis=1)
            rest = jnp.concatenate([cells_ref[z, LANES:, :] for z in both], axis=1)
            wind = jnp.concatenate([winds_ref[z] for z in both], axis=1)
            rest = jnp.concatenate([rest, wind, blank], axis=0)
            main = jnp.dot(main, weights, preferred_element_type=F32).astype(BF16).T.astype(F32)
            rest = jnp.dot(rest, weights, preferred_element_type=F32).astype(BF16).T.astype(F32)
            for side in range(min(2, XS - y)):
                at = pl.ds(y + side + 1, PICKS, stride=ROWS)
                main_ref[at, :] = main[64 * side : 64 * side + PICKS]
                rest_ref[at, :] = rest[64 * side : 64 * side + PICKS]
    east_ref[:COLS, :] = cells_ref[XS - 1]
    east_ref[COLS:, :] = winds_ref[XS - 1, :LEV, :]
    west_ref[...] = cells_ref[0]
    leaving = [pltpu.make_async_copy(send_ref.at[d], send_hbm.at[d], send_sem.at[d]) for d in range(BANDS)]
    pack_messages(meta_ref, main_ref, rest_ref, send_ref, edges_ref, leaving)
    for copy in leaving:
        copy.wait()


STAGE = pltpu.VMEM((24 * ROWS, LANES), F32)
PICKED = pltpu.VMEM((PICKS * ROWS, LANES), F32)


def pick_rows(band, row, cells, winds):
    return pl.pallas_call(
        pick_kernel,
        out_shape=(
            shape((BANDS, WIRE, LANES), BF16),
            shape((2, HALO, LANES), BF16),
            shape((COLS + LEV, LANES), BF16),
            shape((COLS, LANES), BF16),
        ),
        in_specs=[SM, SM, HB, HB],
        out_specs=(HB, VM, VM, VM),
        scratch_shapes=[
            PICKED,
            PICKED,
            pltpu.VMEM((XS, COLS, LANES), BF16),
            pltpu.VMEM((XS, 2 * LEV, LANES), BF16),
            pltpu.VMEM((BANDS, WIRE, LANES), BF16),
            DMA((len(SPANS),)),
            DMA((len(SPANS),)),
            DMA((BANDS,)),
        ],
        compiler_params=params(58),
        name="pick",
    )(band, row, cells, winds)


def added(recv_ref, span):
    total = recv_ref[0, span, :].astype(F32)
    for s in range(1, BANDS):
        total = total + recv_ref[s, span, :].astype(F32)
    return total


def unpack_kernel(recv_ref, rows_ref):
    rows_ref[: 2 * ROWS, :] = added(recv_ref, slice(0, 2 * ROWS)).astype(BF16)
    tail = added(recv_ref, slice(4 * ROWS, 5 * ROWS))
    rows_ref[2 * ROWS :, :] = lanes_below(tail, 2 * LEV).astype(BF16)


def unpack_rows(recv):
    return pl.pallas_call(
        unpack_kernel,
        out_shape=shape((3 * ROWS, LANES), BF16),
        in_specs=[VM],
        out_specs=VM,
        compiler_params=params(8),
        name="unpack",
    )(recv)


def context_kernel(meta_ref, recv_ref, rows_ref, context_ref, to_east_ref, to_west_ref):
    me = meta_ref[0]
    winds = added(recv_ref, slice(5 * ROWS, 6 * ROWS))
    souths = unfolded(added(recv_ref, slice(6 * ROWS, WIRE)), 0, 2 * LEV, 2 * LEV)
    tails = None
    for e in range(2):
        band = meta_ref[2 + 2 * me + e]
        row = meta_ref[2 + BLOCKS + 2 * me + e]
        north = jnp.maximum(pull(winds, (2 * e + 1) * LEV), 0.0)
        south = jnp.minimum(pull(souths, e * LEV), 0.0)
        main = recv_ref[band, (2 + e) * ROWS : (3 + e) * ROWS, :].astype(F32)
        rest = pull(recv_ref[band, 4 * ROWS : 5 * ROWS, :].astype(F32), (2 + e) * LEV)
        for source, there, coef in (
            (jnp.minimum(band + 1, BANDS - 1), (row == LANES - 1) & (band < BANDS - 1), north),
            (jnp.maximum(band - 1, 0), (row == 0) & (band > 0), -south),
        ):
            share = jnp.where(there, coef, 0.0)
            main = main + wide(share) * recv_ref[source, (2 + e) * ROWS : (3 + e) * ROWS, :].astype(F32)
            rest = rest + share * pull(recv_ref[source, 4 * ROWS : 5 * ROWS, :].astype(F32), (2 + e) * LEV)
        context_ref[e] = main
        tails = rest if e == 0 else tails + pltpu.roll(rest, LEV, axis=1)
    context_ref[2] = tails
    context_ref[3] = winds
    context_ref[4] = souths
    clear(to_east_ref, to_west_ref)
    rims = [rows_ref[p * ROWS : (p + 1) * ROWS, :].astype(F32) for p in range(3)] + [winds]
    for at, tile in enumerate(rims):
        to_east_ref[at : at + 1, :] = tile[XS : XS + 1]
        to_west_ref[at : at + 1, :] = tile[1:2]


def unpack_context(meta, recv, rows):
    edge = shape((8, LANES), F32)
    return pl.pallas_call(
        context_kernel,
        out_shape=(shape((5, ROWS, LANES), F32), edge, edge),
        in_specs=[SM, VM, VM],
        out_specs=(VM,) * 3,
        compiler_params=params(8),
        name="context",
    )(meta, recv, rows)


def spread_blocks(rows_ref):
    first = rows_ref[:ROWS, :]
    second = rows_ref[ROWS : 2 * ROWS, :]
    rest = rows_ref[2 * ROWS :, :].astype(F32)
    lower = lanes_below(rest, LEV)
    upper = rest - lower
    blank = jnp.zeros_like(first)
    return jnp.concatenate(
        [
            jnp.concatenate([first, blank, lower.astype(BF16)], axis=1),
            jnp.concatenate([blank, second, upper.astype(BF16)], axis=1),
        ],
        axis=0,
    )


def product_kernel(*refs):
    out_ref = refs[-1]
    rows = [spread_blocks(ref) for ref in refs[:TEAM]]
    for q in range(2):
        span = slice(4 * ROWS * q, 4 * ROWS * (q + 1))
        made = None
        for ops_ref, values in zip(refs[TEAM : 2 * TEAM], rows):
            part = jnp.dot(ops_ref[span, :], values, preferred_element_type=F32)
            made = part if made is None else made + part
        for s in range(4):
            part = made[ROWS * s : ROWS * (s + 1)]
            t = 4 * q + s
            out_ref[t, :ROWS, :] = part[:, :LANES].astype(BF16)
            out_ref[t, ROWS : 2 * ROWS, :] = part[:, LANES : 2 * LANES].astype(BF16)
            out_ref[t, 2 * ROWS :, :] = folded(part[:, 2 * LANES :], 2 * LEV).astype(BF16)


def products(rows, ops):
    return pl.pallas_call(
        product_kernel,
        out_shape=shape((TARGETS, PACK, LANES), BF16),
        in_specs=[VM] * (2 * TEAM),
        out_specs=VM,
        compiler_params=params(6),
        name="product",
    )(*rows, *ops)


def total_kernel(meta_ref, recv_ref, edges_hbm, out_ref, edges_ref, sem_ref):
    arriving = pltpu.make_async_copy(edges_hbm, edges_ref, sem_ref.at[0])
    arriving.start()
    total = recv_ref[0].astype(F32)
    for s in range(1, TARGETS):
        total = total + recv_ref[s].astype(F32)
    total = total.astype(BF16)
    me = meta_ref[0]
    for d in range(BANDS):
        out_ref[d, :PACK, :] = total
    arriving.wait()
    for d in range(BANDS):
        edge = jnp.where(d == me + 1, edges_ref[1], jnp.zeros((HALO, LANES), BF16))
        out_ref[d, PACK:, :] = jnp.where(d == me - 1, edges_ref[0], edge)


def totals(meta, recv, edges):
    return pl.pallas_call(
        total_kernel,
        out_shape=shape((BANDS, PACK + HALO, LANES), BF16),
        in_specs=[SM, VM, HB],
        out_specs=VM,
        scratch_shapes=[pltpu.VMEM((2, HALO, LANES), BF16), DMA((1,))],
        compiler_params=params(4),
        name="total",
    )(meta, recv, edges)


def fill_kernel(recv_ref, message_hbm, out_hbm, total_ref, sem_ref):
    total = recv_ref[0].astype(F32)
    for s in range(1, TARGETS):
        total = total + recv_ref[s].astype(F32)
    total_ref[...] = total.astype(BF16)
    leaving = [
        pltpu.make_async_copy(total_ref, out_hbm.at[d, pl.ds(0, PACK)], sem_ref.at[d]) for d in range(BANDS)
    ]
    for copy in leaving:
        copy.start()
    for copy in leaving:
        copy.wait()


def fill_message(recv, message):
    return pl.pallas_call(
        fill_kernel,
        out_shape=pltpu.HBM((BANDS, PACK + HALO, LANES), BF16),
        in_specs=[VM, HB],
        out_specs=HB,
        scratch_shapes=[pltpu.VMEM((PACK, LANES), BF16), DMA((BANDS,))],
        input_output_aliases={1: 0},
        compiler_params=params(4),
        name="fill",
    )(recv, pltpu.with_memory_space_constraint(message, pltpu.HBM))


def halo_rows(meta_ref, recv_ref):
    me = meta_ref[0]
    halos = []
    for near, there in ((me - 1, me > 0), (me + 1, me < BANDS - 1)):
        source = jnp.clip(near, 0, BANDS - 1)
        main = recv_ref[source, PACK : PACK + ROWS, :].astype(F32)
        rest = recv_ref[source, PACK + ROWS :, :].astype(F32)
        found = (main, unfolded(rest, 0, LEV, LEV), unfolded(rest, 2 * LEV, LEV, LEV))
        halos.append([jnp.where(there, value, 0.0) for value in found])
    return halos[0][:2], halos[1][:2], halos[0][2]


def stage_blocks(recv_ref, main_ref, rest_ref):
    half = ROWS // 2
    for source in range(BANDS):
        packed = recv_ref[source, 2 * ROWS : PACK, :].astype(F32)
        for b in range(2):
            at = (b * BANDS + source) * ROWS
            main_ref[at : at + ROWS, :] = recv_ref[source, b * ROWS : (b + 1) * ROWS, :].astype(F32)
            rest_ref[at : at + half, :] = pull(packed, b * LEV)
            rest_ref[at + half : at + ROWS, :] = pull(packed, (2 + b) * LEV)


def block_sum(meta_ref, row, main_ref, rest_ref):
    main = jnp.zeros((ROWS, LANES), F32)
    rest = jnp.zeros((ROWS, LANES), F32)
    for block in range(BLOCKS):
        share = jnp.where(global_row(meta_ref, block) == row, 1.0, 0.0)
        k = slot(block) * ROWS
        main = main + share * main_ref[k : k + ROWS, :]
        rest = rest + share * rest_ref[k : k + ROWS, :]
    return main, rest


KEPT = 32
GROUP = LANES // KEPT
TALL = COLS + LEV


def stage_corrections(meta_ref, recv_ref, wind_recv_ref, main_ref, rest_ref, tall_ref):
    clear(main_ref, rest_ref)
    me = meta_ref[0]
    halos = halo_rows(meta_ref, recv_ref)
    sums = [list(halos[0]), list(halos[1])]
    for source in range(BANDS):
        packed = recv_ref[source, 2 * ROWS : PACK, :].astype(F32)
        for b in range(2):
            k = b * BANDS + source
            main = recv_ref[source, b * ROWS : (b + 1) * ROWS, :].astype(F32)
            rest = unfolded(packed, b * LEV, 2 * LEV, LEV)
            main_ref[pl.ds(k, ROWS, stride=KEPT), :] = main
            rest_ref[pl.ds(k, ROWS, stride=KEPT), :] = rest
            for at, row in enumerate((me * LANES - 1, (me + 1) * LANES)):
                share = jnp.where(global_row(meta_ref, 2 * source + b) == row, 1.0, 0.0)
                sums[at][0] = sums[at][0] + share * main
                sums[at][1] = sums[at][1] + share * rest
    for at in range(2):
        main_ref[pl.ds(16 + at, ROWS, stride=KEPT), :] = sums[at][0].astype(BF16).astype(F32)
        rest_ref[pl.ds(16 + at, ROWS, stride=KEPT), :] = sums[at][1].astype(BF16).astype(F32)
    wind = halo_rows(meta_ref, wind_recv_ref)[2]
    rest_ref[pl.ds(18, ROWS, stride=KEPT), :] = pltpu.roll(wind, LEV, axis=1)
    for t in range(ROWS // GROUP):
        span = slice(t * LANES, (t + 1) * LANES)
        tall_ref[t * TALL : t * TALL + LANES, :] = main_ref[span, :].astype(BF16).T
        tall_ref[t * TALL + LANES : (t + 1) * TALL, :] = rest_ref[span, :].astype(BF16).T[: 2 * LEV]


def rows_kernel(meta_ref, before_ref, context_ref, west_ref, east_ref, recv_ref, out_ref, main_ref, rest_ref):
    stage_blocks(recv_ref, main_ref, rest_ref)
    me = meta_ref[0]
    sub = lax.broadcasted_iota(jnp.int32, (ROWS, LANES), 0)
    inner = (sub >= 1) & (sub <= XS)

    def rimmed(value, at):
        value = jnp.where(sub == 0, west_ref[at : at + 1, :], value)
        return jnp.where(sub == XS + 1, east_ref[at : at + 1, :], value)

    def known(p):
        return rimmed(before_ref[p * ROWS : (p + 1) * ROWS, :].astype(F32), p)

    last = None
    tail = known(2)
    winds = rimmed(context_ref[3], 3)
    for e in range(2):
        row = global_row(meta_ref, 2 * me + e)
        across = pull(winds, 2 * e * LEV)
        east = jnp.maximum(across, 0.0)
        west = jnp.minimum(pltpu.roll(across, 1, axis=0), 0.0)
        north = jnp.where(row == BANDS * LANES - 1, 0.0, jnp.maximum(pull(winds, (2 * e + 1) * LEV), 0.0))
        south = jnp.minimum(pull(context_ref[4], e * LEV), 0.0)
        coefs = (east, west, north, south)
        added = [block_sum(meta_ref, row + near, main_ref, rest_ref) for near in (-1, 0, 1)]

        def moved(coefs, here, aside, behind, ahead):
            east, west, north, south = coefs
            here = here.astype(BF16).astype(F32)
            centre = 1.0 - east + west - north + south
            made = (
                centre * here
                + (east * pltpu.roll(here, ROWS - 1, axis=0) - west * pltpu.roll(here, 1, axis=0))
                + (aside + (north * ahead - south * behind))
            )
            return jnp.where(inner, made, 0.0)

        main = moved([wide(c) for c in coefs], known(e) + added[1][0], context_ref[e], added[0][0], added[2][0])
        out_ref[e * ROWS : (e + 1) * ROWS, :] = main.astype(BF16)
        rest = pull(tail, e * LEV) + added[1][1]
        rest = moved(coefs, rest, pull(context_ref[2], e * LEV), added[0][1], added[2][1])
        rest = lanes_below(rest, LEV)
        last = rest if e == 0 else last + pltpu.roll(rest, LEV, axis=1)
    out_ref[2 * ROWS :, :] = last.astype(BF16)


def next_rows(*args):
    return pl.pallas_call(
        rows_kernel,
        out_shape=shape((3 * ROWS, LANES), BF16),
        in_specs=[SM] + [VM] * 5,
        out_specs=VM,
        scratch_shapes=[STAGE, STAGE],
        compiler_params=params(4),
        name="rows",
    )(*args)


def place_weights(meta_ref, q):
    sub, lane = iotas((LANES, 2 * LANES))
    kept = sub - q * KEPT
    target = jnp.full(sub.shape, -1, jnp.int32)
    for block in range(BLOCKS):
        at = global_row(meta_ref, block) - meta_ref[0] * LANES
        target = jnp.where(kept == slot(block), jnp.where((at >= 0) & (at < LANES), at, -1), target)
    target = jnp.where((kept == 16) | (kept == 18), LANES, target)
    target = jnp.where(kept == 17, 2 * LANES - 1, target)
    return jnp.where(lane == target, 1.0, 0.0).astype(BF16)


def advance(
    meta_ref, cells_ref, winds_ref, west_ref, east_ref, wind_west_ref, tall_ref, placed_ref, smooth_ref, emit, leaving,
    rounded,
):
    for q in range(GROUP):
        placed_ref[q] = jnp.dot(tall_ref[...], place_weights(meta_ref, q), preferred_element_type=F32)
    top = meta_ref[0] == BANDS - 1

    def smooth(r, base):
        at = (r // GROUP) * TALL
        value = base.astype(F32) + placed_ref[r % GROUP, pl.ds(at, COLS), :LANES]
        if rounded:
            value = value.astype(BF16).astype(F32)
        smooth_ref[r] = value
        return value

    def step(x, ahead):
        ahead = smooth(x + 2, ahead)
        emit(x, stencil(x, top, winds_ref, wind_west_ref, smooth_ref, ahead, placed_ref))

    def body(x, carry):
        step(x, cells_ref[x + 1])
        return carry

    smooth(0, west_ref[:COLS, :])
    smooth(1, cells_ref[0])
    for (start, size), copy in zip(SPANS, leaving):
        for x in range(start, min(start + size, XS - 1)):
            body(x, 0)
        if start + size == XS:
            step(XS - 1, east_ref[...])
        copy.start()


def stencil(x, top, winds_ref, west_ref, smooth_ref, ahead, placed_ref):
    at = ((x + 1) // GROUP) * TALL
    q = (x + 1) % GROUP
    lane = lax.broadcasted_iota(jnp.int32, (LEV, LANES), 1)
    courant = winds_ref[x].astype(F32)
    before = winds_ref[jnp.maximum(x - 1, 0), :LEV, :].astype(F32)
    before = jnp.where(x == 0, west_ref[COLS:, :].astype(F32), before)
    across = courant[:LEV]
    along = jnp.where(top & (lane == LANES - 1), 0.0, courant[LEV:])
    south_along = jnp.where(lane == 0, placed_ref[q, pl.ds(at + COLS, LEV), LANES:], pltpu.roll(along, 1, axis=1))
    east = jnp.maximum(across, 0.0)
    west = jnp.minimum(before, 0.0)
    north = jnp.maximum(along, 0.0)
    south = jnp.minimum(south_along, 0.0)
    centre = 1.0 - east + west - north + south
    made = []
    for v in range(VAR):
        span = slice(v * LEV, (v + 1) * LEV)
        here = smooth_ref[x + 1, span, :]
        edge = placed_ref[q, pl.ds(at + v * LEV, LEV), LANES:]
        above = jnp.where(lane == LANES - 1, edge, pltpu.roll(here, LANES - 1, axis=1))
        below = jnp.where(lane == 0, edge, pltpu.roll(here, 1, axis=1))
        made.append(
            centre * here
            + (east * ahead[span] - west * smooth_ref[x, span, :])
            + (north * above - south * below)
        )
    return made


SCRATCH = [
    pltpu.VMEM((KEPT * ROWS, LANES), F32),
    pltpu.VMEM((KEPT * ROWS, LANES), F32),
    pltpu.VMEM((ROWS // GROUP * TALL, LANES), BF16),
    pltpu.VMEM((GROUP, ROWS // GROUP * TALL, 2 * LANES), F32),
    pltpu.VMEM((XS + 2, COLS, LANES), F32),
]


def first_kernel(
    meta_ref, cells_hbm, winds_hbm, west_ref, east_ref, recv_ref,
    out_hbm, message_hbm, to_east_hbm, to_west_hbm,
    main_ref, rest_ref, tall_ref, placed_ref, smooth_ref, out_ref, out_sem, rim_sem,
    cells_ref, cells_sem, winds_ref, winds_sem, edges_ref, edges_sem,
):
    arriving = copies(cells_hbm, cells_ref, cells_sem) + copies(winds_hbm, winds_ref, winds_sem)
    for copy in arriving:
        copy.start()
    stage_corrections(meta_ref, recv_ref, recv_ref, main_ref, rest_ref, tall_ref)
    for copy in arriving:
        copy.wait()

    def emit(x, made):
        for v in range(VAR):
            out_ref[x, v * LEV : (v + 1) * LEV, :] = made[v].astype(BF16)

    leaving = copies(out_ref, out_hbm, out_sem)
    advance(
        meta_ref, cells_ref, winds_ref, west_ref, east_ref, west_ref, tall_ref, placed_ref, smooth_ref, emit, leaving,
        True,
    )
    rims = [
        pltpu.make_async_copy(out_ref.at[0], to_west_hbm, rim_sem.at[0]),
        pltpu.make_async_copy(out_ref.at[XS - 1], to_east_hbm, rim_sem.at[1]),
    ]
    for copy in rims:
        copy.start()
    sub, lane = iotas((LANES, LANES))
    halves = [(sub == 0) & (lane == 2 * side) | (sub == LANES - 1) & (lane == 2 * side + 1) for side in range(2)]
    ends = jnp.concatenate([jnp.where(hit, 1.0, 0.0) for hit in halves], axis=0).astype(BF16)
    total = None
    for x in range(0, XS, 2):
        pair = jnp.concatenate([out_ref[min(x + side, XS - 1)] for side in range(2)], axis=1)
        found = jnp.dot(pair, ends, preferred_element_type=F32)
        if x == XS - 1:
            found = jnp.where(lax.broadcasted_iota(jnp.int32, found.shape, 1) < 2, found, 0.0)
        found = pltpu.roll(found, 2 * x + 2, axis=1)
        total = found if total is None else total + found
    main_ref[:LANES, :] = total[:LANES].T
    rest = jnp.concatenate([total[LANES:], jnp.zeros((LANES - LEV, LANES), F32)], axis=0)
    rest_ref[:LANES, :] = rest.T
    me = meta_ref[0]
    for at, there in ((0, me - 1), (1, me + 1)):
        main = main_ref[pl.ds(at, ROWS, stride=2), :].astype(BF16)
        rest = folded(rest_ref[pl.ds(at, ROWS, stride=2), :], LEV).astype(BF16)
        edge = jnp.concatenate([main.astype(F32), rest.astype(F32)], axis=0).astype(BF16)
        for d in range(BANDS):
            before = jnp.zeros_like(edge) if at == 0 else edges_ref[d]
            edges_ref[d] = jnp.where(d == there, edge, before)
    rims.append(pltpu.make_async_copy(edges_ref, message_hbm.at[:, pl.ds(PACK, HALO)], edges_sem.at[0]))
    rims[-1].start()
    for copy in leaving + rims:
        copy.wait()


def first_substep(*args):
    return pl.pallas_call(
        first_kernel,
        out_shape=(
            shape((XS, COLS, LANES), BF16),
            shape((BANDS, PACK + HALO, LANES), BF16),
            shape((COLS, LANES), BF16),
            shape((COLS, LANES), BF16),
        ),
        in_specs=[SM, HB, HB] + [VM] * 3,
        out_specs=(HB, HB, HB, HB),
        scratch_shapes=SCRATCH
        + [
            pltpu.VMEM((XS, COLS, LANES), BF16),
            DMA((len(SPANS),)),
            DMA((2,)),
            pltpu.VMEM((XS, COLS, LANES), BF16),
            DMA((len(SPANS),)),
            pltpu.VMEM((XS, 2 * LEV, LANES), BF16),
            DMA((len(SPANS),)),
            pltpu.VMEM((BANDS, HALO, LANES), BF16),
            DMA((1,)),
        ],
        compiler_params=params(58),
        name="first",
    )(*args)


def last_kernel(
    meta_ref, cells_ref, winds_ref, west_ref, east_ref, recv_ref, wind_recv_ref, wind_west_ref,
    out_hbm, main_ref, rest_ref, tall_ref, placed_ref, smooth_ref, out_ref, out_sem,
):
    stage_corrections(meta_ref, recv_ref, wind_recv_ref, main_ref, rest_ref, tall_ref)

    def emit(x, made):
        for v in range(VAR):
            out_ref[x, v * LEV : (v + 1) * LEV, :] = made[v]

    leaving = copies(out_ref, out_hbm, out_sem)
    advance(
        meta_ref, cells_ref, winds_ref, west_ref, east_ref, wind_west_ref, tall_ref, placed_ref, smooth_ref, emit,
        leaving, False,
    )
    for copy in leaving:
        copy.wait()


def last_substep(*args):
    return pl.pallas_call(
        last_kernel,
        out_shape=shape((XS, COLS, LANES), F32),
        in_specs=[SM] + [VM] * 7,
        out_specs=HB,
        scratch_shapes=SCRATCH + [pltpu.VMEM((XS, COLS, LANES), F32), DMA((len(SPANS),))],
        compiler_params=params(30),
        name="last",
    )(*args)


def stay_kernel(cells_hbm, message_hbm, cells_ref, sem_ref):
    arriving = copies(cells_hbm, cells_ref, sem_ref)
    for copy in arriving:
        copy.start()
    for copy in arriving:
        copy.wait()


def bring_back(cells, message):
    return pl.pallas_call(
        stay_kernel,
        out_shape=shape((XS, COLS, LANES), BF16),
        in_specs=[HB, HB],
        out_specs=VM,
        scratch_shapes=[DMA((len(SPANS),))],
        compiler_params=params(4),
        name="stay",
    )(pltpu.with_memory_space_constraint(cells, pltpu.HBM), pltpu.with_memory_space_constraint(message, pltpu.HBM))


TEAMMATES = [[(i, i ^ (16 * (other // 2) + other % 2)) for i in range(LON_DEV)] for other in range(1, TEAM)]
EASTWARD = [(i, (i + 1) % LON_DEV) for i in range(LON_DEV)]
WESTWARD = [(i, (i - 1) % LON_DEV) for i in range(LON_DEV)]
ALONG_Z = [[16 * (place // 2) + 2 * t + place % 2 for t in range(TARGETS)] for place in range(TEAM)]


def by_lat(messages):
    return lax.all_to_all(messages, "lat", 0, 0, tiled=True)


def filtered(rows, ops):
    team = [rows] + [lax.ppermute(rows, "lon", mates) for mates in TEAMMATES]
    partial = products(team, ops)
    return lax.all_to_all(partial, "lon", 0, 0, tiled=True, axis_index_groups=ALONG_Z)


def shards(cotangent, winds, filter_ops, block_band, block_row):
    me = lax.axis_index("lat").astype(jnp.int32).reshape(1)
    at = lax.axis_index("lon").astype(jnp.int32)
    place = ((at >> 4) * 2 + (at & 1)).reshape(1)
    meta = jnp.concatenate([me, place, block_band, block_row])
    made = prepare_operators(meta, jnp.pad(filter_ops, ((0, 0), (1, 2), (0, 0))))
    ops = [made[0]] + [lax.ppermute(part, "lon", mates) for part, mates in zip(made[1:], TEAMMATES)]
    send, edges, to_east, to_west = pick_rows(block_band, block_row, cotangent, winds)
    west = lax.ppermute(to_east, "lon", EASTWARD)
    east = lax.ppermute(to_west, "lon", WESTWARD)
    recv, west, east = lax.optimization_barrier((by_lat(send), west, east))
    rows = unpack_rows(recv)
    swapped = filtered(rows, ops)
    context, row_east, row_west = unpack_context(meta, recv, rows)
    row_from_west = lax.ppermute(row_east, "lon", EASTWARD)
    row_from_east = lax.ppermute(row_west, "lon", WESTWARD)
    swapped, row_from_west, row_from_east = lax.optimization_barrier((swapped, row_from_west, row_from_east))
    given = by_lat(totals(meta, swapped, edges))
    rows = next_rows(meta, rows, context, row_from_west, row_from_east, given)
    swapped = filtered(rows, ops)
    state, message, to_east, to_west = first_substep(meta, cotangent, winds, west, east, given)
    west2 = lax.ppermute(to_east, "lon", EASTWARD)
    east2 = lax.ppermute(to_west, "lon", WESTWARD)
    message = fill_message(swapped, message)
    given2 = by_lat(message)
    return last_substep(meta, bring_back(state, message), winds, west2, east2, given2, given, west)


def solution(mesh):
    return jax.shard_map(
        shards,
        mesh=mesh,
        in_specs=(P("lon", None, "lat"), P("lon", None, "lat"), P("lat", "lon", None), P(), P()),
        out_specs=P("lon", None, "lat"),
        check_vma=False,
    )
```

```python
import jax
import jax.numpy as jnp
from jax import lax
from jax.experimental import pallas as pl
from jax.experimental.pallas import tpu as pltpu
from jax.sharding import PartitionSpec as P

VAR = 5
LEV = 32
COLS = VAR * LEV
XS = 45
ROWS = 48
LANES = 128
BANDS = 8
NLON = 1440
LON_DEV = 32
TARGETS = 8
TEAM = 4
BLOCKS = 16
PICKS = 56
WIRE = 6 * ROWS + 24
PACK = 120
HALO = 72
CHUNK = 9

F32 = jnp.float32
BF16 = jnp.bfloat16
VM = pl.BlockSpec(memory_space=pltpu.VMEM)
SM = pl.BlockSpec(memory_space=pltpu.SMEM)
HB = pl.BlockSpec(memory_space=pl.ANY)
DMA = pltpu.SemaphoreType.DMA
SPANS = [(0, 6), (6, 8), (14, 10), (24, 10), (34, 8), (42, 3)]


def shape(dims, kind):
    return jax.ShapeDtypeStruct(dims, kind)


def params(mib):
    return pltpu.CompilerParams(vmem_limit_bytes=mib * 2**20)


def iotas(dims):
    return (
        lax.broadcasted_iota(jnp.int32, dims, 0),
        lax.broadcasted_iota(jnp.int32, dims, 1),
    )


def lanes_below(value, limit):
    lane = lax.broadcasted_iota(jnp.int32, value.shape, 1)
    return jnp.where(lane < limit, value, jnp.zeros_like(value))


def dot_nt(a, b):
    return lax.dot_general(a, b, (((1,), (1,)), ((), ())), preferred_element_type=F32)


def dot_tn(a, b):
    return lax.dot_general(a, b, (((0,), (0,)), ((), ())), preferred_element_type=F32)


def operator_kernel(meta_ref, ops_ref, *out_refs):
    place = meta_ref[1]
    for t in range(TARGETS):
        tiles = []
        for member in range(TEAM):
            start = XS * ((member // 2) * 2 * TARGETS + 2 * t + member % 2) - 1
            total = None
            first = max(start, 0) // LANES * LANES
            spans = [(first, min(first + 2 * LANES, NLON))]
            if start < 0:
                spans.append(((NLON - 1) // LANES * LANES, NLON))
            if start + XS + 2 > NLON:
                spans.append((0, LANES))
            for low, high in spans:
                row, lane = iotas((ROWS, high - low))
                wanted = start + row
                wanted = jnp.where(wanted < 0, wanted + NLON, wanted)
                wanted = jnp.where(wanted >= NLON, wanted - NLON, wanted)
                hit = (lane + low == wanted) & (row < XS + 2)
                pick = jnp.where(hit, 1.0, 0.0).astype(BF16)
                window = ops_ref[:, :, low:high].reshape(2 * ROWS, high - low)
                part = dot_nt(pick, window)
                total = part if total is None else total + part
            tiles.append(total)
        rows = slice(ROWS * t, ROWS * (t + 1))
        for other in range(TEAM):
            value = tiles[other]
            for member in range(1, TEAM):
                value = jnp.where(place == member, tiles[member ^ other], value)
            out_refs[other][rows, :] = value.astype(BF16)


def prepare_operators(meta, ops):
    out = shape((TARGETS * ROWS, 2 * ROWS), BF16)
    return pl.pallas_call(
        operator_kernel,
        out_shape=(out,) * TEAM,
        in_specs=[SM, VM],
        out_specs=(VM,) * TEAM,
        compiler_params=params(6),
        name="operators",
    )(meta, ops)


def slot(block):
    return (block % 2) * BANDS + block // 2


def global_row(meta_ref, block):
    return meta_ref[2 + block] * LANES + meta_ref[2 + BLOCKS + block]


def clear_rims(ref, count):
    blank = jnp.zeros((count, LANES), ref.dtype)
    for r in (0, XS + 1, XS + 2):
        ref[pl.ds(r, count, stride=ROWS), :] = blank


def pick_weights(meta_ref):
    me = meta_ref[0]
    lane = lax.broadcasted_iota(jnp.int32, (8, LANES), 1)
    pick = lane & 63
    target = jnp.full(lane.shape, -1, jnp.int32)
    for block in range(BLOCKS):
        at = global_row(meta_ref, block) - me * LANES
        for near in range(3):
            target = jnp.where(pick == near * BLOCKS + slot(block), at + (near - 1), target)
    target = jnp.where(pick == 3 * BLOCKS, 0, target)
    target = jnp.where(pick == 3 * BLOCKS + 1, LANES - 1, target)
    sub, lane = iotas((LANES, LANES))
    hit = sub == jnp.broadcast_to(target[:1], (LANES, LANES))
    halves = [jnp.where(hit & ((lane < 64) == side), 1.0, 0.0) for side in (True, False)]
    return jnp.concatenate(halves, axis=0).astype(BF16)


def keep(value, *starts):
    lane = lax.broadcasted_iota(jnp.int32, value.shape, 1)
    hit = (lane >= starts[0]) & (lane < starts[0] + LEV)
    for start in starts[1:]:
        hit = hit | ((lane >= start) & (lane < start + LEV))
    return jnp.where(hit, value, jnp.zeros_like(value))


def pull(value, start):
    moved = pltpu.roll(value, LANES - start, axis=1) if start else value
    return lanes_below(moved, LEV)


def wide(value):
    value = value + pltpu.roll(value, LEV, axis=1)
    return value + pltpu.roll(value, 2 * LEV, axis=1)


def folded(value, width):
    half = ROWS // 2
    return value[:half] + pltpu.roll(value[half:], width, axis=1)


def unfolded(value, start, width, limit):
    low = pltpu.roll(value, LANES - start, axis=1) if start else value
    high = pltpu.roll(value, LANES - start - width, axis=1)
    return jnp.concatenate([lanes_below(low, limit), lanes_below(high, limit)], axis=0)


def pack_messages(meta_ref, main_ref, rest_ref, send_ref, edges_ref, leaving):
    me = meta_ref[0]

    def picked(ref, k):
        return ref[k * ROWS : (k + 1) * ROWS, :]

    def add(d, start, count, value):
        span = slice(start, start + count)
        send_ref[d, span, :] = (send_ref[d, span, :].astype(F32) + value).astype(BF16)

    for block in range(BLOCKS):
        d, e = block // 2, block % 2
        k = slot(block)
        at = global_row(meta_ref, block) - me * LANES

        @pl.when((at >= -1) & (at <= LANES))
        def _():
            mine = (at >= 0) & (at < LANES)
            here = picked(rest_ref, BLOCKS + k)
            behind = picked(rest_ref, k)
            before = pull(behind, 2 * LEV)
            one = lanes_below(jnp.ones_like(here), LEV)
            north = jnp.where(mine, jnp.maximum(pull(here, 2 * LEV), 0.0), one)
            south = jnp.where(mine, jnp.minimum(before, 0.0), -one)
            main = wide(north) * picked(main_ref, 2 * BLOCKS + k) - wide(south) * picked(main_ref, k)
            rest = north * picked(rest_ref, 2 * BLOCKS + k) - south * behind
            send_ref[d, e * ROWS : (e + 1) * ROWS, :] = picked(main_ref, BLOCKS + k).astype(BF16)
            send_ref[d, (2 + e) * ROWS : (3 + e) * ROWS, :] = main.astype(BF16)
            tail = keep(here, 0) + pltpu.roll(rest, 2 * LEV, axis=1)
            add(d, 4 * ROWS, ROWS, pltpu.roll(tail, LEV, axis=1) if e else tail)
            add(d, 5 * ROWS, ROWS, pltpu.roll(keep(here, LEV, 2 * LEV), (1 if e else 3) * LEV, axis=1))
            add(d, 6 * ROWS, ROWS // 2, folded(pltpu.roll(before, LEV, axis=1) if e else before, 2 * LEV))

        if e:
            leaving[d].start()

    for at in range(2):
        k = 3 * BLOCKS + at
        edges_ref[at, :ROWS, :] = picked(main_ref, k).astype(BF16)
        rest = picked(rest_ref, k)
        rest = folded(keep(rest, 0), LEV) + folded(keep(rest, 2 * LEV), LEV)
        edges_ref[at, ROWS:, :] = rest.astype(BF16)


def clear(*refs):
    for ref in refs:
        ref[...] = jnp.zeros(ref.shape, ref.dtype)


def copies(source_ref, target_ref, sem_ref):
    return [
        pltpu.make_async_copy(source_ref.at[pl.ds(start, size)], target_ref.at[pl.ds(start, size)], sem_ref.at[n])
        for n, (start, size) in enumerate(SPANS)
    ]


class Scalars:
    def __init__(self, me, band_ref, row_ref):
        self.me, self.band_ref, self.row_ref = me, band_ref, row_ref

    def __getitem__(self, at):
        if at == 0:
            return self.me
        return self.band_ref[at - 2] if at < 2 + BLOCKS else self.row_ref[at - 2 - BLOCKS]


def pick_kernel(
    band_ref, row_ref, cells_hbm, winds_hbm, send_hbm, edges_ref, east_ref, west_ref,
    main_ref, rest_ref, cells_ref, winds_ref, send_ref, cells_sem, winds_sem, send_sem,
):
    meta_ref = Scalars(lax.axis_index("lat").astype(jnp.int32), band_ref, row_ref)
    arriving = list(zip(copies(cells_hbm, cells_ref, cells_sem), copies(winds_hbm, winds_ref, winds_sem)))
    for pair in arriving:
        for copy in pair:
            copy.start()
    clear_rims(main_ref, PICKS)
    clear_rims(rest_ref, PICKS)
    weights = pick_weights(meta_ref)
    clear(send_ref)
    blank = jnp.zeros((LEV, 2 * LANES), BF16)
    for (start, size), pair in zip(SPANS, arriving):
        for copy in pair:
            copy.wait()
        for y in range(start, start + size, 2):
            both = (y, min(y + 1, XS - 1))
            main = jnp.concatenate([cells_ref[z, :LANES, :] for z in both], axis=1)
            rest = jnp.concatenate([cells_ref[z, LANES:, :] for z in both], axis=1)
            wind = jnp.concatenate([winds_ref[z] for z in both], axis=1)
            rest = jnp.concatenate([rest, wind, blank], axis=0)
            main = jnp.dot(main, weights, preferred_element_type=F32).astype(BF16).T.astype(F32)
            rest = jnp.dot(rest, weights, preferred_element_type=F32).astype(BF16).T.astype(F32)
            for side in range(min(2, XS - y)):
                at = pl.ds(y + side + 1, PICKS, stride=ROWS)
                main_ref[at, :] = main[64 * side : 64 * side + PICKS]
                rest_ref[at, :] = rest[64 * side : 64 * side + PICKS]
    east_ref[:COLS, :] = cells_ref[XS - 1]
    east_ref[COLS:, :] = winds_ref[XS - 1, :LEV, :]
    west_ref[...] = cells_ref[0]
    leaving = [pltpu.make_async_copy(send_ref.at[d], send_hbm.at[d], send_sem.at[d]) for d in range(BANDS)]
    pack_messages(meta_ref, main_ref, rest_ref, send_ref, edges_ref, leaving)
    for copy in leaving:
        copy.wait()


STAGE = pltpu.VMEM((24 * ROWS, LANES), F32)
PICKED = pltpu.VMEM((PICKS * ROWS, LANES), F32)


def pick_rows(band, row, cells, winds):
    return pl.pallas_call(
        pick_kernel,
        out_shape=(
            shape((BANDS, WIRE, LANES), BF16),
            shape((2, HALO, LANES), BF16),
            shape((COLS + LEV, LANES), BF16),
            shape((COLS, LANES), BF16),
        ),
        in_specs=[SM, SM, HB, HB],
        out_specs=(HB, VM, VM, VM),
        scratch_shapes=[
            PICKED,
            PICKED,
            pltpu.VMEM((XS, COLS, LANES), BF16),
            pltpu.VMEM((XS, 2 * LEV, LANES), BF16),
            pltpu.VMEM((BANDS, WIRE, LANES), BF16),
            DMA((len(SPANS),)),
            DMA((len(SPANS),)),
            DMA((BANDS,)),
        ],
        compiler_params=params(58),
        name="pick",
    )(band, row, cells, winds)


def added(recv_ref, span):
    total = recv_ref[0, span, :].astype(F32)
    for s in range(1, BANDS):
        total = total + recv_ref[s, span, :].astype(F32)
    return total


def unpack_kernel(recv_ref, rows_ref):
    rows_ref[: 2 * ROWS, :] = added(recv_ref, slice(0, 2 * ROWS)).astype(BF16)
    tail = added(recv_ref, slice(4 * ROWS, 5 * ROWS))
    rows_ref[2 * ROWS :, :] = lanes_below(tail, 2 * LEV).astype(BF16)


def unpack_rows(recv):
    return pl.pallas_call(
        unpack_kernel,
        out_shape=shape((3 * ROWS, LANES), BF16),
        in_specs=[VM],
        out_specs=VM,
        compiler_params=params(8),
        name="unpack",
    )(recv)


def context_kernel(meta_ref, recv_ref, rows_ref, context_ref, to_east_ref, to_west_ref):
    me = meta_ref[0]
    winds = added(recv_ref, slice(5 * ROWS, 6 * ROWS))
    souths = unfolded(added(recv_ref, slice(6 * ROWS, WIRE)), 0, 2 * LEV, 2 * LEV)
    tails = None
    for e in range(2):
        band = meta_ref[2 + 2 * me + e]
        row = meta_ref[2 + BLOCKS + 2 * me + e]
        north = jnp.maximum(pull(winds, (2 * e + 1) * LEV), 0.0)
        south = jnp.minimum(pull(souths, e * LEV), 0.0)
        main = recv_ref[band, (2 + e) * ROWS : (3 + e) * ROWS, :].astype(F32)
        rest = pull(recv_ref[band, 4 * ROWS : 5 * ROWS, :].astype(F32), (2 + e) * LEV)
        for source, there, coef in (
            (jnp.minimum(band + 1, BANDS - 1), (row == LANES - 1) & (band < BANDS - 1), north),
            (jnp.maximum(band - 1, 0), (row == 0) & (band > 0), -south),
        ):
            share = jnp.where(there, coef, 0.0)
            main = main + wide(share) * recv_ref[source, (2 + e) * ROWS : (3 + e) * ROWS, :].astype(F32)
            rest = rest + share * pull(recv_ref[source, 4 * ROWS : 5 * ROWS, :].astype(F32), (2 + e) * LEV)
        context_ref[e] = main
        tails = rest if e == 0 else tails + pltpu.roll(rest, LEV, axis=1)
    context_ref[2] = tails
    context_ref[3] = winds
    context_ref[4] = souths
    clear(to_east_ref, to_west_ref)
    rims = [rows_ref[p * ROWS : (p + 1) * ROWS, :].astype(F32) for p in range(3)] + [winds]
    for at, tile in enumerate(rims):
        to_east_ref[at : at + 1, :] = tile[XS : XS + 1]
        to_west_ref[at : at + 1, :] = tile[1:2]


def unpack_context(meta, recv, rows):
    edge = shape((8, LANES), F32)
    return pl.pallas_call(
        context_kernel,
        out_shape=(shape((5, ROWS, LANES), F32), edge, edge),
        in_specs=[SM, VM, VM],
        out_specs=(VM,) * 3,
        compiler_params=params(8),
        name="context",
    )(meta, recv, rows)


def spread_blocks(rows_ref):
    first = rows_ref[:ROWS, :]
    second = rows_ref[ROWS : 2 * ROWS, :]
    rest = rows_ref[2 * ROWS :, :].astype(F32)
    lower = lanes_below(rest, LEV)
    upper = rest - lower
    blank = jnp.zeros_like(first)
    return jnp.concatenate(
        [
            jnp.concatenate([first, blank, lower.astype(BF16)], axis=1),
            jnp.concatenate([blank, second, upper.astype(BF16)], axis=1),
        ],
        axis=0,
    )


def product_kernel(*refs):
    out_hbm, out_ref, sem_ref = refs[2 * TEAM :]
    leaving = []
    rows = [spread_blocks(ref) for ref in refs[:TEAM]]
    for q in range(2):
        span = slice(4 * ROWS * q, 4 * ROWS * (q + 1))
        made = None
        for ops_ref, values in zip(refs[TEAM : 2 * TEAM], rows):
            part = jnp.dot(ops_ref[span, :], values, preferred_element_type=F32)
            made = part if made is None else made + part
        for s in range(4):
            part = made[ROWS * s : ROWS * (s + 1)]
            t = 4 * q + s
            out_ref[t, :ROWS, :] = part[:, :LANES].astype(BF16)
            out_ref[t, ROWS : 2 * ROWS, :] = part[:, LANES : 2 * LANES].astype(BF16)
            out_ref[t, 2 * ROWS :, :] = folded(part[:, 2 * LANES :], 2 * LEV).astype(BF16)
        half = pl.ds(4 * q, 4)
        leaving.append(pltpu.make_async_copy(out_ref.at[half], out_hbm.at[half], sem_ref.at[q]))
        leaving[-1].start()
    for copy in leaving:
        copy.wait()


def products(rows, ops):
    return pl.pallas_call(
        product_kernel,
        out_shape=pltpu.HBM((TARGETS, PACK, LANES), BF16),
        in_specs=[VM] * (2 * TEAM),
        out_specs=HB,
        scratch_shapes=[pltpu.VMEM((TARGETS, PACK, LANES), BF16), DMA((2,))],
        compiler_params=params(6),
        name="product",
    )(*rows, *ops)


def total_kernel(meta_ref, recv_ref, edges_hbm, out_ref, edges_ref, sem_ref):
    arriving = pltpu.make_async_copy(edges_hbm, edges_ref, sem_ref.at[0])
    arriving.start()
    total = recv_ref[0].astype(F32)
    for s in range(1, TARGETS):
        total = total + recv_ref[s].astype(F32)
    total = total.astype(BF16)
    me = meta_ref[0]
    for d in range(BANDS):
        out_ref[d, :PACK, :] = total
    arriving.wait()
    for d in range(BANDS):
        edge = jnp.where(d == me + 1, edges_ref[1], jnp.zeros((HALO, LANES), BF16))
        out_ref[d, PACK:, :] = jnp.where(d == me - 1, edges_ref[0], edge)


def totals(meta, recv, edges):
    return pl.pallas_call(
        total_kernel,
        out_shape=shape((BANDS, PACK + HALO, LANES), BF16),
        in_specs=[SM, VM, HB],
        out_specs=VM,
        scratch_shapes=[pltpu.VMEM((2, HALO, LANES), BF16), DMA((1,))],
        compiler_params=params(4),
        name="total",
    )(meta, recv, edges)


def fill_kernel(recv_ref, message_hbm, out_hbm, total_ref, sem_ref):
    total = recv_ref[0].astype(F32)
    for s in range(1, TARGETS):
        total = total + recv_ref[s].astype(F32)
    total_ref[...] = total.astype(BF16)
    leaving = [
        pltpu.make_async_copy(total_ref, out_hbm.at[d, pl.ds(0, PACK)], sem_ref.at[d]) for d in range(BANDS)
    ]
    for copy in leaving:
        copy.start()
    for copy in leaving:
        copy.wait()


def fill_message(recv, message):
    return pl.pallas_call(
        fill_kernel,
        out_shape=pltpu.HBM((BANDS, PACK + HALO, LANES), BF16),
        in_specs=[VM, HB],
        out_specs=HB,
        scratch_shapes=[pltpu.VMEM((PACK, LANES), BF16), DMA((BANDS,))],
        input_output_aliases={1: 0},
        compiler_params=params(4),
        name="fill",
    )(recv, pltpu.with_memory_space_constraint(message, pltpu.HBM))


def halo_rows(meta_ref, recv_ref):
    me = meta_ref[0]
    halos = []
    for near, there in ((me - 1, me > 0), (me + 1, me < BANDS - 1)):
        source = jnp.clip(near, 0, BANDS - 1)
        main = recv_ref[source, PACK : PACK + ROWS, :].astype(F32)
        rest = recv_ref[source, PACK + ROWS :, :].astype(F32)
        found = (main, unfolded(rest, 0, LEV, LEV), unfolded(rest, 2 * LEV, LEV, LEV))
        halos.append([jnp.where(there, value, 0.0) for value in found])
    return halos[0][:2], halos[1][:2], halos[0][2]


def stage_blocks(recv_ref, main_ref, rest_ref):
    half = ROWS // 2
    for source in range(BANDS):
        packed = recv_ref[source, 2 * ROWS : PACK, :].astype(F32)
        for b in range(2):
            at = (b * BANDS + source) * ROWS
            main_ref[at : at + ROWS, :] = recv_ref[source, b * ROWS : (b + 1) * ROWS, :].astype(F32)
            rest_ref[at : at + half, :] = pull(packed, b * LEV)
            rest_ref[at + half : at + ROWS, :] = pull(packed, (2 + b) * LEV)


def block_sum(meta_ref, row, main_ref, rest_ref):
    main = jnp.zeros((ROWS, LANES), F32)
    rest = jnp.zeros((ROWS, LANES), F32)
    for block in range(BLOCKS):
        share = jnp.where(global_row(meta_ref, block) == row, 1.0, 0.0)
        k = slot(block) * ROWS
        main = main + share * main_ref[k : k + ROWS, :]
        rest = rest + share * rest_ref[k : k + ROWS, :]
    return main, rest


KEPT = 32
GROUP = LANES // KEPT
TALL = COLS + LEV


def stage_corrections(meta_ref, recv_ref, wind_recv_ref, main_ref, rest_ref, tall_ref):
    clear(main_ref, rest_ref)
    me = meta_ref[0]
    halos = halo_rows(meta_ref, recv_ref)
    sums = [list(halos[0]), list(halos[1])]
    for source in range(BANDS):
        packed = recv_ref[source, 2 * ROWS : PACK, :].astype(F32)
        for b in range(2):
            k = b * BANDS + source
            main = recv_ref[source, b * ROWS : (b + 1) * ROWS, :].astype(F32)
            rest = unfolded(packed, b * LEV, 2 * LEV, LEV)
            main_ref[pl.ds(k, ROWS, stride=KEPT), :] = main
            rest_ref[pl.ds(k, ROWS, stride=KEPT), :] = rest
            for at, row in enumerate((me * LANES - 1, (me + 1) * LANES)):
                share = jnp.where(global_row(meta_ref, 2 * source + b) == row, 1.0, 0.0)
                sums[at][0] = sums[at][0] + share * main
                sums[at][1] = sums[at][1] + share * rest
    for at in range(2):
        main_ref[pl.ds(16 + at, ROWS, stride=KEPT), :] = sums[at][0].astype(BF16).astype(F32)
        rest_ref[pl.ds(16 + at, ROWS, stride=KEPT), :] = sums[at][1].astype(BF16).astype(F32)
    wind = halo_rows(meta_ref, wind_recv_ref)[2]
    rest_ref[pl.ds(18, ROWS, stride=KEPT), :] = pltpu.roll(wind, LEV, axis=1)
    for t in range(ROWS // GROUP):
        span = slice(t * LANES, (t + 1) * LANES)
        tall_ref[t * TALL : t * TALL + LANES, :] = main_ref[span, :].astype(BF16).T
        tall_ref[t * TALL + LANES : (t + 1) * TALL, :] = rest_ref[span, :].astype(BF16).T[: 2 * LEV]


def rows_kernel(meta_ref, before_ref, context_ref, west_ref, east_ref, recv_ref, out_ref, main_ref, rest_ref):
    stage_blocks(recv_ref, main_ref, rest_ref)
    me = meta_ref[0]
    sub = lax.broadcasted_iota(jnp.int32, (ROWS, LANES), 0)
    inner = (sub >= 1) & (sub <= XS)

    def rimmed(value, at):
        value = jnp.where(sub == 0, west_ref[at : at + 1, :], value)
        return jnp.where(sub == XS + 1, east_ref[at : at + 1, :], value)

    def known(p):
        return rimmed(before_ref[p * ROWS : (p + 1) * ROWS, :].astype(F32), p)

    last = None
    tail = known(2)
    winds = rimmed(context_ref[3], 3)
    for e in range(2):
        row = global_row(meta_ref, 2 * me + e)
        across = pull(winds, 2 * e * LEV)
        east = jnp.maximum(across, 0.0)
        west = jnp.minimum(pltpu.roll(across, 1, axis=0), 0.0)
        north = jnp.where(row == BANDS * LANES - 1, 0.0, jnp.maximum(pull(winds, (2 * e + 1) * LEV), 0.0))
        south = jnp.minimum(pull(context_ref[4], e * LEV), 0.0)
        coefs = (east, west, north, south)
        added = [block_sum(meta_ref, row + near, main_ref, rest_ref) for near in (-1, 0, 1)]

        def moved(coefs, here, aside, behind, ahead):
            east, west, north, south = coefs
            here = here.astype(BF16).astype(F32)
            centre = 1.0 - east + west - north + south
            made = (
                centre * here
                + (east * pltpu.roll(here, ROWS - 1, axis=0) - west * pltpu.roll(here, 1, axis=0))
                + (aside + (north * ahead - south * behind))
            )
            return jnp.where(inner, made, 0.0)

        main = moved([wide(c) for c in coefs], known(e) + added[1][0], context_ref[e], added[0][0], added[2][0])
        out_ref[e * ROWS : (e + 1) * ROWS, :] = main.astype(BF16)
        rest = pull(tail, e * LEV) + added[1][1]
        rest = moved(coefs, rest, pull(context_ref[2], e * LEV), added[0][1], added[2][1])
        rest = lanes_below(rest, LEV)
        last = rest if e == 0 else last + pltpu.roll(rest, LEV, axis=1)
    out_ref[2 * ROWS :, :] = last.astype(BF16)


def next_rows(*args):
    return pl.pallas_call(
        rows_kernel,
        out_shape=shape((3 * ROWS, LANES), BF16),
        in_specs=[SM] + [VM] * 5,
        out_specs=VM,
        scratch_shapes=[STAGE, STAGE],
        compiler_params=params(4),
        name="rows",
    )(*args)


def place_weights(meta_ref, q):
    sub, lane = iotas((LANES, 2 * LANES))
    kept = sub - q * KEPT
    target = jnp.full(sub.shape, -1, jnp.int32)
    for block in range(BLOCKS):
        at = global_row(meta_ref, block) - meta_ref[0] * LANES
        target = jnp.where(kept == slot(block), jnp.where((at >= 0) & (at < LANES), at, -1), target)
    target = jnp.where((kept == 16) | (kept == 18), LANES, target)
    target = jnp.where(kept == 17, 2 * LANES - 1, target)
    return jnp.where(lane == target, 1.0, 0.0).astype(BF16)


def advance(
    meta_ref, cells_ref, winds_ref, west_ref, east_ref, wind_west_ref, tall_ref, placed_ref, smooth_ref, emit, leaving,
    rounded,
):
    for q in range(GROUP):
        placed_ref[q] = jnp.dot(tall_ref[...], place_weights(meta_ref, q), preferred_element_type=F32)
    top = meta_ref[0] == BANDS - 1

    def smooth(r, base):
        at = (r // GROUP) * TALL
        value = base.astype(F32) + placed_ref[r % GROUP, pl.ds(at, COLS), :LANES]
        if rounded:
            value = value.astype(BF16).astype(F32)
        smooth_ref[r] = value
        return value

    def step(x, ahead):
        ahead = smooth(x + 2, ahead)
        emit(x, stencil(x, top, winds_ref, wind_west_ref, smooth_ref, ahead, placed_ref))

    def body(x, carry):
        step(x, cells_ref[x + 1])
        return carry

    smooth(0, west_ref[:COLS, :])
    smooth(1, cells_ref[0])
    for (start, size), copy in zip(SPANS, leaving):
        for x in range(start, min(start + size, XS - 1)):
            body(x, 0)
        if start + size == XS:
            step(XS - 1, east_ref[...])
        copy.start()


def stencil(x, top, winds_ref, west_ref, smooth_ref, ahead, placed_ref):
    at = ((x + 1) // GROUP) * TALL
    q = (x + 1) % GROUP
    lane = lax.broadcasted_iota(jnp.int32, (LEV, LANES), 1)
    courant = winds_ref[x].astype(F32)
    before = winds_ref[jnp.maximum(x - 1, 0), :LEV, :].astype(F32)
    before = jnp.where(x == 0, west_ref[COLS:, :].astype(F32), before)
    across = courant[:LEV]
    along = jnp.where(top & (lane == LANES - 1), 0.0, courant[LEV:])
    south_along = jnp.where(lane == 0, placed_ref[q, pl.ds(at + COLS, LEV), LANES:], pltpu.roll(along, 1, axis=1))
    east = jnp.maximum(across, 0.0)
    west = jnp.minimum(before, 0.0)
    north = jnp.maximum(along, 0.0)
    south = jnp.minimum(south_along, 0.0)
    centre = 1.0 - east + west - north + south
    made = []
    for v in range(VAR):
        span = slice(v * LEV, (v + 1) * LEV)
        here = smooth_ref[x + 1, span, :]
        edge = placed_ref[q, pl.ds(at + v * LEV, LEV), LANES:]
        above = jnp.where(lane == LANES - 1, edge, pltpu.roll(here, LANES - 1, axis=1))
        below = jnp.where(lane == 0, edge, pltpu.roll(here, 1, axis=1))
        made.append(
            centre * here
            + (east * ahead[span] - west * smooth_ref[x, span, :])
            + (north * above - south * below)
        )
    return made


SCRATCH = [
    pltpu.VMEM((KEPT * ROWS, LANES), F32),
    pltpu.VMEM((KEPT * ROWS, LANES), F32),
    pltpu.VMEM((ROWS // GROUP * TALL, LANES), BF16),
    pltpu.VMEM((GROUP, ROWS // GROUP * TALL, 2 * LANES), F32),
    pltpu.VMEM((XS + 2, COLS, LANES), F32),
]


def first_kernel(
    meta_ref, cells_hbm, winds_hbm, west_ref, east_ref, recv_ref,
    out_hbm, message_hbm, to_east_hbm, to_west_hbm,
    main_ref, rest_ref, tall_ref, placed_ref, smooth_ref, out_ref, out_sem, rim_sem,
    cells_ref, cells_sem, winds_ref, winds_sem, edges_ref, edges_sem,
):
    arriving = copies(cells_hbm, cells_ref, cells_sem) + copies(winds_hbm, winds_ref, winds_sem)
    for copy in arriving:
        copy.start()
    stage_corrections(meta_ref, recv_ref, recv_ref, main_ref, rest_ref, tall_ref)
    for copy in arriving:
        copy.wait()

    def emit(x, made):
        for v in range(VAR):
            out_ref[x, v * LEV : (v + 1) * LEV, :] = made[v].astype(BF16)

    leaving = copies(out_ref, out_hbm, out_sem)
    advance(
        meta_ref, cells_ref, winds_ref, west_ref, east_ref, west_ref, tall_ref, placed_ref, smooth_ref, emit, leaving,
        True,
    )
    rims = [
        pltpu.make_async_copy(out_ref.at[0], to_west_hbm, rim_sem.at[0]),
        pltpu.make_async_copy(out_ref.at[XS - 1], to_east_hbm, rim_sem.at[1]),
    ]
    for copy in rims:
        copy.start()
    sub, lane = iotas((LANES, LANES))
    halves = [(sub == 0) & (lane == 2 * side) | (sub == LANES - 1) & (lane == 2 * side + 1) for side in range(2)]
    ends = jnp.concatenate([jnp.where(hit, 1.0, 0.0) for hit in halves], axis=0).astype(BF16)
    total = None
    for x in range(0, XS, 2):
        pair = jnp.concatenate([out_ref[min(x + side, XS - 1)] for side in range(2)], axis=1)
        found = jnp.dot(pair, ends, preferred_element_type=F32)
        if x == XS - 1:
            found = jnp.where(lax.broadcasted_iota(jnp.int32, found.shape, 1) < 2, found, 0.0)
        found = pltpu.roll(found, 2 * x + 2, axis=1)
        total = found if total is None else total + found
    main_ref[:LANES, :] = total[:LANES].T
    rest = jnp.concatenate([total[LANES:], jnp.zeros((LANES - LEV, LANES), F32)], axis=0)
    rest_ref[:LANES, :] = rest.T
    me = meta_ref[0]
    for at, there in ((0, me - 1), (1, me + 1)):
        main = main_ref[pl.ds(at, ROWS, stride=2), :].astype(BF16)
        rest = folded(rest_ref[pl.ds(at, ROWS, stride=2), :], LEV).astype(BF16)
        edge = jnp.concatenate([main.astype(F32), rest.astype(F32)], axis=0).astype(BF16)
        for d in range(BANDS):
            before = jnp.zeros_like(edge) if at == 0 else edges_ref[d]
            edges_ref[d] = jnp.where(d == there, edge, before)
    rims.append(pltpu.make_async_copy(edges_ref, message_hbm.at[:, pl.ds(PACK, HALO)], edges_sem.at[0]))
    rims[-1].start()
    for copy in leaving + rims:
        copy.wait()


def first_substep(*args):
    return pl.pallas_call(
        first_kernel,
        out_shape=(
            shape((XS, COLS, LANES), BF16),
            shape((BANDS, PACK + HALO, LANES), BF16),
            shape((COLS, LANES), BF16),
            shape((COLS, LANES), BF16),
        ),
        in_specs=[SM, HB, HB] + [VM] * 3,
        out_specs=(HB, HB, HB, HB),
        scratch_shapes=SCRATCH
        + [
            pltpu.VMEM((XS, COLS, LANES), BF16),
            DMA((len(SPANS),)),
            DMA((2,)),
            pltpu.VMEM((XS, COLS, LANES), BF16),
            DMA((len(SPANS),)),
            pltpu.VMEM((XS, 2 * LEV, LANES), BF16),
            DMA((len(SPANS),)),
            pltpu.VMEM((BANDS, HALO, LANES), BF16),
            DMA((1,)),
        ],
        compiler_params=params(58),
        name="first",
    )(*args)


def last_kernel(
    meta_ref, cells_ref, winds_ref, west_ref, east_ref, recv_ref, wind_recv_ref, wind_west_ref,
    out_hbm, main_ref, rest_ref, tall_ref, placed_ref, smooth_ref, out_ref, out_sem,
):
    stage_corrections(meta_ref, recv_ref, wind_recv_ref, main_ref, rest_ref, tall_ref)

    def emit(x, made):
        for v in range(VAR):
            out_ref[x, v * LEV : (v + 1) * LEV, :] = made[v]

    leaving = copies(out_ref, out_hbm, out_sem)
    advance(
        meta_ref, cells_ref, winds_ref, west_ref, east_ref, wind_west_ref, tall_ref, placed_ref, smooth_ref, emit,
        leaving, False,
    )
    for copy in leaving:
        copy.wait()


def last_substep(*args):
    return pl.pallas_call(
        last_kernel,
        out_shape=shape((XS, COLS, LANES), F32),
        in_specs=[SM] + [VM] * 7,
        out_specs=HB,
        scratch_shapes=SCRATCH + [pltpu.VMEM((XS, COLS, LANES), F32), DMA((len(SPANS),))],
        compiler_params=params(30),
        name="last",
    )(*args)


def stay_kernel(cells_hbm, message_hbm, cells_ref, sem_ref):
    arriving = copies(cells_hbm, cells_ref, sem_ref)
    for copy in arriving:
        copy.start()
    for copy in arriving:
        copy.wait()


def bring_back(cells, message):
    return pl.pallas_call(
        stay_kernel,
        out_shape=shape((XS, COLS, LANES), BF16),
        in_specs=[HB, HB],
        out_specs=VM,
        scratch_shapes=[DMA((len(SPANS),))],
        compiler_params=params(4),
        name="stay",
    )(pltpu.with_memory_space_constraint(cells, pltpu.HBM), pltpu.with_memory_space_constraint(message, pltpu.HBM))


TEAMMATES = [[(i, i ^ (16 * (other // 2) + other % 2)) for i in range(LON_DEV)] for other in range(1, TEAM)]
EASTWARD = [(i, (i + 1) % LON_DEV) for i in range(LON_DEV)]
WESTWARD = [(i, (i - 1) % LON_DEV) for i in range(LON_DEV)]
ALONG_Z = [[16 * (place // 2) + 2 * t + place % 2 for t in range(TARGETS)] for place in range(TEAM)]


def by_lat(messages):
    return lax.all_to_all(messages, "lat", 0, 0, tiled=True)


def filtered(rows, ops):
    team = [rows] + [lax.ppermute(rows, "lon", mates) for mates in TEAMMATES]
    partial = products(team, ops)
    return lax.all_to_all(partial, "lon", 0, 0, tiled=True, axis_index_groups=ALONG_Z)


def shards(cotangent, winds, filter_ops, block_band, block_row):
    me = lax.axis_index("lat").astype(jnp.int32).reshape(1)
    at = lax.axis_index("lon").astype(jnp.int32)
    place = ((at >> 4) * 2 + (at & 1)).reshape(1)
    meta = jnp.concatenate([me, place, block_band, block_row])
    made = prepare_operators(meta, jnp.pad(filter_ops, ((0, 0), (1, 2), (0, 0))))
    ops = [made[0]] + [lax.ppermute(part, "lon", mates) for part, mates in zip(made[1:], TEAMMATES)]
    send, edges, to_east, to_west = pick_rows(block_band, block_row, cotangent, winds)
    west = lax.ppermute(to_east, "lon", EASTWARD)
    east = lax.ppermute(to_west, "lon", WESTWARD)
    recv, west, east = lax.optimization_barrier((by_lat(send), west, east))
    rows = unpack_rows(recv)
    swapped = filtered(rows, ops)
    context, row_east, row_west = unpack_context(meta, recv, rows)
    row_from_west = lax.ppermute(row_east, "lon", EASTWARD)
    row_from_east = lax.ppermute(row_west, "lon", WESTWARD)
    swapped, row_from_west, row_from_east = lax.optimization_barrier((swapped, row_from_west, row_from_east))
    given = by_lat(totals(meta, swapped, edges))
    rows = next_rows(meta, rows, context, row_from_west, row_from_east, given)
    swapped = filtered(rows, ops)
    state, message, to_east, to_west = first_substep(meta, cotangent, winds, west, east, given)
    west2 = lax.ppermute(to_east, "lon", EASTWARD)
    east2 = lax.ppermute(to_west, "lon", WESTWARD)
    message = fill_message(swapped, message)
    given2 = by_lat(message)
    return last_substep(meta, bring_back(state, message), winds, west2, east2, given2, given, west)


def solution(mesh):
    return jax.shard_map(
        shards,
        mesh=mesh,
        in_specs=(P("lon", None, "lat"), P("lon", None, "lat"), P("lat", "lon", None), P(), P()),
        out_specs=P("lon", None, "lat"),
        check_vma=False,
    )
```
